32 devices in a mesh: slab: 2 (over y), seq: 4 (over z), head: 4 (over x, core).
Axes of the slice: x: 2, y: 2, z: 4, core: 2. Of those that a mesh axis runs over, the one named last changes fastest.
Arguments:
- values_first: bfloat16 [4, 1024, 1024], P('slab', 'seq', 'head'), parts along dimension 0, may hold values from -6 to 6
- keys_first: bfloat16 [4, 1024, 1024], P('slab', 'seq', 'head'), parts along dimension 0, may hold values from -0.5 to 0.5
- queries_first: bfloat16 [4, 1024, 1024], P('slab', 'seq', 'head'), parts along dimension 0, may hold values from -0.5 to 0.5
- steps_first: float32 [4, 8, 1024], P('slab', 'head', 'seq'), parts along dimension 0, may hold values from 0 to 0.35
- rates_first: float32 [8], P('head'), may hold values from 1 to 2
- skip_first: float32 [8], P('head'), may hold values from 1 to 4
- gain_first: float32 [1024], P('head'), may hold values from 0.5 to 1.5
- w_values: bfloat16 [8, 128, 128], P('head'), may hold values from -0.5 to 0.5
- w_keys: bfloat16 [8, 128, 256], P('head'), may hold values from -0.046875 to 0.046875
- w_step: bfloat16 [8, 128], P('head'), may hold values from -0.5 to 0.5
- step_bias: float32 [8], P('head'), may hold values from -1 to 1
- rates_second: float32 [8], P('head'), may hold values from 0 to 0.04
- skip_second: float32 [8], P('head'), may hold values from 1 to 4
- gain_second: float32 [1024], P('head'), may hold values from 0.5 to 1.5
Outputs:
- mixed: bfloat16 [4, 1024, 1024], P('slab', 'seq', 'head'), parts along dimension 0
The draws below stay inside these ranges and needn't reach their ends.
There are 2 independent parts, one for each index of `slab`. The reference program is written for one: setup_inputs(seed, part) draws one part's arguments, and reference() takes and returns one part's arrays. A program takes and returns all parts, laid end to end along the dimension named above; an argument that names none is the same for every part. Nothing has to cross between parts.
All inputs are finite; a program needn't handle non-finite values.
Results may differ from the reference program's by a relative error of at most 0.007.
Values may be sent and summed in bfloat16 or wider, within the bound.
A program may use at most 64 MiB of HBM per device.

```python
import math
import jax
import jax.numpy as jnp
from jax import lax

ATTN_UNIT_COUNT = 8
P_SIZE = 128
N = 128
BLOCK = 256
BATCH_PLATES = 2
GR = 32
GC = 32
TILE_SERIES = 1024
TOK_DEV = 256


def draw_steps_first(key, part):
    key_order, key_base, key_place, lookup_extent = jax.random.split(key, 4)
    ranking = jax.random.permutation(key_order, ATTN_UNIT_COUNT)
    keeping = ATTN_UNIT_COUNT // 2
    slow_heads = (ranking < keeping)[None, :, None]
    initial_speed = jax.random.uniform(key_base, (BATCH_PLATES, ATTN_UNIT_COUNT, TILE_SERIES), jnp.float32, 0.5, 1.5)
    tile_locations = jax.random.randint(key_place, (BATCH_PLATES, ATTN_UNIT_COUNT, 2), 0, TILE_SERIES)
    tile_location_index = lax.broadcasted_iota(jnp.int32, (BATCH_PLATES, ATTN_UNIT_COUNT, TILE_SERIES), 2)
    segment_bundles = jnp.logical_or(tile_location_index == tile_locations[:, :, 0:1], tile_location_index == tile_locations[:, :, 1:2])
    segment_extent = jax.random.uniform(lookup_extent, (BATCH_PLATES, ATTN_UNIT_COUNT, 1), jnp.float32, 0.25, 0.35)
    lagging_increments = jnp.where(segment_bundles, segment_extent, initial_speed * (0.4 / TILE_SERIES))
    return jnp.where(slow_heads, lagging_increments, initial_speed * 0.025)


def draw_rates_second(key, part):
    key_order, key_slow, key_fast = jax.random.split(key, 3)
    ranking = jax.random.permutation(key_order, ATTN_UNIT_COUNT)
    keeping = ATTN_UNIT_COUNT // 2
    slow_heads = ranking < keeping
    slow_rate = jax.random.uniform(key_slow, (ATTN_UNIT_COUNT,), jnp.float32, 0.5, 1.0) * (0.3 / TILE_SERIES)
    fast_rate = jnp.exp(jax.random.uniform(key_fast, (ATTN_UNIT_COUNT,), jnp.float32, jnp.log(0.02), jnp.log(0.04)))
    return jnp.where(slow_heads, slow_rate, fast_rate)


def level_of(stream_key, dims, cuts, least, largest):
    level = 1.0
    for position, parts in cuts:
        heights = jax.random.uniform(jax.random.fold_in(jax.random.fold_in(stream_key, 6), position), (parts,), jnp.float32, least / len(cuts), largest / len(cuts))
        level = level * jnp.repeat(jnp.exp(heights), dims[position] // parts).reshape((-1,) + (1,) * (len(dims) - 1 - position))
    return level


def centred(key, shape, scale, bound, pieces=(), held_as=jnp.bfloat16):
    level = level_of(key, shape, pieces, -0.22, 0.18) if pieces else 1.0
    array = jax.random.normal(key, shape, jnp.float32) * scale * level
    return jnp.minimum(jnp.maximum(array, -bound), bound).astype(held_as)


def setup_inputs(seed: int = 0, part: int = 0) -> dict:
    splits = jax.random.split(jax.random.key(seed), 15)
    part_splits = jax.random.split(jax.random.fold_in(splits[14], part), 15)
    values_first = centred(part_splits[0], (BATCH_PLATES, TILE_SERIES, ATTN_UNIT_COUNT * P_SIZE), 1.0, 6.0, ((1, 4), (2, 4)))
    keys_first = centred(part_splits[1], (BATCH_PLATES, TILE_SERIES, ATTN_UNIT_COUNT * N), N ** -0.5, 0.5, ((1, 4), (2, 4)))
    queries_first = centred(part_splits[2], (BATCH_PLATES, TILE_SERIES, ATTN_UNIT_COUNT * N), N ** -0.5, 0.5, ((1, 4), (2, 4)))
    steps_first = draw_steps_first(jax.random.fold_in(jax.random.fold_in(splits[14], part), 71), part)
    rates_first = jnp.clip(jnp.exp(math.log(2.0) - 0.6931472 * jax.random.uniform(splits[4], (ATTN_UNIT_COUNT,), jnp.float32) ** level_of(splits[4], (ATTN_UNIT_COUNT,), ((0, 4),), -0.2, 0.2)), 1.0, 2.0)
    skip_first = jnp.clip(jnp.exp(math.log(4.0) - 1.3862944 * jax.random.uniform(splits[5], (ATTN_UNIT_COUNT,), jnp.float32) ** level_of(splits[5], (ATTN_UNIT_COUNT,), ((0, 4),), -0.2, 0.2)), 1.0, 4.0)
    gain_first = jnp.clip(1.0 + 0.1 * jax.random.normal(splits[6], (ATTN_UNIT_COUNT * P_SIZE,), jnp.float32), 0.5, 1.5)
    w_values = centred(splits[7], (ATTN_UNIT_COUNT, P_SIZE, P_SIZE), P_SIZE ** -0.5, 0.5, ((0, 4),))
    w_keys = centred(splits[8], (ATTN_UNIT_COUNT, P_SIZE, 2 * N), (P_SIZE * N) ** -0.5, 0.046875, ((0, 4),))
    w_step = centred(splits[9], (ATTN_UNIT_COUNT, P_SIZE), P_SIZE ** -0.5, 0.5, ((0, 4),))
    step_bias = jnp.clip(jax.random.uniform(splits[10], (ATTN_UNIT_COUNT,), jnp.float32, -1.0, 1.0) * level_of(splits[10], (ATTN_UNIT_COUNT,), ((0, 4),), -0.4, 0.0), -1.0, 1.0)
    rates_second = draw_rates_second(jax.random.fold_in(splits[14], 71), part)
    skip_second = jnp.clip(jnp.exp(math.log(4.0) - 1.3862944 * jax.random.uniform(splits[12], (ATTN_UNIT_COUNT,), jnp.float32) ** level_of(splits[12], (ATTN_UNIT_COUNT,), ((0, 4),), -0.2, 0.2)), 1.0, 4.0)
    gain_second = jnp.clip(1.0 + 0.1 * jax.random.normal(splits[13], (ATTN_UNIT_COUNT * P_SIZE,), jnp.float32), 0.5, 1.5)
    return {"values_first": values_first, "keys_first": keys_first, "queries_first": queries_first, "steps_first": steps_first, "rates_first": rates_first, "skip_first": skip_first, "gain_first": gain_first, "w_values": w_values, "w_keys": w_keys, "w_step": w_step, "step_bias": step_bias, "rates_second": rates_second, "skip_second": skip_second, "gain_second": gain_second}


def rounded(values):
    return lax.optimization_barrier(values.astype(jnp.bfloat16)).astype(jnp.float32)

def reference_scan(values, keys_in, queries, log_decay, skip, gain):
    length = values.shape[0]
    block_len = min(BLOCK, TOK_DEV)
    blocks = length // block_len
    value_blocks = values.astype(jnp.float32).reshape(blocks, block_len, ATTN_UNIT_COUNT, P_SIZE)
    key_blocks = keys_in.astype(jnp.float32).reshape(blocks, block_len, ATTN_UNIT_COUNT, N)
    query_blocks = queries.astype(jnp.float32).reshape(blocks, block_len, ATTN_UNIT_COUNT, N)
    log_blocks = jnp.transpose(log_decay.astype(jnp.float32).reshape(ATTN_UNIT_COUNT, blocks, block_len), (1, 0, 2))
    row_ids = lax.broadcasted_iota(jnp.int32, (block_len, block_len), 0)
    col_ids = lax.broadcasted_iota(jnp.int32, (block_len, block_len), 1)

    def advance(carried, entry_item):
        value_block, key_block, query_block, log_block = entry_item
        running = jnp.cumsum(log_block, axis=1)
        scores = jnp.einsum('ihn,jhn->hij', query_block, key_block, precision=lax.Precision.HIGHEST)
        spread = running[:, :, None] - running[:, None, :]
        decays = jnp.exp(jnp.where(row_ids >= col_ids, spread, -jnp.inf))
        mixing = rounded(scores * decays)
        inner_sum = jnp.einsum('hij,jhp->ihp', mixing, value_block, precision=lax.Precision.HIGHEST)
        outer_sum = jnp.einsum('ihn,hnp->ihp', query_block, rounded(carried), precision=lax.Precision.HIGHEST)
        raw_out = inner_sum + outer_sum * jnp.exp(running).T[:, :, None] + skip[None, :, None] * value_block
        scaled = raw_out * lax.rsqrt(lax.optimization_barrier(jnp.mean(raw_out * raw_out, axis=-1, keepdims=True)) + 1e-05)
        normed = (scaled * gain.reshape(ATTN_UNIT_COUNT, P_SIZE)[None]).astype(jnp.bfloat16)
        to_end = jnp.exp(running[:, -1:] - running)
        weighted = rounded(key_block * to_end.T[:, :, None])
        local_state = jnp.einsum('jhn,jhp->hnp', weighted, value_block, precision=lax.Precision.HIGHEST)
        updated = jnp.exp(running[:, -1])[:, None, None] * carried + local_state
        return (updated, normed)
    final_state, normed_all = lax.scan(advance, jnp.zeros((ATTN_UNIT_COUNT, N, P_SIZE), jnp.float32), (value_blocks, key_blocks, query_blocks, log_blocks))
    return normed_all.reshape(length, ATTN_UNIT_COUNT * P_SIZE)

def reference(values_first, keys_first, queries_first, steps_first, rates_first, skip_first, gain_first, w_values, w_keys, w_step, step_bias, rates_second, skip_second, gain_second):

    def one_slab(entry_item):
        values_one, keys_one, queries_one, steps_one = entry_item
        first_out = reference_scan(values_one, keys_one, queries_one, -rates_first[:, None] * steps_one, skip_first, gain_first)
        columns = jnp.transpose(first_out.reshape(GR, GC, ATTN_UNIT_COUNT, P_SIZE), (1, 0, 2, 3)).reshape(TILE_SERIES, ATTN_UNIT_COUNT, P_SIZE).astype(jnp.float32)
        values_two = rounded(jnp.einsum('lhp,hpk->lhk', columns, w_values.astype(jnp.float32), precision=lax.Precision.HIGHEST))
        keys_two = rounded(jnp.einsum('lhp,hpk->lhk', columns, w_keys.astype(jnp.float32), precision=lax.Precision.HIGHEST))
        step_pre = rounded(jnp.einsum('lhp,hp->hl', columns, w_step.astype(jnp.float32), precision=lax.Precision.HIGHEST))
        steps_two = jax.nn.softplus(step_pre + step_bias[:, None])
        second_out = reference_scan(values_two.reshape(TILE_SERIES, ATTN_UNIT_COUNT * P_SIZE), keys_two[:, :, :N].reshape(TILE_SERIES, ATTN_UNIT_COUNT * N), keys_two[:, :, N:].reshape(TILE_SERIES, ATTN_UNIT_COUNT * N), -rates_second[:, None] * steps_two, skip_second, gain_second)
        second_home = jnp.transpose(second_out.reshape(GC, GR, ATTN_UNIT_COUNT * P_SIZE), (1, 0, 2)).reshape(TILE_SERIES, ATTN_UNIT_COUNT * P_SIZE)
        return (first_out.astype(jnp.float32) + second_home.astype(jnp.float32)).astype(jnp.bfloat16)
    return lax.map(one_slab, (values_first, keys_first, queries_first, steps_first))
```

```python
import functools
import math

import jax
import jax.numpy as jnp
from jax import lax
from jax.experimental import pallas as pl
from jax.experimental.pallas import tpu as pltpu
from jax.sharding import PartitionSpec as P

N = 128
BLOCK = 256
ROWS_DEV = 8
VMEM_GRANT = 16 << 20
GROUP = 2
ORDER = (0, 1, 2, 3)
FINISH = (2, 3, 0, 1)
MAPS_TWO = (True, False)
MAPS_THREE = (False, False)


def cumulated(terms, axis):
    size = terms.shape[axis]
    ranks = lax.iota(jnp.int32, size)
    upper = (ranks[:, None] <= ranks[None, :]).astype(jnp.float32)
    sums = jnp.einsum(
        "...j,ji->...i",
        jnp.moveaxis(terms, axis, -1),
        upper,
        precision=lax.Precision.HIGHEST,
    )
    return jnp.moveaxis(sums, -1, axis)


def block_terms(values, keys_in, queries, log_decay, block_len):
    slab_count, length, feat_width = values.shape
    head_count = log_decay.shape[1]
    blocks = length // block_len
    value_blocks = values.reshape(
        slab_count, blocks, block_len, head_count, feat_width // head_count
    )
    key_blocks = keys_in.reshape(
        slab_count, blocks, block_len, head_count, keys_in.shape[2] // head_count
    )
    query_blocks = queries.reshape(
        slab_count, blocks, block_len, head_count, queries.shape[2] // head_count
    )
    running = cumulated(log_decay.reshape(slab_count, head_count, blocks, block_len), 3)
    running_sc = jnp.transpose(running, (0, 2, 1, 3))
    running_pos = jnp.transpose(running, (0, 2, 3, 1))
    scores = jnp.einsum(
        "scihn,scjhn->schij", query_blocks, key_blocks, preferred_element_type=jnp.float32
    )
    row_ids = lax.broadcasted_iota(jnp.int32, (block_len, block_len), 0)
    col_ids = lax.broadcasted_iota(jnp.int32, (block_len, block_len), 1)
    spread = running_sc[..., :, None] - running_sc[..., None, :]
    decays = jnp.exp(jnp.where(row_ids >= col_ids, spread, -jnp.inf))
    mixing = (scores * decays).astype(jnp.bfloat16)
    inner_sum = jnp.einsum(
        "schij,scjhp->scihp", mixing, value_blocks, preferred_element_type=jnp.float32
    )
    to_end = jnp.exp(running_pos[:, :, -1:, :] - running_pos)
    weighted = (key_blocks * to_end[..., None]).astype(jnp.bfloat16)
    local_states = jnp.einsum(
        "scjhn,scjhp->schnp", weighted, value_blocks, preferred_element_type=jnp.float32
    )
    block_logs = running_sc[..., -1]
    return (value_blocks, query_blocks, running_pos, inner_sum, local_states, block_logs)


def entry_states(local_states, block_logs):

    def advance(carried, entry_item):
        update, log_total = entry_item
        return (jnp.exp(log_total)[..., None, None] * carried + update, carried)

    start_state = jnp.zeros(local_states.shape[:1] + local_states.shape[2:], jnp.float32)
    final_state, entries = lax.scan(
        advance, start_state, (jnp.moveaxis(local_states, 1, 0), jnp.moveaxis(block_logs, 1, 0))
    )
    return (final_state, jnp.moveaxis(entries, 0, 1))


def carry_into(final_state, device_log):
    log_totals = lax.all_gather(device_log[None], "seq", axis=0, tiled=True)
    my_index = lax.axis_index("seq")
    ranks_all = lax.iota(jnp.int32, log_totals.shape[0])
    between = jnp.logical_and(
        ranks_all[None, :] > ranks_all[:, None], ranks_all[None, :] < my_index
    ).astype(jnp.float32)
    span_logs = jnp.einsum("dk,ksh->dsh", between, log_totals, precision=lax.Precision.HIGHEST)
    weights = jnp.where((ranks_all < my_index)[:, None, None], jnp.exp(span_logs), 0.0)
    return jnp.sum(
        weights[..., None, None] * lax.all_gather(final_state[None], "seq", axis=0, tiled=True),
        axis=0,
    )


def selective_scan(values, keys_in, queries, log_decay, skip, gain):
    block_len = min(BLOCK, values.shape[1])
    value_blocks, query_blocks, running_pos, inner_sum, local_states, block_logs = block_terms(
        values, keys_in, queries, log_decay, block_len
    )
    final_state, entries = entry_states(local_states, block_logs)
    carried = carry_into(final_state, jnp.sum(block_logs, axis=1))
    before = cumulated(block_logs, 1) - block_logs
    states = (entries + jnp.exp(before)[..., None, None] * carried[:, None]).astype(jnp.bfloat16)
    outer_sum = jnp.einsum(
        "scihn,schnp->scihp", query_blocks, states, preferred_element_type=jnp.float32
    )
    raw_out = (
        inner_sum
        + outer_sum * jnp.exp(running_pos)[..., None]
        + skip[:, None] * value_blocks.astype(jnp.float32)
    )
    scaled = raw_out * lax.rsqrt(jnp.mean(raw_out * raw_out, axis=-1, keepdims=True) + 1e-05)
    normed = (scaled * gain.reshape(skip.shape[0], -1)).astype(jnp.bfloat16)
    return normed.reshape(normed.shape[0], -1, normed.shape[3] * normed.shape[4])


def project_rows(features, w_values, w_keys, w_step):
    slab_count, length, feat_width = features.shape
    head_count = w_values.shape[0]
    split_feat = features.reshape(slab_count, length, head_count, feat_width // head_count)
    values_two = jnp.einsum(
        "slhp,hpk->slhk", split_feat, w_values, preferred_element_type=jnp.float32
    ).astype(jnp.bfloat16)
    keys_two = jnp.einsum(
        "slhp,hpk->slhk", split_feat, w_keys, preferred_element_type=jnp.float32
    ).astype(jnp.bfloat16)
    step_pre = jnp.einsum(
        "slhp,hp->slh", split_feat, w_step, preferred_element_type=jnp.float32
    ).astype(jnp.bfloat16)
    return (values_two, keys_two, step_pre)


def second_scan(values_two, keys_two, step_pre, step_bias, rates_second, skip_second, gain_second):
    slab_count, length, head_count, key_width = keys_two.shape
    step_size = jax.nn.softplus(step_pre.astype(jnp.float32) + step_bias)
    log_decay = -rates_second[None, :, None] * jnp.transpose(step_size, (0, 2, 1))
    return selective_scan(
        values_two.reshape(slab_count, length, -1),
        keys_two[..., :N].reshape(slab_count, length, -1),
        keys_two[..., N:].reshape(slab_count, length, -1),
        log_decay,
        skip_second,
        gain_second,
    )


def columns_from(received):
    slab_count, rows_all, cols_here, last_width = received.shape
    return jnp.transpose(received, (0, 2, 1, 3)).reshape(
        slab_count, cols_here * rows_all, last_width
    )


def local(
    values_first,
    keys_first,
    queries_first,
    steps_first,
    rates_first,
    skip_first,
    gain_first,
    w_values,
    w_keys,
    w_step,
    step_bias,
    rates_second,
    skip_second,
    gain_second,
):
    log_first = -rates_first[None, :, None] * steps_first
    first_out = selective_scan(
        values_first, keys_first, queries_first, log_first, skip_first, gain_first
    )
    slab_count, length, feat_width = first_out.shape
    home_grid = first_out.reshape(slab_count, ROWS_DEV, length // ROWS_DEV, feat_width)
    received = lax.all_to_all(home_grid, "seq", split_axis=2, concat_axis=1, tiled=True)
    rows_all = received.shape[1]
    cols_here = received.shape[2]
    values_two, keys_two, step_pre = project_rows(columns_from(received), w_values, w_keys, w_step)
    result = second_scan(
        values_two, keys_two, step_pre, step_bias, rates_second, skip_second, gain_second
    )
    column_out = result.reshape(received.shape[0], cols_here, rows_all, result.shape[2])
    home_back = lax.all_to_all(column_out, "seq", split_axis=2, concat_axis=1, tiled=True)
    second_home = jnp.transpose(home_back, (0, 2, 1, 3)).reshape(slab_count, length, feat_width)
    return (first_out.astype(jnp.float32) + second_home.astype(jnp.float32)).astype(jnp.bfloat16)


def cumsum_rows(rows, upper):
    high = rows.astype(jnp.bfloat16).astype(jnp.float32)
    rest = rows - high
    mid = rest.astype(jnp.bfloat16).astype(jnp.float32)
    low = rest - mid
    count = rows.shape[0]
    stacked = jnp.concatenate([high, mid, low, jnp.zeros_like(low)], axis=0).astype(jnp.bfloat16)
    sums = jnp.dot(stacked, upper, preferred_element_type=jnp.float32)
    return sums[:count] + sums[count : 2 * count] + sums[2 * count : 3 * count]


def dot_nt(left, right):
    return lax.dot_general(
        left, right, (((1,), (1,)), ((), ())), preferred_element_type=jnp.float32
    )


def dot_tn(left, right):
    return lax.dot_general(
        left, right, (((0,), (0,)), ((), ())), preferred_element_type=jnp.float32
    )


def column_of(run_row, width):
    return jnp.transpose(jnp.broadcast_to(run_row, (width, run_row.shape[1])))


def inner_part(values, keys_in, queries, run_row, run_col, skip):
    length, width = values.shape
    half = length // 2
    lower = lax.broadcasted_iota(jnp.int32, (half, half), 0) >= lax.broadcasted_iota(
        jnp.int32, (half, half), 1
    )
    reps = half // width

    def decay(rows, columns, masked):
        left = jnp.concatenate([run_col[rows]] * reps, axis=1) if reps > 1 else run_col[rows]
        spread = left - run_row[:, columns]
        return jnp.exp(jnp.where(lower, spread, -jnp.inf) if masked else spread)

    top, bottom = slice(0, half), slice(half, length)
    scores_top = dot_nt(queries[top], keys_in[top])
    scores_bottom = dot_nt(queries[bottom], keys_in)
    mix_top = (scores_top * decay(top, top, True)).astype(jnp.bfloat16)
    mix_bottom = jnp.concatenate(
        [
            (scores_bottom[:, top] * decay(bottom, top, False)).astype(jnp.bfloat16),
            (scores_bottom[:, bottom] * decay(bottom, bottom, True)).astype(jnp.bfloat16),
        ],
        axis=1,
    )
    inner = jnp.concatenate(
        [
            jnp.dot(mix_top, values[top], preferred_element_type=jnp.float32),
            jnp.dot(mix_bottom, values, preferred_element_type=jnp.float32),
        ],
        axis=0,
    )
    return inner + skip * values.astype(jnp.float32)


def state_part(values, keys_in, run_col):
    last = run_col[run_col.shape[0] - 1 :, :]
    weighted = (keys_in.astype(jnp.float32) * jnp.exp(last - run_col)).astype(jnp.bfloat16)
    return dot_tn(weighted, values)


def outer_part(queries, run_col, state):
    outer = jnp.dot(queries, state.astype(jnp.bfloat16), preferred_element_type=jnp.float32)
    return jnp.exp(run_col) * outer


def advanced(state, run_col, update):
    return jnp.exp(run_col[run_col.shape[0] - 1 :, :]) * state + update


def norm_factor(raw):
    return lax.rsqrt(jnp.mean(raw * raw, axis=1, keepdims=True) + 1e-05)


def decay_outer(queries, run_col, state):
    outer = jnp.dot(queries, state, preferred_element_type=jnp.float32)
    return jnp.exp(run_col) * outer


def inner_any_order(values, keys_in, queries, run_row, run_col, bias, skip):
    length, width = values.shape
    left = jnp.concatenate([run_col] * (length // width), axis=1)
    scores = dot_nt(queries, keys_in)
    mixing = (scores * jnp.exp(left - run_row + bias)).astype(jnp.bfloat16)
    inner = jnp.dot(mixing, values, preferred_element_type=jnp.float32)
    return inner + skip * values.astype(jnp.float32)


def fused_kernel(parts, heads, side, *refs):
    values, keys_in, queries, steps, w_values, w_keys = refs[:6]
    small_in, out = refs[6:14], refs[14]
    v_buf, k_buf, q_buf, step_buf, wv_buf, wk_buf = refs[15:21]
    small = refs[21:29]
    w_step, gain_first, gain_second = small[:3]
    rates_first, skip_first, step_bias, rates_second, skip_second = small[3:]
    row_buf, col_buf, update_buf, raw_buf, stage_state, stage_raw = refs[29:35]
    state_in, back_in, far_in, rows_in, raw_in, maps_in = refs[35:41]
    first_buf, column_buf, second_buf, home_buf, bias_buf, upper_buf, run_state = refs[41:48]
    own_sem, unit_sem, state_send, rows_send, raw_send, maps_send = refs[48:54]
    state_recv, back_recv, far_recv, rows_recv, raw_recv, maps_recv = refs[54:60]
    first_send, first_recv, second_send, second_recv, ready = refs[60:]
    me = lax.axis_index("seq")
    length, width = raw_buf.shape[1:]
    slabs = parts // heads
    last_part = parts - 1
    rows_here, cols_here = side // parts, length // side
    chunk = rows_here * cols_here
    groups = parts // GROUP
    my_head = lax.rem(me, heads)
    mesh_id = pl.DeviceIdType.MESH
    even = lax.rem(lax.axis_index("head"), 2) == 0

    def chosen(modes):
        if modes[0] == modes[1]:
            return me >= 0 if modes[0] else me < 0
        return even if modes[0] else jnp.logical_not(even)

    maps_two, maps_three = chosen(MAPS_TWO), chosen(MAPS_THREE)
    states_two, states_three = jnp.logical_not(maps_two), jnp.logical_not(maps_three)
    left = me < 2
    started = []

    def send(condition, copy):
        @pl.when(condition)
        def _():
            copy.start()

        started.append((condition, copy))


    def lanes(head):
        return slice(head * width, (head + 1) * width)

    def of_unit(array, unit):
        return array[unit // heads, :, lanes(unit % heads)]

    barrier = pltpu.get_barrier_semaphore()

    def greet(sources, target):
        @pl.when(sources)
        def _():
            pl.semaphore_signal(
                barrier, inc=1, device_id={"seq": target}, device_id_type=mesh_id
            )

    for target in range(1, parts):
        greet(me != target, target)
    greet(me == 1, 0)

    step_copy = pltpu.make_async_copy(steps, step_buf, own_sem.at[0])
    step_copy.start()
    small_copies = [
        pltpu.make_async_copy(src, dst, own_sem.at[3 + index])
        for index, (src, dst) in enumerate(zip(small_in, small))
    ]
    unit_copies = [
        [
            pltpu.make_async_copy(src.at[slab], dst.at[slab], unit_sem.at[kind, slab])
            for slab in range(slabs)
        ]
        for kind, (src, dst) in enumerate(((keys_in, k_buf), (values, v_buf), (queries, q_buf)))
    ]
    weight_copies = [
        pltpu.make_async_copy(w_values.at[my_head], wv_buf, own_sem.at[1]),
        pltpu.make_async_copy(w_keys.at[my_head], wk_buf, own_sem.at[2]),
    ]
    early = [*unit_copies[0], *unit_copies[1]]
    late = [*unit_copies[2], *small_copies[:3], *small_copies[4:], *weight_copies]
    small_copies[3].start()
    for copy in early + late:
        copy.start()

    square = (length, length)
    upper = jnp.where(
        lax.broadcasted_iota(jnp.int32, square, 0) <= lax.broadcasted_iota(jnp.int32, square, 1),
        1.0,
        0.0,
    ).astype(jnp.bfloat16)

    def remote(src, dst, send_sem, recv_sem, target):
        return pltpu.make_async_remote_copy(
            src_ref=src,
            dst_ref=dst,
            send_sem=send_sem,
            recv_sem=recv_sem,
            device_id={"seq": target},
            device_id_type=mesh_id,
        )

    def state_copy(unit, target):
        return remote(
            stage_state.at[unit],
            state_in.at[unit],
            state_send.at[target, unit],
            state_recv.at[unit],
            target,
        )

    def back_copy():
        return remote(stage_state.at[0], back_in, state_send.at[0, 0], back_recv, 0)

    def far_copy(unit, target):
        return remote(
            stage_state.at[unit],
            far_in.at[unit],
            state_send.at[target, unit],
            far_recv.at[unit],
            target,
        )

    def rows_copy(source, target):
        return remote(
            row_buf, rows_in.at[source], rows_send.at[target], rows_recv.at[source], target
        )

    def raw_copy(source, target):
        return remote(
            stage_raw.at[target],
            raw_in.at[source],
            raw_send.at[target],
            raw_recv.at[source],
            target,
        )

    def maps_copy(source, target):
        return remote(
            queries.at[target // heads, :, lanes(target % heads)],
            maps_in.at[source],
            maps_send.at[target],
            maps_recv.at[source],
            target,
        )

    def first_copy(unit, group, source):
        return remote(
            first_buf.at[unit, pl.ds(group * GROUP, GROUP)],
            column_buf.at[pl.ds(group * GROUP, GROUP), source],
            first_send.at[unit, group],
            first_recv.at[source, group],
            unit,
        )

    def second_copy(group, target, source):
        return remote(
            second_buf.at[target, pl.ds(group * GROUP, GROUP)],
            home_buf.at[source, pl.ds(group * GROUP, GROUP)],
            second_send.at[target, group],
            second_recv.at[source, group],
            target,
        )

    step_copy.wait()
    small_copies[3].wait()
    logs = [
        -rates_first[head] * step_buf[slab, head : head + 1, :]
        for slab in range(slabs)
        for head in range(heads)
    ]
    logs = jnp.concatenate(logs + logs[:1] * (-parts % 8), axis=0)
    running = cumsum_rows(logs, upper)
    row_buf[...] = running
    columns_of = [column_of(running[unit : unit + 1], width) for unit in range(parts)]
    for copy in early:
        copy.wait()
    @pl.when(me > 1)
    def _():
        pl.semaphore_wait(barrier, last_part)

    for target in (0, 1):
        send((me == 2) & maps_two, maps_copy(2, target))
        send((me == 3) & maps_three, maps_copy(3, target))
    send(me == 2, maps_copy(2, 3))
    send(me == 3, maps_copy(3, 2))
    updates = [
        state_part(of_unit(v_buf, unit), of_unit(k_buf, unit), columns_of[unit])
        for unit in range(parts)
    ]
    for unit in range(parts):
        stage_state[unit] = updates[unit].astype(jnp.bfloat16)

    @pl.when(me == 0)
    def _():
        pl.semaphore_wait(barrier, 1)

    for unit in range(parts):
        send(me == 0, state_copy(unit, 1))

    @pl.when(me == 0)
    def _():
        state_in[...] = jnp.zeros_like(state_in)

    for unit in range(parts):
        col_buf[unit] = columns_of[unit]
        update_buf[unit] = updates[unit]
    for copy in late:
        copy.wait()
    raws = [
        inner_part(
            of_unit(v_buf, unit),
            of_unit(k_buf, unit),
            of_unit(q_buf, unit),
            running[unit : unit + 1],
            columns_of[unit],
            skip_first[unit % heads],
        )
        for unit in range(parts)
    ]
    for unit in range(parts):
        raw_buf[unit] = raws[unit]
        stage_raw[unit] = raws[unit].astype(jnp.bfloat16)

    for target in (0, 1):
        send((me == 2) & maps_two, raw_copy(2, target))
        send((me == 3) & maps_three, raw_copy(3, target))
    for target in (0, 1):
        send((me == 2) & (maps_two | maps_three), rows_copy(2, target))
        send((me == 3) & maps_three, rows_copy(3, target))
        send((me == 2) & maps_three, far_copy(target, target))
    send(me == 2, rows_copy(2, 3))
    send(me == 3, rows_copy(3, 2))
    for unit in (0, 1):
        send((me == 2) & states_three, far_copy(unit, 3))
    send(me == 2, far_copy(3, 3))
    send(me == 2, raw_copy(2, 3))
    send(me == 3, raw_copy(3, 2))

    def rank_of(index):
        owner, inside = lax.div(index, chunk), lax.rem(index, chunk)
        row, col = lax.div(inside, cols_here), lax.rem(inside, cols_here)
        return col * side + owner * rows_here + row

    rank_sub = rank_of(lax.broadcasted_iota(jnp.int32, (length, width), 0))
    rank_sub = jnp.concatenate([rank_sub] * (length // width), axis=1)
    rank_lane = rank_of(lax.broadcasted_iota(jnp.int32, (8, length), 1))[0:1]
    bias_buf[...] = jnp.where(rank_lane <= rank_sub, 0.0, -jnp.inf)
    upper_buf[...] = jnp.where(rank_sub <= rank_lane, 1.0, 0.0).astype(jnp.bfloat16)

    def ordered(normed):
        return [
            jnp.concatenate(
                [
                    normed[row * side + block * cols_here : row * side + (block + 1) * cols_here]
                    for row in range(rows_here)
                ],
                axis=0,
            ).astype(jnp.bfloat16)
            for block in range(parts)
        ]

    def finish(unit):
        raw = raw_buf[unit] + decay_outer(of_unit(q_buf, unit), col_buf[unit], state_in[unit])
        normed = raw * norm_factor(raw) * gain_first[:, lanes(unit % heads)]
        for block, piece in enumerate(ordered(normed)):
            first_buf[unit, block] = piece

        @pl.when(me == unit)
        def _():
            for block in range(parts):
                column_buf[block, unit] = first_buf[unit, block]

    def send_first(condition, unit):
        for group in range(groups):
            send(condition, first_copy(unit, group, me))

    @pl.when(me == 1)
    def _():
        pl.semaphore_wait(barrier, last_part)
        pl.semaphore_signal(ready, inc=1, device_id={"seq": 0}, device_id_type=mesh_id)

    for unit in ORDER:
        @pl.when(me == 1)
        def _():
            state_copy(unit, 1).wait_recv()
            last = jnp.exp(col_buf[unit, length - 1 :, :])
            carried = last * state_in[unit].astype(jnp.float32) + update_buf[unit]
            stage_state[unit] = carried.astype(jnp.bfloat16)

        if unit > 1:
            send(me == 1, state_copy(unit, unit))
        else:
            send((me == 1) & states_three, state_copy(unit, 3))
            send((me == 1) & states_two, state_copy(unit, 2))
            if unit == 0:
                send((me == 1) & (maps_two | maps_three), back_copy())

    @pl.when(left)
    def _():
        for unit in FINISH:
            finish(unit)

    send_first(me == 0, 1)
    for unit in FINISH:
        if unit != 1:
            send_first(me == 1, unit)

    def state_three(base, unit):
        row = rows_in[2, pl.ds(unit, 1), :]
        last = jnp.exp(jnp.broadcast_to(row[:, length - 1 :], (1, width)))
        carried = last * base.astype(jnp.float32) + far_in[unit].astype(jnp.float32)
        return carried.astype(jnp.bfloat16)

    @pl.when((me == 3) | (left & (maps_two | maps_three)))
    def _():
        rows_copy(2, me).wait_recv()

    for unit in (0, 1):
        @pl.when((me == 2) & states_two)
        def _():
            state_copy(unit, 2).wait_recv()
            finish(unit)

        @pl.when((me == 3) & states_three)
        def _():
            state_copy(unit, 3).wait_recv()
            far_copy(unit, 3).wait_recv()
            state_in[unit] = state_three(state_in[unit], unit)
            finish(unit)

        send_first(((me == 2) & states_two) | ((me == 3) & states_three), unit)

    def pick(head, select):
        chosen_one = select(0)
        for index in range(1, heads):
            chosen_one = jnp.where(head == index, select(index), chosen_one)
        return chosen_one

    gain_one = pick(my_head, lambda h: gain_first[:, lanes(h)])

    def absorb(source, state):
        maps_copy(source, 0).wait_recv()
        raw_copy(source, me).wait_recv()
        run_col = column_of(rows_in[source, pl.ds(me, 1), :], width)
        raw = raw_in[source].astype(jnp.float32) + decay_outer(maps_in[source], run_col, state)
        normed = raw * norm_factor(raw) * gain_one
        for block, piece in enumerate(ordered(normed)):
            column_buf[block, source] = piece

    @pl.when(me == 2)
    def _():
        state_copy(2, 2).wait_recv()
        finish(2)
        rows_copy(3, 2).wait_recv()
        last = jnp.exp(col_buf[2, length - 1 :, :])
        carried = last * state_in[2].astype(jnp.float32) + update_buf[2]
        absorb(3, carried.astype(jnp.bfloat16))

    @pl.when(me == 3)
    def _():
        state_copy(3, 3).wait_recv()
        absorb(2, state_in[3])
        far_copy(3, 3).wait_recv()
        state_in[3] = state_three(state_in[3], 3)
        finish(3)

    @pl.when(me == 0)
    def _():
        pl.semaphore_wait(ready, 1)

    for unit in (3, 2):
        send_first(me == 0, unit)

    for owner in (0, 1):
        if owner == 0:
            @pl.when((me == 0) & (maps_two | maps_three))
            def _():
                back_copy().wait_recv()

        base = back_in if owner == 0 else stage_state.at[1]

        @pl.when((me == owner) & maps_two)
        def _():
            absorb(2, base[...])

        @pl.when((me == owner) & maps_three)
        def _():
            far_copy(owner, owner).wait_recv()
            rows_copy(3, owner).wait_recv()
            absorb(3, state_three(base[...], owner))

    def whole(source):
        if source < 2:
            return me != source
        own = me == (3 if source == 2 else 2)
        absorbed = left & (maps_two if source == 2 else maps_three)
        return jnp.logical_not(own | absorbed | (me == source))

    step_row = pick(my_head, lambda h: w_step[...].astype(jnp.float32)[h : h + 1, :])
    step_rows = jnp.broadcast_to(step_row, (16, width)).astype(jnp.bfloat16)
    gain_two = pick(my_head, lambda h: gain_second[:, lanes(h)])

    def local_terms(columns):
        values_two = jnp.dot(columns, wv_buf[...], preferred_element_type=jnp.float32).astype(
            jnp.bfloat16
        )
        keys_two = jnp.dot(columns, wk_buf[...], preferred_element_type=jnp.float32).astype(
            jnp.bfloat16
        )
        pre = dot_nt(step_rows, columns)[0:8].astype(jnp.bfloat16).astype(jnp.float32)
        shifted = pre + step_bias[my_head]
        soft = jnp.maximum(shifted, 0.0) + jnp.log1p(jnp.exp(-jnp.abs(shifted)))
        run_row = cumsum_rows(-rates_second[my_head] * soft, upper_buf[...])[0:1]
        run_col = column_of(run_row, width)
        half = keys_two.shape[1] // 2
        keys_now, queries_now = keys_two[:, :half], keys_two[:, half:]
        raw = inner_any_order(
            values_two,
            keys_now,
            queries_now,
            run_row,
            run_col,
            bias_buf[...],
            skip_second[my_head],
        )
        return raw, queries_now, run_col, state_part(values_two, keys_now, run_col)

    for group in range(groups):
        for source in range(parts):
            @pl.when(whole(source))
            def _():
                first_copy(me, group, source).wait_recv()

        blocks = range(group * GROUP, (group + 1) * GROUP)
        terms = [local_terms(column_buf[block].reshape(length, width)) for block in blocks]
        for block, (raw, queries_now, run_col, update) in zip(blocks, terms):
            if block == 0:
                state = update
            else:
                before = run_state[...] if block == blocks[0] else state
                raw = raw + outer_part(queries_now, run_col, before)
                state = advanced(before, run_col, update)
            normed = (raw * norm_factor(raw) * gain_two).astype(jnp.bfloat16)
            for target in range(parts):
                piece = normed[target * chunk : (target + 1) * chunk].astype(jnp.float32)
                piece = piece + column_buf[block, target].astype(jnp.float32)
                second_buf[target, block] = piece.astype(jnp.bfloat16)
        run_state[...] = state
        for target in range(parts):
            send(me != target, second_copy(group, target, me))

            @pl.when(me == target)
            def _():
                for block in blocks:
                    home_buf[target, block] = second_buf[target, block]

    for group in range(groups):
        for source in range(parts):
            @pl.when(me != source)
            def _():
                second_copy(group, me, source).wait_recv()

        if (group + 1) * GROUP % 2:
            continue
        for pair in range(max((group + 1) * GROUP - max(GROUP, 2), 0), (group + 1) * GROUP, 2):
            for unit in range(parts):
                total = [home_buf[unit, block].astype(jnp.float32) for block in (pair, pair + 1)]
                for row in range(rows_here):
                    place = slice(row * cols_here, (row + 1) * cols_here)
                    out[
                        unit // heads,
                        pl.ds(row * side + pair * cols_here, 2 * cols_here),
                        lanes(unit % heads),
                    ] = jnp.concatenate([part[place] for part in total], axis=0).astype(
                        jnp.bfloat16
                    )

    for condition, copy in started:
        @pl.when(condition)
        def _():
            copy.wait_send()


def local_fused(
    parts,
    values_first,
    keys_first,
    queries_first,
    steps_first,
    rates_first,
    skip_first,
    gain_first,
    w_values,
    w_keys,
    w_step,
    step_bias,
    rates_second,
    skip_second,
    gain_second,
):
    slab_count, length, feat_width = values_first.shape
    heads = rates_first.shape[0]
    width = feat_width // heads
    side = math.isqrt(parts * length)
    chunk = length // parts
    groups = parts // GROUP
    anywhere = pl.BlockSpec(memory_space=pl.ANY)
    dma = pltpu.SemaphoreType.DMA

    def vmem(dtype, *shape):
        return pltpu.VMEM(shape, dtype)

    bf16, f32 = jnp.bfloat16, jnp.float32
    return pl.pallas_call(
        functools.partial(fused_kernel, parts, heads, side),
        out_shape=jax.ShapeDtypeStruct(values_first.shape, bf16),
        in_specs=[anywhere] * 14,
        out_specs=pl.BlockSpec(memory_space=pltpu.VMEM),
        scratch_shapes=[
            vmem(bf16, *values_first.shape),
            vmem(bf16, *keys_first.shape),
            vmem(bf16, *queries_first.shape),
            vmem(f32, *steps_first.shape),
            vmem(bf16, *w_values.shape[1:]),
            vmem(bf16, *w_keys.shape[1:]),
            vmem(bf16, *w_step.shape),
            vmem(f32, 1, feat_width),
            vmem(f32, 1, feat_width),
        ]
        + [pltpu.SMEM((heads,), f32)] * 5
        + [
            vmem(f32, parts + -parts % 8, length),
            vmem(f32, parts, length, width),
            vmem(f32, parts, width, width),
            vmem(f32, parts, length, width),
            vmem(bf16, parts, width, width),
            vmem(bf16, parts, length, width),
            vmem(bf16, parts, width, width),
            vmem(bf16, width, width),
            vmem(bf16, parts, width, width),
            vmem(f32, parts, parts + -parts % 8, length),
            vmem(bf16, parts, length, width),
            vmem(bf16, parts, length, width),
            vmem(bf16, parts, parts, chunk, width),
            vmem(bf16, parts, parts, chunk, width),
            vmem(bf16, parts, parts, chunk, width),
            vmem(bf16, parts, parts, chunk, width),
            vmem(f32, length, length),
            vmem(bf16, length, length),
            vmem(f32, width, width),
            dma((11,)),
            dma((3, parts)),
            dma((parts, parts)),
            dma((parts,)),
            dma((parts,)),
            dma((parts,)),
            dma((parts,)),
            dma,
            dma((parts,)),
            dma((parts,)),
            dma((parts,)),
            dma((parts,)),
            dma((parts, groups)),
            dma((parts, groups)),
            dma((parts, groups)),
            dma((parts, groups)),
            pltpu.SemaphoreType.REGULAR,
        ],
        compiler_params=pltpu.CompilerParams(
            collective_id=0, has_side_effects=True, vmem_limit_bytes=VMEM_GRANT
        ),
    )(
        *(
            pltpu.with_memory_space_constraint(array, pltpu.HBM)
            for array in (
                values_first,
                keys_first,
                queries_first,
                steps_first,
                w_values,
                w_keys,
                w_step,
                gain_first.reshape(1, -1),
                gain_second.reshape(1, -1),
                rates_first,
                skip_first,
                step_bias,
                rates_second,
                skip_second,
            )
        )
    )


def fits_fused(parts, args):
    values, w_values, w_keys = args[0], args[7], args[8]
    slab_count, length, feat_width = values.shape
    heads = args[4].shape[0]
    side = math.isqrt(parts * length)
    return (
        slab_count * heads == parts
        and parts == len(ORDER)
        and (side // parts) * (length // side) % 16 == 0
        and length <= BLOCK
        and length % 256 == 0
        and side * side == parts * length
        and side % parts == 0
        and length % side == 0
        and (length // side) % 8 == 0
        and feat_width // heads == 128
        and w_values.shape[1:] == (128, 128)
        and w_keys.shape[1:] == (128, 256)
    )


def solution(mesh):
    parts = mesh.shape["seq"]

    def chosen(*args):
        if fits_fused(parts, args):
            return local_fused(parts, *args)
        return local(*args)

    placed = (
        P("slab", "seq", "head"),
        P("slab", "seq", "head"),
        P("slab", "seq", "head"),
        P("slab", "head", "seq"),
        P("head"),
        P("head"),
        P("head"),
        P("head", None, None),
        P("head", None, None),
        P("head", None),
        P("head"),
        P("head"),
        P("head"),
        P("head"),
    )
    return jax.shard_map(
        chosen, mesh=mesh, in_specs=placed, out_specs=P("slab", "seq", "head"), check_vma=False
    )
```

```python
import functools
import math

import jax
import jax.numpy as jnp
from jax import lax
from jax.experimental import pallas as pl
from jax.experimental.pallas import tpu as pltpu
from jax.sharding import PartitionSpec as P

N = 128
BLOCK = 256
ROWS_DEV = 8
VMEM_GRANT = 16 << 20
GROUP = 2
ORDER = (0, 1, 2, 3)
FINISH = (2, 3, 0, 1)
MAPS_TWO = (True, False)
MAPS_THREE = (False, False)
ACROSS_TWO = (True, False)
ACROSS_THREE = (True, True)
CHAIN = (False, True)


def cumulated(terms, axis):
    size = terms.shape[axis]
    ranks = lax.iota(jnp.int32, size)
    upper = (ranks[:, None] <= ranks[None, :]).astype(jnp.float32)
    sums = jnp.einsum(
        "...j,ji->...i",
        jnp.moveaxis(terms, axis, -1),
        upper,
        precision=lax.Precision.HIGHEST,
    )
    return jnp.moveaxis(sums, -1, axis)


def block_terms(values, keys_in, queries, log_decay, block_len):
    slab_count, length, feat_width = values.shape
    head_count = log_decay.shape[1]
    blocks = length // block_len
    value_blocks = values.reshape(
        slab_count, blocks, block_len, head_count, feat_width // head_count
    )
    key_blocks = keys_in.reshape(
        slab_count, blocks, block_len, head_count, keys_in.shape[2] // head_count
    )
    query_blocks = queries.reshape(
        slab_count, blocks, block_len, head_count, queries.shape[2] // head_count
    )
    running = cumulated(log_decay.reshape(slab_count, head_count, blocks, block_len), 3)
    running_sc = jnp.transpose(running, (0, 2, 1, 3))
    running_pos = jnp.transpose(running, (0, 2, 3, 1))
    scores = jnp.einsum(
        "scihn,scjhn->schij", query_blocks, key_blocks, preferred_element_type=jnp.float32
    )
    row_ids = lax.broadcasted_iota(jnp.int32, (block_len, block_len), 0)
    col_ids = lax.broadcasted_iota(jnp.int32, (block_len, block_len), 1)
    spread = running_sc[..., :, None] - running_sc[..., None, :]
    decays = jnp.exp(jnp.where(row_ids >= col_ids, spread, -jnp.inf))
    mixing = (scores * decays).astype(jnp.bfloat16)
    inner_sum = jnp.einsum(
        "schij,scjhp->scihp", mixing, value_blocks, preferred_element_type=jnp.float32
    )
    to_end = jnp.exp(running_pos[:, :, -1:, :] - running_pos)
    weighted = (key_blocks * to_end[..., None]).astype(jnp.bfloat16)
    local_states = jnp.einsum(
        "scjhn,scjhp->schnp", weighted, value_blocks, preferred_element_type=jnp.float32
    )
    block_logs = running_sc[..., -1]
    return (value_blocks, query_blocks, running_pos, inner_sum, local_states, block_logs)


def entry_states(local_states, block_logs):

    def advance(carried, entry_item):
        update, log_total = entry_item
        return (jnp.exp(log_total)[..., None, None] * carried + update, carried)

    start_state = jnp.zeros(local_states.shape[:1] + local_states.shape[2:], jnp.float32)
    final_state, entries = lax.scan(
        advance, start_state, (jnp.moveaxis(local_states, 1, 0), jnp.moveaxis(block_logs, 1, 0))
    )
    return (final_state, jnp.moveaxis(entries, 0, 1))


def carry_into(final_state, device_log):
    log_totals = lax.all_gather(device_log[None], "seq", axis=0, tiled=True)
    my_index = lax.axis_index("seq")
    ranks_all = lax.iota(jnp.int32, log_totals.shape[0])
    between = jnp.logical_and(
        ranks_all[None, :] > ranks_all[:, None], ranks_all[None, :] < my_index
    ).astype(jnp.float32)
    span_logs = jnp.einsum("dk,ksh->dsh", between, log_totals, precision=lax.Precision.HIGHEST)
    weights = jnp.where((ranks_all < my_index)[:, None, None], jnp.exp(span_logs), 0.0)
    return jnp.sum(
        weights[..., None, None] * lax.all_gather(final_state[None], "seq", axis=0, tiled=True),
        axis=0,
    )


def selective_scan(values, keys_in, queries, log_decay, skip, gain):
    block_len = min(BLOCK, values.shape[1])
    value_blocks, query_blocks, running_pos, inner_sum, local_states, block_logs = block_terms(
        values, keys_in, queries, log_decay, block_len
    )
    final_state, entries = entry_states(local_states, block_logs)
    carried = carry_into(final_state, jnp.sum(block_logs, axis=1))
    before = cumulated(block_logs, 1) - block_logs
    states = (entries + jnp.exp(before)[..., None, None] * carried[:, None]).astype(jnp.bfloat16)
    outer_sum = jnp.einsum(
        "scihn,schnp->scihp", query_blocks, states, preferred_element_type=jnp.float32
    )
    raw_out = (
        inner_sum
        + outer_sum * jnp.exp(running_pos)[..., None]
        + skip[:, None] * value_blocks.astype(jnp.float32)
    )
    scaled = raw_out * lax.rsqrt(jnp.mean(raw_out * raw_out, axis=-1, keepdims=True) + 1e-05)
    normed = (scaled * gain.reshape(skip.shape[0], -1)).astype(jnp.bfloat16)
    return normed.reshape(normed.shape[0], -1, normed.shape[3] * normed.shape[4])


def project_rows(features, w_values, w_keys, w_step):
    slab_count, length, feat_width = features.shape
    head_count = w_values.shape[0]
    split_feat = features.reshape(slab_count, length, head_count, feat_width // head_count)
    values_two = jnp.einsum(
        "slhp,hpk->slhk", split_feat, w_values, preferred_element_type=jnp.float32
    ).astype(jnp.bfloat16)
    keys_two = jnp.einsum(
        "slhp,hpk->slhk", split_feat, w_keys, preferred_element_type=jnp.float32
    ).astype(jnp.bfloat16)
    step_pre = jnp.einsum(
        "slhp,hp->slh", split_feat, w_step, preferred_element_type=jnp.float32
    ).astype(jnp.bfloat16)
    return (values_two, keys_two, step_pre)


def second_scan(values_two, keys_two, step_pre, step_bias, rates_second, skip_second, gain_second):
    slab_count, length, head_count, key_width = keys_two.shape
    step_size = jax.nn.softplus(step_pre.astype(jnp.float32) + step_bias)
    log_decay = -rates_second[None, :, None] * jnp.transpose(step_size, (0, 2, 1))
    return selective_scan(
        values_two.reshape(slab_count, length, -1),
        keys_two[..., :N].reshape(slab_count, length, -1),
        keys_two[..., N:].reshape(slab_count, length, -1),
        log_decay,
        skip_second,
        gain_second,
    )


def columns_from(received):
    slab_count, rows_all, cols_here, last_width = received.shape
    return jnp.transpose(received, (0, 2, 1, 3)).reshape(
        slab_count, cols_here * rows_all, last_width
    )


def local(
    values_first,
    keys_first,
    queries_first,
    steps_first,
    rates_first,
    skip_first,
    gain_first,
    w_values,
    w_keys,
    w_step,
    step_bias,
    rates_second,
    skip_second,
    gain_second,
):
    log_first = -rates_first[None, :, None] * steps_first
    first_out = selective_scan(
        values_first, keys_first, queries_first, log_first, skip_first, gain_first
    )
    slab_count, length, feat_width = first_out.shape
    home_grid = first_out.reshape(slab_count, ROWS_DEV, length // ROWS_DEV, feat_width)
    received = lax.all_to_all(home_grid, "seq", split_axis=2, concat_axis=1, tiled=True)
    rows_all = received.shape[1]
    cols_here = received.shape[2]
    values_two, keys_two, step_pre = project_rows(columns_from(received), w_values, w_keys, w_step)
    result = second_scan(
        values_two, keys_two, step_pre, step_bias, rates_second, skip_second, gain_second
    )
    column_out = result.reshape(received.shape[0], cols_here, rows_all, result.shape[2])
    home_back = lax.all_to_all(column_out, "seq", split_axis=2, concat_axis=1, tiled=True)
    second_home = jnp.transpose(home_back, (0, 2, 1, 3)).reshape(slab_count, length, feat_width)
    return (first_out.astype(jnp.float32) + second_home.astype(jnp.float32)).astype(jnp.bfloat16)


def cumsum_rows(rows, upper):
    high = rows.astype(jnp.bfloat16).astype(jnp.float32)
    rest = rows - high
    mid = rest.astype(jnp.bfloat16).astype(jnp.float32)
    low = rest - mid
    count = rows.shape[0]
    stacked = jnp.concatenate([high, mid, low, jnp.zeros_like(low)], axis=0).astype(jnp.bfloat16)
    sums = jnp.dot(stacked, upper, preferred_element_type=jnp.float32)
    return sums[:count] + sums[count : 2 * count] + sums[2 * count : 3 * count]


def dot_nt(left, right):
    return lax.dot_general(
        left, right, (((1,), (1,)), ((), ())), preferred_element_type=jnp.float32
    )


def dot_tn(left, right):
    return lax.dot_general(
        left, right, (((0,), (0,)), ((), ())), preferred_element_type=jnp.float32
    )


def column_of(run_row, width):
    return jnp.transpose(jnp.broadcast_to(run_row, (width, run_row.shape[1])))


def inner_part(values, keys_in, queries, run_row, run_col, skip):
    length, width = values.shape
    half = length // 2
    lower = lax.broadcasted_iota(jnp.int32, (half, half), 0) >= lax.broadcasted_iota(
        jnp.int32, (half, half), 1
    )
    reps = half // width

    def decay(rows, columns, masked):
        left = jnp.concatenate([run_col[rows]] * reps, axis=1) if reps > 1 else run_col[rows]
        spread = left - run_row[:, columns]
        return jnp.exp(jnp.where(lower, spread, -jnp.inf) if masked else spread)

    top, bottom = slice(0, half), slice(half, length)
    scores_top = dot_nt(queries[top], keys_in[top])
    scores_bottom = dot_nt(queries[bottom], keys_in)
    mix_top = (scores_top * decay(top, top, True)).astype(jnp.bfloat16)
    mix_bottom = jnp.concatenate(
        [
            (scores_bottom[:, top] * decay(bottom, top, False)).astype(jnp.bfloat16),
            (scores_bottom[:, bottom] * decay(bottom, bottom, True)).astype(jnp.bfloat16),
        ],
        axis=1,
    )
    inner = jnp.concatenate(
        [
            jnp.dot(mix_top, values[top], preferred_element_type=jnp.float32),
            jnp.dot(mix_bottom, values, preferred_element_type=jnp.float32),
        ],
        axis=0,
    )
    return inner + skip * values.astype(jnp.float32)


def state_part(values, keys_in, run_col):
    last = run_col[run_col.shape[0] - 1 :, :]
    weighted = (keys_in.astype(jnp.float32) * jnp.exp(last - run_col)).astype(jnp.bfloat16)
    return dot_tn(weighted, values)


def outer_part(queries, run_col, state):
    outer = jnp.dot(queries, state.astype(jnp.bfloat16), preferred_element_type=jnp.float32)
    return jnp.exp(run_col) * outer


def advanced(state, run_col, update):
    return jnp.exp(run_col[run_col.shape[0] - 1 :, :]) * state + update


def norm_factor(raw):
    return lax.rsqrt(jnp.mean(raw * raw, axis=1, keepdims=True) + 1e-05)


def decay_outer(queries, run_col, state):
    outer = jnp.dot(queries, state, preferred_element_type=jnp.float32)
    return jnp.exp(run_col) * outer


def inner_any_order(values, keys_in, queries, run_row, run_col, bias, skip):
    length, width = values.shape
    left = jnp.concatenate([run_col] * (length // width), axis=1)
    scores = dot_nt(queries, keys_in)
    mixing = (scores * jnp.exp(left - run_row + bias)).astype(jnp.bfloat16)
    inner = jnp.dot(mixing, values, preferred_element_type=jnp.float32)
    return inner + skip * values.astype(jnp.float32)


def fused_kernel(parts, heads, side, *refs):
    values, keys_in, queries, steps, w_values, w_keys = refs[:6]
    small_in, out = refs[6:14], refs[14]
    v_buf, k_buf, q_buf, step_buf, wv_buf, wk_buf = refs[15:21]
    small = refs[21:29]
    w_step, gain_first, gain_second = small[:3]
    rates_first, skip_first, step_bias, rates_second, skip_second = small[3:]
    row_buf, col_buf, update_buf, raw_buf, stage_state, stage_raw = refs[29:35]
    state_in, back_in, far_in, rows_in, raw_in, maps_in = refs[35:41]
    first_buf, column_buf, second_buf, home_buf, bias_buf, upper_buf, run_state = refs[41:48]
    own_sem, unit_sem, state_send, rows_send, raw_send, maps_send = refs[48:54]
    state_recv, back_recv, far_recv, rows_recv, raw_recv, maps_recv = refs[54:60]
    first_send, first_recv, second_send, second_recv, ready = refs[60:]
    me = lax.axis_index("seq")
    length, width = raw_buf.shape[1:]
    slabs = parts // heads
    last_part = parts - 1
    rows_here, cols_here = side // parts, length // side
    chunk = rows_here * cols_here
    groups = parts // GROUP
    my_head = lax.rem(me, heads)
    mesh_id = pl.DeviceIdType.MESH
    even = lax.rem(lax.axis_index("head"), 2) == 0

    def chosen(modes):
        if modes[0] == modes[1]:
            return me >= 0 if modes[0] else me < 0
        return even if modes[0] else jnp.logical_not(even)

    maps_two, maps_three = chosen(MAPS_TWO), chosen(MAPS_THREE)
    chain = chosen(CHAIN)
    far_needed = jnp.logical_not(maps_three | chain)
    across_two, across_three = chosen(ACROSS_TWO), chosen(ACROSS_THREE)
    whole_two, whole_three = jnp.logical_not(across_two), jnp.logical_not(across_three)
    states_two, states_three = jnp.logical_not(maps_two), jnp.logical_not(maps_three)
    left = me < 2
    started = []

    def send(condition, copy):
        @pl.when(condition)
        def _():
            copy.start()

        started.append((condition, copy))


    def lanes(head):
        return slice(head * width, (head + 1) * width)

    def of_unit(array, unit):
        return array[unit // heads, :, lanes(unit % heads)]

    barrier = pltpu.get_barrier_semaphore()

    def greet(sources, target):
        @pl.when(sources)
        def _():
            pl.semaphore_signal(
                barrier, inc=1, device_id={"seq": target}, device_id_type=mesh_id
            )

    for target in range(1, parts):
        greet(me != target, target)
    greet(me == 1, 0)

    step_copy = pltpu.make_async_copy(steps, step_buf, own_sem.at[0])
    step_copy.start()
    small_copies = [
        pltpu.make_async_copy(src, dst, own_sem.at[3 + index])
        for index, (src, dst) in enumerate(zip(small_in, small))
    ]
    unit_copies = [
        [
            pltpu.make_async_copy(src.at[slab], dst.at[slab], unit_sem.at[kind, slab])
            for slab in range(slabs)
        ]
        for kind, (src, dst) in enumerate(((keys_in, k_buf), (values, v_buf), (queries, q_buf)))
    ]
    weight_copies = [
        pltpu.make_async_copy(w_values.at[my_head], wv_buf, own_sem.at[1]),
        pltpu.make_async_copy(w_keys.at[my_head], wk_buf, own_sem.at[2]),
    ]
    early = [*unit_copies[0], *unit_copies[1]]
    late = [*unit_copies[2], *small_copies[:3], *small_copies[4:], *weight_copies]
    small_copies[3].start()
    for copy in early + late:
        copy.start()

    square = (length, length)
    upper = jnp.where(
        lax.broadcasted_iota(jnp.int32, square, 0) <= lax.broadcasted_iota(jnp.int32, square, 1),
        1.0,
        0.0,
    ).astype(jnp.bfloat16)

    def remote(src, dst, send_sem, recv_sem, target):
        return pltpu.make_async_remote_copy(
            src_ref=src,
            dst_ref=dst,
            send_sem=send_sem,
            recv_sem=recv_sem,
            device_id={"seq": target},
            device_id_type=mesh_id,
        )

    def state_copy(unit, target):
        return remote(
            stage_state.at[unit],
            state_in.at[unit],
            state_send.at[target, unit],
            state_recv.at[unit],
            target,
        )

    def back_copy():
        return remote(stage_state.at[0], back_in, state_send.at[0, 0], back_recv, 0)

    def far_copy(unit, target):
        return remote(
            stage_state.at[unit],
            far_in.at[unit],
            state_send.at[target, unit],
            far_recv.at[unit],
            target,
        )

    def rows_copy(source, target):
        return remote(
            row_buf, rows_in.at[source], rows_send.at[target], rows_recv.at[source], target
        )

    def raw_copy(source, target):
        return remote(
            stage_raw.at[target],
            raw_in.at[source],
            raw_send.at[target],
            raw_recv.at[source],
            target,
        )

    def maps_copy(source, target):
        return remote(
            queries.at[target // heads, :, lanes(target % heads)],
            maps_in.at[source],
            maps_send.at[target],
            maps_recv.at[source],
            target,
        )

    def first_copy(unit, group, source):
        return remote(
            first_buf.at[unit, pl.ds(group * GROUP, GROUP)],
            column_buf.at[pl.ds(group * GROUP, GROUP), source],
            first_send.at[unit, group],
            first_recv.at[source, group],
            unit,
        )

    def second_copy(group, target, source):
        return remote(
            second_buf.at[target, pl.ds(group * GROUP, GROUP)],
            home_buf.at[source, pl.ds(group * GROUP, GROUP)],
            second_send.at[target, group],
            second_recv.at[source, group],
            target,
        )

    step_copy.wait()
    small_copies[3].wait()
    logs = [
        -rates_first[head] * step_buf[slab, head : head + 1, :]
        for slab in range(slabs)
        for head in range(heads)
    ]
    logs = jnp.concatenate(logs + logs[:1] * (-parts % 8), axis=0)
    running = cumsum_rows(logs, upper)
    row_buf[...] = running
    columns_of = [column_of(running[unit : unit + 1], width) for unit in range(parts)]
    for copy in early:
        copy.wait()
    @pl.when(me > 1)
    def _():
        pl.semaphore_wait(barrier, last_part)

    for target in (0, 1):
        send((me == 2) & maps_two, maps_copy(2, target))
        send((me == 3) & maps_three, maps_copy(3, target))
    send((me == 3) & across_three, maps_copy(3, 2))
    updates = [
        state_part(of_unit(v_buf, unit), of_unit(k_buf, unit), columns_of[unit])
        for unit in range(parts)
    ]
    for unit in range(parts):
        stage_state[unit] = updates[unit].astype(jnp.bfloat16)

    rows_right = far_needed | across_two | whole_three
    send((me == 2) & rows_right, rows_copy(2, 3))
    for unit in (0, 1):
        send((me == 2) & far_needed, far_copy(unit, 3))
    send((me == 2) & across_two, far_copy(3, 3))
    send((me == 2) & whole_three, far_copy(2, 3))
    send((me == 2) & across_two, maps_copy(2, 3))
    for target in (0, 1):
        send((me == 2) & (maps_two | maps_three), rows_copy(2, target))
        send((me == 3) & maps_three, rows_copy(3, target))
        send((me == 2) & maps_three, far_copy(target, target))
    send((me == 3) & across_three, rows_copy(3, 2))

    @pl.when(me == 0)
    def _():
        pl.semaphore_wait(barrier, 1)

    for unit in range(parts):
        send(me == 0, state_copy(unit, 1))

    @pl.when(me == 0)
    def _():
        state_in[...] = jnp.zeros_like(state_in)

    for unit in range(parts):
        col_buf[unit] = columns_of[unit]
        update_buf[unit] = updates[unit]
    for copy in late:
        copy.wait()
    raws = [
        inner_part(
            of_unit(v_buf, unit),
            of_unit(k_buf, unit),
            of_unit(q_buf, unit),
            running[unit : unit + 1],
            columns_of[unit],
            skip_first[unit % heads],
        )
        for unit in range(parts)
    ]
    for unit in range(parts):
        raw_buf[unit] = raws[unit]
        stage_raw[unit] = raws[unit].astype(jnp.bfloat16)

    for target in (0, 1):
        send((me == 2) & maps_two, raw_copy(2, target))
        send((me == 3) & maps_three, raw_copy(3, target))
    send((me == 2) & across_two, raw_copy(2, 3))
    send((me == 3) & across_three, raw_copy(3, 2))

    def rank_of(index):
        owner, inside = lax.div(index, chunk), lax.rem(index, chunk)
        row, col = lax.div(inside, cols_here), lax.rem(inside, cols_here)
        return col * side + owner * rows_here + row

    rank_sub = rank_of(lax.broadcasted_iota(jnp.int32, (length, width), 0))
    rank_sub = jnp.concatenate([rank_sub] * (length // width), axis=1)
    rank_lane = rank_of(lax.broadcasted_iota(jnp.int32, (8, length), 1))[0:1]
    bias_buf[...] = jnp.where(rank_lane <= rank_sub, 0.0, -jnp.inf)
    upper_buf[...] = jnp.where(rank_sub <= rank_lane, 1.0, 0.0).astype(jnp.bfloat16)

    def ordered(normed):
        return [
            jnp.concatenate(
                [
                    normed[row * side + block * cols_here : row * side + (block + 1) * cols_here]
                    for row in range(rows_here)
                ],
                axis=0,
            ).astype(jnp.bfloat16)
            for block in range(parts)
        ]

    def finish(unit):
        raw = raw_buf[unit] + decay_outer(of_unit(q_buf, unit), col_buf[unit], state_in[unit])
        normed = raw * norm_factor(raw) * gain_first[:, lanes(unit % heads)]
        for block, piece in enumerate(ordered(normed)):
            first_buf[unit, block] = piece

        @pl.when(me == unit)
        def _():
            for block in range(parts):
                column_buf[block, unit] = first_buf[unit, block]

    def send_first(condition, unit):
        for group in range(groups):
            send(condition, first_copy(unit, group, me))

    @pl.when(me == 1)
    def _():
        pl.semaphore_wait(barrier, last_part)
        pl.semaphore_signal(ready, inc=1, device_id={"seq": 0}, device_id_type=mesh_id)

    for unit in ORDER:
        @pl.when(me == 1)
        def _():
            state_copy(unit, 1).wait_recv()
            last = jnp.exp(col_buf[unit, length - 1 :, :])
            carried = last * state_in[unit].astype(jnp.float32) + update_buf[unit]
            stage_state[unit] = carried.astype(jnp.bfloat16)

        if unit > 1:
            send((me == 1) & (across_two if unit == 3 else whole_three), state_copy(unit, 3))
            send((me == 1) & (whole_two if unit == 3 else me == 1), state_copy(unit, 2))
        else:
            send((me == 1) & far_needed, state_copy(unit, 3))
            send((me == 1) & (states_two | chain), state_copy(unit, 2))
            if unit == 0:
                send((me == 1) & (maps_two | maps_three), back_copy())

    @pl.when(left)
    def _():
        for unit in FINISH:
            finish(unit)

    send_first(me == 0, 1)
    for unit in FINISH:
        if unit != 1:
            send_first(me == 1, unit)

    def state_three(base, unit):
        row = rows_in[2, pl.ds(unit, 1), :]
        last = jnp.exp(jnp.broadcast_to(row[:, length - 1 :], (1, width)))
        carried = last * base.astype(jnp.float32) + far_in[unit].astype(jnp.float32)
        return carried.astype(jnp.bfloat16)

    @pl.when(((me == 3) & rows_right) | (left & (maps_two | maps_three)))
    def _():
        rows_copy(2, me).wait_recv()

    def advance(unit):
        state_copy(unit, 2).wait_recv()
        last = jnp.exp(col_buf[unit, length - 1 :, :])
        carried = last * state_in[unit].astype(jnp.float32) + update_buf[unit]
        stage_state[unit] = carried.astype(jnp.bfloat16)

    for unit in (0, 1):
        @pl.when((me == 2) & (states_two | chain))
        def _():
            advance(unit)

        send((me == 2) & chain, state_copy(unit, 3))

        @pl.when((me == 2) & states_two)
        def _():
            finish(unit)

        @pl.when((me == 3) & states_three)
        def _():
            state_copy(unit, 3).wait_recv()

            @pl.when(far_needed)
            def _():
                far_copy(unit, 3).wait_recv()
                state_in[unit] = state_three(state_in[unit], unit)

            finish(unit)

        send_first(((me == 2) & states_two) | ((me == 3) & states_three), unit)

    def pick(head, select):
        chosen_one = select(0)
        for index in range(1, heads):
            chosen_one = jnp.where(head == index, select(index), chosen_one)
        return chosen_one

    gain_one = pick(my_head, lambda h: gain_first[:, lanes(h)])

    def absorb(source, state):
        maps_copy(source, 0).wait_recv()
        raw_copy(source, me).wait_recv()
        run_col = column_of(rows_in[source, pl.ds(me, 1), :], width)
        raw = raw_in[source].astype(jnp.float32) + decay_outer(maps_in[source], run_col, state)
        normed = raw * norm_factor(raw) * gain_one
        for block, piece in enumerate(ordered(normed)):
            column_buf[block, source] = piece

    @pl.when((me == 2) & whole_two)
    def _():
        advance(3)

    send((me == 2) & whole_two, state_copy(3, 3))

    @pl.when((me == 2) & whole_two)
    def _():
        finish(3)

    send_first((me == 2) & whole_two, 3)

    @pl.when((me == 3) & whole_three)
    def _():
        state_copy(2, 3).wait_recv()
        far_copy(2, 3).wait_recv()
        state_in[2] = state_three(state_in[2], 2)
        finish(2)

    send_first((me == 3) & whole_three, 2)

    @pl.when(me == 2)
    def _():
        state_copy(2, 2).wait_recv()
        finish(2)

    @pl.when((me == 2) & across_three)
    def _():
        rows_copy(3, 2).wait_recv()
        last = jnp.exp(col_buf[2, length - 1 :, :])
        carried = last * state_in[2].astype(jnp.float32) + update_buf[2]
        absorb(3, carried.astype(jnp.bfloat16))

    @pl.when(me == 3)
    def _():
        state_copy(3, 3).wait_recv()

        @pl.when(across_two)
        def _():
            absorb(2, state_in[3])

            far_copy(3, 3).wait_recv()
            state_in[3] = state_three(state_in[3], 3)

        finish(3)

    @pl.when(me == 0)
    def _():
        pl.semaphore_wait(ready, 1)

    for unit in (3, 2):
        send_first(me == 0, unit)

    for owner in (0, 1):
        if owner == 0:
            @pl.when((me == 0) & (maps_two | maps_three))
            def _():
                back_copy().wait_recv()

        base = back_in if owner == 0 else stage_state.at[1]

        @pl.when((me == owner) & maps_two)
        def _():
            absorb(2, base[...])

        @pl.when((me == owner) & maps_three)
        def _():
            far_copy(owner, owner).wait_recv()
            rows_copy(3, owner).wait_recv()
            absorb(3, state_three(base[...], owner))

    def whole(source):
        if source < 2:
            return me != source
        own = (me == 3) & across_two if source == 2 else (me == 2) & across_three
        absorbed = left & (maps_two if source == 2 else maps_three)
        return jnp.logical_not(own | absorbed | (me == source))

    step_row = pick(my_head, lambda h: w_step[...].astype(jnp.float32)[h : h + 1, :])
    step_rows = jnp.broadcast_to(step_row, (16, width)).astype(jnp.bfloat16)
    gain_two = pick(my_head, lambda h: gain_second[:, lanes(h)])

    def local_terms(columns):
        values_two = jnp.dot(columns, wv_buf[...], preferred_element_type=jnp.float32).astype(
            jnp.bfloat16
        )
        keys_two = jnp.dot(columns, wk_buf[...], preferred_element_type=jnp.float32).astype(
            jnp.bfloat16
        )
        pre = dot_nt(step_rows, columns)[0:8].astype(jnp.bfloat16).astype(jnp.float32)
        shifted = pre + step_bias[my_head]
        soft = jnp.maximum(shifted, 0.0) + jnp.log1p(jnp.exp(-jnp.abs(shifted)))
        run_row = cumsum_rows(-rates_second[my_head] * soft, upper_buf[...])[0:1]
        run_col = column_of(run_row, width)
        half = keys_two.shape[1] // 2
        keys_now, queries_now = keys_two[:, :half], keys_two[:, half:]
        raw = inner_any_order(
            values_two,
            keys_now,
            queries_now,
            run_row,
            run_col,
            bias_buf[...],
            skip_second[my_head],
        )
        return raw, queries_now, run_col, state_part(values_two, keys_now, run_col)

    for group in range(groups):
        for source in range(parts):
            @pl.when(whole(source))
            def _():
                first_copy(me, group, source).wait_recv()

        blocks = range(group * GROUP, (group + 1) * GROUP)
        terms = [local_terms(column_buf[block].reshape(length, width)) for block in blocks]
        for block, (raw, queries_now, run_col, update) in zip(blocks, terms):
            if block == 0:
                state = update
            else:
                before = run_state[...] if block == blocks[0] else state
                raw = raw + outer_part(queries_now, run_col, before)
                state = advanced(before, run_col, update)
            normed = (raw * norm_factor(raw) * gain_two).astype(jnp.bfloat16)
            for target in range(parts):
                piece = normed[target * chunk : (target + 1) * chunk].astype(jnp.float32)
                piece = piece + column_buf[block, target].astype(jnp.float32)
                second_buf[target, block] = piece.astype(jnp.bfloat16)
        run_state[...] = state
        for target in range(parts):
            send(me != target, second_copy(group, target, me))

            @pl.when(me == target)
            def _():
                for block in blocks:
                    home_buf[target, block] = second_buf[target, block]

    for group in range(groups):
        for source in range(parts):
            @pl.when(me != source)
            def _():
                second_copy(group, me, source).wait_recv()

        if (group + 1) * GROUP % 2:
            continue
        for pair in range(max((group + 1) * GROUP - max(GROUP, 2), 0), (group + 1) * GROUP, 2):
            for unit in range(parts):
                total = [home_buf[unit, block].astype(jnp.float32) for block in (pair, pair + 1)]
                for row in range(rows_here):
                    place = slice(row * cols_here, (row + 1) * cols_here)
                    out[
                        unit // heads,
                        pl.ds(row * side + pair * cols_here, 2 * cols_here),
                        lanes(unit % heads),
                    ] = jnp.concatenate([part[place] for part in total], axis=0).astype(
                        jnp.bfloat16
                    )

    for condition, copy in started:
        @pl.when(condition)
        def _():
            copy.wait_send()


def local_fused(
    parts,
    values_first,
    keys_first,
    queries_first,
    steps_first,
    rates_first,
    skip_first,
    gain_first,
    w_values,
    w_keys,
    w_step,
    step_bias,
    rates_second,
    skip_second,
    gain_second,
):
    slab_count, length, feat_width = values_first.shape
    heads = rates_first.shape[0]
    width = feat_width // heads
    side = math.isqrt(parts * length)
    chunk = length // parts
    groups = parts // GROUP
    anywhere = pl.BlockSpec(memory_space=pl.ANY)
    dma = pltpu.SemaphoreType.DMA

    def vmem(dtype, *shape):
        return pltpu.VMEM(shape, dtype)

    bf16, f32 = jnp.bfloat16, jnp.float32
    return pl.pallas_call(
        functools.partial(fused_kernel, parts, heads, side),
        out_shape=jax.ShapeDtypeStruct(values_first.shape, bf16),
        in_specs=[anywhere] * 14,
        out_specs=pl.BlockSpec(memory_space=pltpu.VMEM),
        scratch_shapes=[
            vmem(bf16, *values_first.shape),
            vmem(bf16, *keys_first.shape),
            vmem(bf16, *queries_first.shape),
            vmem(f32, *steps_first.shape),
            vmem(bf16, *w_values.shape[1:]),
            vmem(bf16, *w_keys.shape[1:]),
            vmem(bf16, *w_step.shape),
            vmem(f32, 1, feat_width),
            vmem(f32, 1, feat_width),
        ]
        + [pltpu.SMEM((heads,), f32)] * 5
        + [
            vmem(f32, parts + -parts % 8, length),
            vmem(f32, parts, length, width),
            vmem(f32, parts, width, width),
            vmem(f32, parts, length, width),
            vmem(bf16, parts, width, width),
            vmem(bf16, parts, length, width),
            vmem(bf16, parts, width, width),
            vmem(bf16, width, width),
            vmem(bf16, parts, width, width),
            vmem(f32, parts, parts + -parts % 8, length),
            vmem(bf16, parts, length, width),
            vmem(bf16, parts, length, width),
            vmem(bf16, parts, parts, chunk, width),
            vmem(bf16, parts, parts, chunk, width),
            vmem(bf16, parts, parts, chunk, width),
            vmem(bf16, parts, parts, chunk, width),
            vmem(f32, length, length),
            vmem(bf16, length, length),
            vmem(f32, width, width),
            dma((11,)),
            dma((3, parts)),
            dma((parts, parts)),
            dma((parts,)),
            dma((parts,)),
            dma((parts,)),
            dma((parts,)),
            dma,
            dma((parts,)),
            dma((parts,)),
            dma((parts,)),
            dma((parts,)),
            dma((parts, groups)),
            dma((parts, groups)),
            dma((parts, groups)),
            dma((parts, groups)),
            pltpu.SemaphoreType.REGULAR,
        ],
        compiler_params=pltpu.CompilerParams(
            collective_id=0, has_side_effects=True, vmem_limit_bytes=VMEM_GRANT
        ),
    )(
        *(
            pltpu.with_memory_space_constraint(array, pltpu.HBM)
            for array in (
                values_first,
                keys_first,
                queries_first,
                steps_first,
                w_values,
                w_keys,
                w_step,
                gain_first.reshape(1, -1),
                gain_second.reshape(1, -1),
                rates_first,
                skip_first,
                step_bias,
                rates_second,
                skip_second,
            )
        )
    )


def fits_fused(parts, args):
    values, w_values, w_keys = args[0], args[7], args[8]
    slab_count, length, feat_width = values.shape
    heads = args[4].shape[0]
    side = math.isqrt(parts * length)
    return (
        slab_count * heads == parts
        and parts == len(ORDER)
        and (side // parts) * (length // side) % 16 == 0
        and length <= BLOCK
        and length % 256 == 0
        and side * side == parts * length
        and side % parts == 0
        and length % side == 0
        and (length // side) % 8 == 0
        and feat_width // heads == 128
        and w_values.shape[1:] == (128, 128)
        and w_keys.shape[1:] == (128, 256)
    )


def solution(mesh):
    parts = mesh.shape["seq"]

    def chosen(*args):
        if fits_fused(parts, args):
            return local_fused(parts, *args)
        return local(*args)

    placed = (
        P("slab", "seq", "head"),
        P("slab", "seq", "head"),
        P("slab", "seq", "head"),
        P("slab", "head", "seq"),
        P("head"),
        P("head"),
        P("head"),
        P("head", None, None),
        P("head", None, None),
        P("head", None),
        P("head"),
        P("head"),
        P("head"),
        P("head"),
    )
    return jax.shard_map(
        chosen, mesh=mesh, in_specs=placed, out_specs=P("slab", "seq", "head"), check_vma=False
    )
```

```python
import functools
import math

import jax
import jax.numpy as jnp
from jax import lax
from jax.experimental import pallas as pl
from jax.experimental.pallas import tpu as pltpu
from jax.sharding import PartitionSpec as P

N = 128
BLOCK = 256
ROWS_DEV = 8
VMEM_GRANT = 16 << 20
GROUP = 2
ORDER = (0, 1, 2, 3)
FINISH = ((2, 3), (0,), (1,))
MAPS_TWO = (True, False)
MAPS_THREE = (False, False)
ACROSS_TWO = (True, False)
ACROSS_THREE = (True, True)
CHAIN = (False, True)


def cumulated(terms, axis):
    size = terms.shape[axis]
    ranks = lax.iota(jnp.int32, size)
    upper = (ranks[:, None] <= ranks[None, :]).astype(jnp.float32)
    sums = jnp.einsum(
        "...j,ji->...i",
        jnp.moveaxis(terms, axis, -1),
        upper,
        precision=lax.Precision.HIGHEST,
    )
    return jnp.moveaxis(sums, -1, axis)


def block_terms(values, keys_in, queries, log_decay, block_len):
    slab_count, length, feat_width = values.shape
    head_count = log_decay.shape[1]
    blocks = length // block_len
    value_blocks = values.reshape(
        slab_count, blocks, block_len, head_count, feat_width // head_count
    )
    key_blocks = keys_in.reshape(
        slab_count, blocks, block_len, head_count, keys_in.shape[2] // head_count
    )
    query_blocks = queries.reshape(
        slab_count, blocks, block_len, head_count, queries.shape[2] // head_count
    )
    running = cumulated(log_decay.reshape(slab_count, head_count, blocks, block_len), 3)
    running_sc = jnp.transpose(running, (0, 2, 1, 3))
    running_pos = jnp.transpose(running, (0, 2, 3, 1))
    scores = jnp.einsum(
        "scihn,scjhn->schij", query_blocks, key_blocks, preferred_element_type=jnp.float32
    )
    row_ids = lax.broadcasted_iota(jnp.int32, (block_len, block_len), 0)
    col_ids = lax.broadcasted_iota(jnp.int32, (block_len, block_len), 1)
    spread = running_sc[..., :, None] - running_sc[..., None, :]
    decays = jnp.exp(jnp.where(row_ids >= col_ids, spread, -jnp.inf))
    mixing = (scores * decays).astype(jnp.bfloat16)
    inner_sum = jnp.einsum(
        "schij,scjhp->scihp", mixing, value_blocks, preferred_element_type=jnp.float32
    )
    to_end = jnp.exp(running_pos[:, :, -1:, :] - running_pos)
    weighted = (key_blocks * to_end[..., None]).astype(jnp.bfloat16)
    local_states = jnp.einsum(
        "scjhn,scjhp->schnp", weighted, value_blocks, preferred_element_type=jnp.float32
    )
    block_logs = running_sc[..., -1]
    return (value_blocks, query_blocks, running_pos, inner_sum, local_states, block_logs)


def entry_states(local_states, block_logs):

    def advance(carried, entry_item):
        update, log_total = entry_item
        return (jnp.exp(log_total)[..., None, None] * carried + update, carried)

    start_state = jnp.zeros(local_states.shape[:1] + local_states.shape[2:], jnp.float32)
    final_state, entries = lax.scan(
        advance, start_state, (jnp.moveaxis(local_states, 1, 0), jnp.moveaxis(block_logs, 1, 0))
    )
    return (final_state, jnp.moveaxis(entries, 0, 1))


def carry_into(final_state, device_log):
    log_totals = lax.all_gather(device_log[None], "seq", axis=0, tiled=True)
    my_index = lax.axis_index("seq")
    ranks_all = lax.iota(jnp.int32, log_totals.shape[0])
    between = jnp.logical_and(
        ranks_all[None, :] > ranks_all[:, None], ranks_all[None, :] < my_index
    ).astype(jnp.float32)
    span_logs = jnp.einsum("dk,ksh->dsh", between, log_totals, precision=lax.Precision.HIGHEST)
    weights = jnp.where((ranks_all < my_index)[:, None, None], jnp.exp(span_logs), 0.0)
    return jnp.sum(
        weights[..., None, None] * lax.all_gather(final_state[None], "seq", axis=0, tiled=True),
        axis=0,
    )


def selective_scan(values, keys_in, queries, log_decay, skip, gain):
    block_len = min(BLOCK, values.shape[1])
    value_blocks, query_blocks, running_pos, inner_sum, local_states, block_logs = block_terms(
        values, keys_in, queries, log_decay, block_len
    )
    final_state, entries = entry_states(local_states, block_logs)
    carried = carry_into(final_state, jnp.sum(block_logs, axis=1))
    before = cumulated(block_logs, 1) - block_logs
    states = (entries + jnp.exp(before)[..., None, None] * carried[:, None]).astype(jnp.bfloat16)
    outer_sum = jnp.einsum(
        "scihn,schnp->scihp", query_blocks, states, preferred_element_type=jnp.float32
    )
    raw_out = (
        inner_sum
        + outer_sum * jnp.exp(running_pos)[..., None]
        + skip[:, None] * value_blocks.astype(jnp.float32)
    )
    scaled = raw_out * lax.rsqrt(jnp.mean(raw_out * raw_out, axis=-1, keepdims=True) + 1e-05)
    normed = (scaled * gain.reshape(skip.shape[0], -1)).astype(jnp.bfloat16)
    return normed.reshape(normed.shape[0], -1, normed.shape[3] * normed.shape[4])


def project_rows(features, w_values, w_keys, w_step):
    slab_count, length, feat_width = features.shape
    head_count = w_values.shape[0]
    split_feat = features.reshape(slab_count, length, head_count, feat_width // head_count)
    values_two = jnp.einsum(
        "slhp,hpk->slhk", split_feat, w_values, preferred_element_type=jnp.float32
    ).astype(jnp.bfloat16)
    keys_two = jnp.einsum(
        "slhp,hpk->slhk", split_feat, w_keys, preferred_element_type=jnp.float32
    ).astype(jnp.bfloat16)
    step_pre = jnp.einsum(
        "slhp,hp->slh", split_feat, w_step, preferred_element_type=jnp.float32
    ).astype(jnp.bfloat16)
    return (values_two, keys_two, step_pre)


def second_scan(values_two, keys_two, step_pre, step_bias, rates_second, skip_second, gain_second):
    slab_count, length, head_count, key_width = keys_two.shape
    step_size = jax.nn.softplus(step_pre.astype(jnp.float32) + step_bias)
    log_decay = -rates_second[None, :, None] * jnp.transpose(step_size, (0, 2, 1))
    return selective_scan(
        values_two.reshape(slab_count, length, -1),
        keys_two[..., :N].reshape(slab_count, length, -1),
        keys_two[..., N:].reshape(slab_count, length, -1),
        log_decay,
        skip_second,
        gain_second,
    )


def columns_from(received):
    slab_count, rows_all, cols_here, last_width = received.shape
    return jnp.transpose(received, (0, 2, 1, 3)).reshape(
        slab_count, cols_here * rows_all, last_width
    )


def local(
    values_first,
    keys_first,
    queries_first,
    steps_first,
    rates_first,
    skip_first,
    gain_first,
    w_values,
    w_keys,
    w_step,
    step_bias,
    rates_second,
    skip_second,
    gain_second,
):
    log_first = -rates_first[None, :, None] * steps_first
    first_out = selective_scan(
        values_first, keys_first, queries_first, log_first, skip_first, gain_first
    )
    slab_count, length, feat_width = first_out.shape
    home_grid = first_out.reshape(slab_count, ROWS_DEV, length // ROWS_DEV, feat_width)
    received = lax.all_to_all(home_grid, "seq", split_axis=2, concat_axis=1, tiled=True)
    rows_all = received.shape[1]
    cols_here = received.shape[2]
    values_two, keys_two, step_pre = project_rows(columns_from(received), w_values, w_keys, w_step)
    result = second_scan(
        values_two, keys_two, step_pre, step_bias, rates_second, skip_second, gain_second
    )
    column_out = result.reshape(received.shape[0], cols_here, rows_all, result.shape[2])
    home_back = lax.all_to_all(column_out, "seq", split_axis=2, concat_axis=1, tiled=True)
    second_home = jnp.transpose(home_back, (0, 2, 1, 3)).reshape(slab_count, length, feat_width)
    return (first_out.astype(jnp.float32) + second_home.astype(jnp.float32)).astype(jnp.bfloat16)


def cumsum_rows(rows, upper):
    high = rows.astype(jnp.bfloat16).astype(jnp.float32)
    rest = rows - high
    mid = rest.astype(jnp.bfloat16).astype(jnp.float32)
    low = rest - mid
    count = rows.shape[0]
    stacked = jnp.concatenate([high, mid, low, jnp.zeros_like(low)], axis=0).astype(jnp.bfloat16)
    sums = jnp.dot(stacked, upper, preferred_element_type=jnp.float32)
    return sums[:count] + sums[count : 2 * count] + sums[2 * count : 3 * count]


def dot_nt(left, right):
    return lax.dot_general(
        left, right, (((1,), (1,)), ((), ())), preferred_element_type=jnp.float32
    )


def dot_tn(left, right):
    return lax.dot_general(
        left, right, (((0,), (0,)), ((), ())), preferred_element_type=jnp.float32
    )


def column_of(run_row, width):
    return jnp.transpose(jnp.broadcast_to(run_row, (width, run_row.shape[1])))


def inner_part(values, keys_in, queries, run_row, run_col, skip):
    length, width = values.shape
    half = length // 2
    lower = lax.broadcasted_iota(jnp.int32, (half, half), 0) >= lax.broadcasted_iota(
        jnp.int32, (half, half), 1
    )
    reps = half // width

    def decay(rows, columns, masked):
        left = jnp.concatenate([run_col[rows]] * reps, axis=1) if reps > 1 else run_col[rows]
        spread = left - run_row[:, columns]
        return jnp.exp(jnp.where(lower, spread, -jnp.inf) if masked else spread)

    top, bottom = slice(0, half), slice(half, length)
    scores_top = dot_nt(queries[top], keys_in[top])
    scores_bottom = dot_nt(queries[bottom], keys_in)
    mix_top = (scores_top * decay(top, top, True)).astype(jnp.bfloat16)
    mix_bottom = jnp.concatenate(
        [
            (scores_bottom[:, top] * decay(bottom, top, False)).astype(jnp.bfloat16),
            (scores_bottom[:, bottom] * decay(bottom, bottom, True)).astype(jnp.bfloat16),
        ],
        axis=1,
    )
    inner = jnp.concatenate(
        [
            jnp.dot(mix_top, values[top], preferred_element_type=jnp.float32),
            jnp.dot(mix_bottom, values, preferred_element_type=jnp.float32),
        ],
        axis=0,
    )
    return inner + skip * values.astype(jnp.float32)


def state_part(values, keys_in, run_col):
    last = run_col[run_col.shape[0] - 1 :, :]
    weighted = (keys_in.astype(jnp.float32) * jnp.exp(last - run_col)).astype(jnp.bfloat16)
    return dot_tn(weighted, values)


def outer_part(queries, run_col, state):
    outer = jnp.dot(queries, state.astype(jnp.bfloat16), preferred_element_type=jnp.float32)
    return jnp.exp(run_col) * outer


def advanced(state, run_col, update):
    return jnp.exp(run_col[run_col.shape[0] - 1 :, :]) * state + update


def norm_factor(raw):
    return lax.rsqrt(jnp.mean(raw * raw, axis=1, keepdims=True) + 1e-05)


def decay_outer(queries, run_col, state):
    outer = jnp.dot(queries, state, preferred_element_type=jnp.float32)
    return jnp.exp(run_col) * outer


def inner_any_order(values, keys_in, queries, run_row, run_col, bias, skip):
    length, width = values.shape
    left = jnp.concatenate([run_col] * (length // width), axis=1)
    scores = dot_nt(queries, keys_in)
    mixing = (scores * jnp.exp(left - run_row + bias)).astype(jnp.bfloat16)
    inner = jnp.dot(mixing, values, preferred_element_type=jnp.float32)
    return inner + skip * values.astype(jnp.float32)


def fused_kernel(parts, heads, side, *refs):
    values, keys_in, queries, steps, w_values, w_keys = refs[:6]
    small_in, out = refs[6:14], refs[14]
    v_buf, k_buf, q_buf, step_buf, wv_buf, wk_buf = refs[15:21]
    small = refs[21:29]
    w_step, gain_first, gain_second = small[:3]
    rates_first, skip_first, step_bias, rates_second, skip_second = small[3:]
    row_buf, col_buf, update_buf, raw_buf, stage_state, stage_raw = refs[29:35]
    state_in, back_in, far_in, rows_in, raw_in, maps_in = refs[35:41]
    first_buf, column_buf, second_buf, home_buf, bias_buf, upper_buf, run_state = refs[41:48]
    own_sem, unit_sem, state_send, rows_send, raw_send, maps_send = refs[48:54]
    state_recv, back_recv, far_recv, rows_recv, raw_recv, maps_recv = refs[54:60]
    first_send, first_recv, second_send, second_recv, ready = refs[60:]
    me = lax.axis_index("seq")
    length, width = raw_buf.shape[1:]
    slabs = parts // heads
    last_part = parts - 1
    rows_here, cols_here = side // parts, length // side
    chunk = rows_here * cols_here
    groups = parts // GROUP
    my_head = lax.rem(me, heads)
    mesh_id = pl.DeviceIdType.MESH
    even = lax.rem(lax.axis_index("head"), 2) == 0

    def chosen(modes):
        if modes[0] == modes[1]:
            return me >= 0 if modes[0] else me < 0
        return even if modes[0] else jnp.logical_not(even)

    maps_two, maps_three = chosen(MAPS_TWO), chosen(MAPS_THREE)
    chain = chosen(CHAIN)
    far_needed = jnp.logical_not(maps_three | chain)
    across_two, across_three = chosen(ACROSS_TWO), chosen(ACROSS_THREE)
    whole_two, whole_three = jnp.logical_not(across_two), jnp.logical_not(across_three)
    states_two, states_three = jnp.logical_not(maps_two), jnp.logical_not(maps_three)
    left = me < 2
    started = []

    def send(condition, copy):
        @pl.when(condition)
        def _():
            copy.start()

        started.append((condition, copy))


    def lanes(head):
        return slice(head * width, (head + 1) * width)

    def of_unit(array, unit):
        return array[unit // heads, :, lanes(unit % heads)]

    barrier = pltpu.get_barrier_semaphore()

    def greet(sources, target):
        @pl.when(sources)
        def _():
            pl.semaphore_signal(
                barrier, inc=1, device_id={"seq": target}, device_id_type=mesh_id
            )

    for target in range(1, parts):
        greet(me != target, target)
    greet(me == 1, 0)

    step_copy = pltpu.make_async_copy(steps, step_buf, own_sem.at[0])
    step_copy.start()
    small_copies = [
        pltpu.make_async_copy(src, dst, own_sem.at[3 + index])
        for index, (src, dst) in enumerate(zip(small_in, small))
    ]
    unit_copies = [
        [
            pltpu.make_async_copy(src.at[slab], dst.at[slab], unit_sem.at[kind, slab])
            for slab in range(slabs)
        ]
        for kind, (src, dst) in enumerate(((keys_in, k_buf), (values, v_buf), (queries, q_buf)))
    ]
    weight_copies = [
        pltpu.make_async_copy(w_values.at[my_head], wv_buf, own_sem.at[1]),
        pltpu.make_async_copy(w_keys.at[my_head], wk_buf, own_sem.at[2]),
    ]
    early = [*unit_copies[0], *unit_copies[1]]
    late = [*unit_copies[2], *small_copies[:3], *small_copies[4:], *weight_copies]
    small_copies[3].start()
    for copy in early + late:
        copy.start()

    square = (length, length)
    upper = jnp.where(
        lax.broadcasted_iota(jnp.int32, square, 0) <= lax.broadcasted_iota(jnp.int32, square, 1),
        1.0,
        0.0,
    ).astype(jnp.bfloat16)

    def remote(src, dst, send_sem, recv_sem, target):
        return pltpu.make_async_remote_copy(
            src_ref=src,
            dst_ref=dst,
            send_sem=send_sem,
            recv_sem=recv_sem,
            device_id={"seq": target},
            device_id_type=mesh_id,
        )

    def state_copy(unit, target):
        return remote(
            stage_state.at[unit],
            state_in.at[unit],
            state_send.at[target, unit],
            state_recv.at[unit],
            target,
        )

    def back_copy():
        return remote(stage_state.at[0], back_in, state_send.at[0, 0], back_recv, 0)

    def far_copy(unit, target):
        return remote(
            stage_state.at[unit],
            far_in.at[unit],
            state_send.at[target, unit],
            far_recv.at[unit],
            target,
        )

    def rows_copy(source, target):
        return remote(
            row_buf, rows_in.at[source], rows_send.at[target], rows_recv.at[source], target
        )

    def raw_copy(source, target):
        return remote(
            stage_raw.at[target],
            raw_in.at[source],
            raw_send.at[target],
            raw_recv.at[source],
            target,
        )

    def maps_copy(source, target):
        return remote(
            queries.at[target // heads, :, lanes(target % heads)],
            maps_in.at[source],
            maps_send.at[target],
            maps_recv.at[source],
            target,
        )

    def first_copy(unit, group, source):
        return remote(
            first_buf.at[unit, pl.ds(group * GROUP, GROUP)],
            column_buf.at[pl.ds(group * GROUP, GROUP), source],
            first_send.at[unit, group],
            first_recv.at[source, group],
            unit,
        )

    def second_copy(group, target, source):
        return remote(
            second_buf.at[target, pl.ds(group * GROUP, GROUP)],
            home_buf.at[source, pl.ds(group * GROUP, GROUP)],
            second_send.at[target, group],
            second_recv.at[source, group],
            target,
        )

    step_copy.wait()
    small_copies[3].wait()
    logs = [
        -rates_first[head] * step_buf[slab, head : head + 1, :]
        for slab in range(slabs)
        for head in range(heads)
    ]
    logs = jnp.concatenate(logs + logs[:1] * (-parts % 8), axis=0)
    running = cumsum_rows(logs, upper)
    row_buf[...] = running
    columns_of = [column_of(running[unit : unit + 1], width) for unit in range(parts)]
    for copy in early:
        copy.wait()
    @pl.when(me > 1)
    def _():
        pl.semaphore_wait(barrier, last_part)

    @pl.when(me == last_part)
    def _():
        pl.semaphore_signal(ready, inc=1, device_id={"seq": 0}, device_id_type=mesh_id)

    for target in (0, 1):
        send((me == 2) & maps_two, maps_copy(2, target))
        send((me == 3) & maps_three, maps_copy(3, target))
    send((me == 3) & across_three, maps_copy(3, 2))
    updates = [
        state_part(of_unit(v_buf, unit), of_unit(k_buf, unit), columns_of[unit])
        for unit in range(parts)
    ]
    for unit in range(parts):
        stage_state[unit] = updates[unit].astype(jnp.bfloat16)

    rows_right = far_needed | across_two | whole_three
    send((me == 2) & rows_right, rows_copy(2, 3))
    for unit in (0, 1):
        send((me == 2) & far_needed, far_copy(unit, 3))
    send((me == 2) & across_two, far_copy(3, 3))
    send((me == 2) & whole_three, far_copy(2, 3))
    for target in (0, 1):
        send((me == 2) & (maps_two | maps_three), rows_copy(2, target))
        send((me == 3) & maps_three, rows_copy(3, target))
        send((me == 2) & maps_three, far_copy(target, target))
    send((me == 3) & across_three, rows_copy(3, 2))

    @pl.when(me == 0)
    def _():
        pl.semaphore_wait(barrier, 1)

    for unit in range(parts):
        send(me == 0, state_copy(unit, 1))

    @pl.when(me == 0)
    def _():
        state_in[...] = jnp.zeros_like(state_in)

    for unit in range(parts):
        col_buf[unit] = columns_of[unit]
        update_buf[unit] = updates[unit]
    for copy in late:
        copy.wait()
    raws = [
        inner_part(
            of_unit(v_buf, unit),
            of_unit(k_buf, unit),
            of_unit(q_buf, unit),
            running[unit : unit + 1],
            columns_of[unit],
            skip_first[unit % heads],
        )
        for unit in range(parts)
    ]
    for unit in range(parts):
        raw_buf[unit] = raws[unit]
        stage_raw[unit] = raws[unit].astype(jnp.bfloat16)

    for target in (0, 1):
        send((me == 2) & maps_two, raw_copy(2, target))
        send((me == 3) & maps_three, raw_copy(3, target))
    send((me == 2) & across_two, maps_copy(2, 3))
    send((me == 2) & across_two, raw_copy(2, 3))
    send((me == 3) & across_three, raw_copy(3, 2))

    def rank_of(index):
        owner, inside = lax.div(index, chunk), lax.rem(index, chunk)
        row, col = lax.div(inside, cols_here), lax.rem(inside, cols_here)
        return col * side + owner * rows_here + row

    rank_sub = rank_of(lax.broadcasted_iota(jnp.int32, (length, width), 0))
    rank_sub = jnp.concatenate([rank_sub] * (length // width), axis=1)
    rank_lane = rank_of(lax.broadcasted_iota(jnp.int32, (8, length), 1))[0:1]
    bias_buf[...] = jnp.where(rank_lane <= rank_sub, 0.0, -jnp.inf)
    upper_buf[...] = jnp.where(rank_sub <= rank_lane, 1.0, 0.0).astype(jnp.bfloat16)

    def ordered(normed):
        return [
            jnp.concatenate(
                [
                    normed[row * side + block * cols_here : row * side + (block + 1) * cols_here]
                    for row in range(rows_here)
                ],
                axis=0,
            ).astype(jnp.bfloat16)
            for block in range(parts)
        ]

    def finish(unit):
        raw = raw_buf[unit] + decay_outer(of_unit(q_buf, unit), col_buf[unit], state_in[unit])
        normed = raw * norm_factor(raw) * gain_first[:, lanes(unit % heads)]
        for block, piece in enumerate(ordered(normed)):
            first_buf[unit, block] = piece

        @pl.when(me == unit)
        def _():
            for block in range(parts):
                column_buf[block, unit] = first_buf[unit, block]

    def send_first(condition, *units):
        for group in range(groups):
            for unit in units:
                send(condition, first_copy(unit, group, me))

    @pl.when(me == 1)
    def _():
        pl.semaphore_wait(barrier, last_part)

    for unit in ORDER:
        @pl.when(me == 1)
        def _():
            state_copy(unit, 1).wait_recv()
            last = jnp.exp(col_buf[unit, length - 1 :, :])
            carried = last * state_in[unit].astype(jnp.float32) + update_buf[unit]
            stage_state[unit] = carried.astype(jnp.bfloat16)

        if unit > 1:
            send((me == 1) & (across_two if unit == 3 else whole_three), state_copy(unit, 3))
            send((me == 1) & (whole_two if unit == 3 else me == 1), state_copy(unit, 2))
        else:
            send((me == 1) & far_needed, state_copy(unit, 3))
            send((me == 1) & (states_two | chain), state_copy(unit, 2))
            if unit == 0:
                send((me == 1) & (maps_two | maps_three), back_copy())

    for units in FINISH:
        @pl.when(left)
        def _():
            for unit in units:
                finish(unit)

        if units == (1,):
            send_first(me == 0, *units)
        else:
            send_first(me == 1, *[unit for unit in units if unit != 1])

    def state_three(base, unit):
        row = rows_in[2, pl.ds(unit, 1), :]
        last = jnp.exp(jnp.broadcast_to(row[:, length - 1 :], (1, width)))
        carried = last * base.astype(jnp.float32) + far_in[unit].astype(jnp.float32)
        return carried.astype(jnp.bfloat16)

    @pl.when(((me == 3) & rows_right) | (left & (maps_two | maps_three)))
    def _():
        rows_copy(2, me).wait_recv()

    def advance(unit):
        state_copy(unit, 2).wait_recv()
        last = jnp.exp(col_buf[unit, length - 1 :, :])
        carried = last * state_in[unit].astype(jnp.float32) + update_buf[unit]
        stage_state[unit] = carried.astype(jnp.bfloat16)

    for unit in (0, 1):
        @pl.when((me == 2) & (states_two | chain))
        def _():
            advance(unit)

        send((me == 2) & chain, state_copy(unit, 3))

        @pl.when((me == 2) & states_two)
        def _():
            finish(unit)

        @pl.when((me == 3) & states_three)
        def _():
            state_copy(unit, 3).wait_recv()

            @pl.when(far_needed)
            def _():
                far_copy(unit, 3).wait_recv()
                state_in[unit] = state_three(state_in[unit], unit)

            finish(unit)

        send_first(((me == 2) & states_two) | ((me == 3) & states_three), unit)

    def pick(head, select):
        chosen_one = select(0)
        for index in range(1, heads):
            chosen_one = jnp.where(head == index, select(index), chosen_one)
        return chosen_one

    gain_one = pick(my_head, lambda h: gain_first[:, lanes(h)])

    def absorb(source, state):
        maps_copy(source, 0).wait_recv()
        raw_copy(source, me).wait_recv()
        run_col = column_of(rows_in[source, pl.ds(me, 1), :], width)
        raw = raw_in[source].astype(jnp.float32) + decay_outer(maps_in[source], run_col, state)
        normed = raw * norm_factor(raw) * gain_one
        for block, piece in enumerate(ordered(normed)):
            column_buf[block, source] = piece

    @pl.when((me == 2) & whole_two)
    def _():
        advance(3)

    send((me == 2) & whole_two, state_copy(3, 3))

    @pl.when((me == 2) & whole_two)
    def _():
        finish(3)

    send_first((me == 2) & whole_two, 3)

    @pl.when((me == 3) & whole_three)
    def _():
        state_copy(2, 3).wait_recv()
        far_copy(2, 3).wait_recv()
        state_in[2] = state_three(state_in[2], 2)
        finish(2)

    send_first((me == 3) & whole_three, 2)

    @pl.when(me == 2)
    def _():
        state_copy(2, 2).wait_recv()
        finish(2)

    @pl.when((me == 2) & across_three)
    def _():
        rows_copy(3, 2).wait_recv()
        last = jnp.exp(col_buf[2, length - 1 :, :])
        carried = last * state_in[2].astype(jnp.float32) + update_buf[2]
        absorb(3, carried.astype(jnp.bfloat16))

    @pl.when(me == 3)
    def _():
        state_copy(3, 3).wait_recv()

        @pl.when(across_two)
        def _():
            absorb(2, state_in[3])

            far_copy(3, 3).wait_recv()
            state_in[3] = state_three(state_in[3], 3)

        finish(3)

    @pl.when(me == 0)
    def _():
        pl.semaphore_wait(ready, 1)

    send_first(me == 0, 2, 3)

    for owner in (0, 1):
        if owner == 0:
            @pl.when((me == 0) & (maps_two | maps_three))
            def _():
                back_copy().wait_recv()

        base = back_in if owner == 0 else stage_state.at[1]

        @pl.when((me == owner) & maps_two)
        def _():
            absorb(2, base[...])

        @pl.when((me == owner) & maps_three)
        def _():
            far_copy(owner, owner).wait_recv()
            rows_copy(3, owner).wait_recv()
            absorb(3, state_three(base[...], owner))

    def whole(source):
        if source < 2:
            return me != source
        own = (me == 3) & across_two if source == 2 else (me == 2) & across_three
        absorbed = left & (maps_two if source == 2 else maps_three)
        return jnp.logical_not(own | absorbed | (me == source))

    step_row = pick(my_head, lambda h: w_step[...].astype(jnp.float32)[h : h + 1, :])
    step_rows = jnp.broadcast_to(step_row, (16, width)).astype(jnp.bfloat16)
    gain_two = pick(my_head, lambda h: gain_second[:, lanes(h)])

    def local_terms(columns):
        values_two = jnp.dot(columns, wv_buf[...], preferred_element_type=jnp.float32).astype(
            jnp.bfloat16
        )
        keys_two = jnp.dot(columns, wk_buf[...], preferred_element_type=jnp.float32).astype(
            jnp.bfloat16
        )
        pre = dot_nt(step_rows, columns)[0:8].astype(jnp.bfloat16).astype(jnp.float32)
        shifted = pre + step_bias[my_head]
        soft = jnp.maximum(shifted, 0.0) + jnp.log1p(jnp.exp(-jnp.abs(shifted)))
        run_row = cumsum_rows(-rates_second[my_head] * soft, upper_buf[...])[0:1]
        run_col = column_of(run_row, width)
        half = keys_two.shape[1] // 2
        keys_now, queries_now = keys_two[:, :half], keys_two[:, half:]
        raw = inner_any_order(
            values_two,
            keys_now,
            queries_now,
            run_row,
            run_col,
            bias_buf[...],
            skip_second[my_head],
        )
        return raw, queries_now, run_col, state_part(values_two, keys_now, run_col)

    for group in range(groups):
        for source in range(parts):
            @pl.when(whole(source))
            def _():
                first_copy(me, group, source).wait_recv()

        blocks = range(group * GROUP, (group + 1) * GROUP)
        terms = [local_terms(column_buf[block].reshape(length, width)) for block in blocks]
        for block, (raw, queries_now, run_col, update) in zip(blocks, terms):
            if block == 0:
                state = update
            else:
                before = run_state[...] if block == blocks[0] else state
                raw = raw + outer_part(queries_now, run_col, before)
                state = advanced(before, run_col, update)
            normed = (raw * norm_factor(raw) * gain_two).astype(jnp.bfloat16)
            for target in range(parts):
                piece = normed[target * chunk : (target + 1) * chunk].astype(jnp.float32)
                piece = piece + column_buf[block, target].astype(jnp.float32)
                second_buf[target, block] = piece.astype(jnp.bfloat16)
        run_state[...] = state
        for target in range(parts):
            send(me != target, second_copy(group, target, me))

            @pl.when(me == target)
            def _():
                for block in blocks:
                    home_buf[target, block] = second_buf[target, block]

    for group in range(groups):
        for source in range(parts):
            @pl.when(me != source)
            def _():
                second_copy(group, me, source).wait_recv()

        if (group + 1) * GROUP % 2:
            continue
        for pair in range(max((group + 1) * GROUP - max(GROUP, 2), 0), (group + 1) * GROUP, 2):
            for unit in range(parts):
                total = [home_buf[unit, block].astype(jnp.float32) for block in (pair, pair + 1)]
                for row in range(rows_here):
                    place = slice(row * cols_here, (row + 1) * cols_here)
                    out[
                        unit // heads,
                        pl.ds(row * side + pair * cols_here, 2 * cols_here),
                        lanes(unit % heads),
                    ] = jnp.concatenate([part[place] for part in total], axis=0).astype(
                        jnp.bfloat16
                    )

    for condition, copy in started:
        @pl.when(condition)
        def _():
            copy.wait_send()


def local_fused(
    parts,
    values_first,
    keys_first,
    queries_first,
    steps_first,
    rates_first,
    skip_first,
    gain_first,
    w_values,
    w_keys,
    w_step,
    step_bias,
    rates_second,
    skip_second,
    gain_second,
):
    slab_count, length, feat_width = values_first.shape
    heads = rates_first.shape[0]
    width = feat_width // heads
    side = math.isqrt(parts * length)
    chunk = length // parts
    groups = parts // GROUP
    anywhere = pl.BlockSpec(memory_space=pl.ANY)
    dma = pltpu.SemaphoreType.DMA

    def vmem(dtype, *shape):
        return pltpu.VMEM(shape, dtype)

    bf16, f32 = jnp.bfloat16, jnp.float32
    return pl.pallas_call(
        functools.partial(fused_kernel, parts, heads, side),
        out_shape=jax.ShapeDtypeStruct(values_first.shape, bf16),
        in_specs=[anywhere] * 14,
        out_specs=pl.BlockSpec(memory_space=pltpu.VMEM),
        scratch_shapes=[
            vmem(bf16, *values_first.shape),
            vmem(bf16, *keys_first.shape),
            vmem(bf16, *queries_first.shape),
            vmem(f32, *steps_first.shape),
            vmem(bf16, *w_values.shape[1:]),
            vmem(bf16, *w_keys.shape[1:]),
            vmem(bf16, *w_step.shape),
            vmem(f32, 1, feat_width),
            vmem(f32, 1, feat_width),
        ]
        + [pltpu.SMEM((heads,), f32)] * 5
        + [
            vmem(f32, parts + -parts % 8, length),
            vmem(f32, parts, length, width),
            vmem(f32, parts, width, width),
            vmem(f32, parts, length, width),
            vmem(bf16, parts, width, width),
            vmem(bf16, parts, length, width),
            vmem(bf16, parts, width, width),
            vmem(bf16, width, width),
            vmem(bf16, parts, width, width),
            vmem(f32, parts, parts + -parts % 8, length),
            vmem(bf16, parts, length, width),
            vmem(bf16, parts, length, width),
            vmem(bf16, parts, parts, chunk, width),
            vmem(bf16, parts, parts, chunk, width),
            vmem(bf16, parts, parts, chunk, width),
            vmem(bf16, parts, parts, chunk, width),
            vmem(f32, length, length),
            vmem(bf16, length, length),
            vmem(f32, width, width),
            dma((11,)),
            dma((3, parts)),
            dma((parts, parts)),
            dma((parts,)),
            dma((parts,)),
            dma((parts,)),
            dma((parts,)),
            dma,
            dma((parts,)),
            dma((parts,)),
            dma((parts,)),
            dma((parts,)),
            dma((parts, groups)),
            dma((parts, groups)),
            dma((parts, groups)),
            dma((parts, groups)),
            pltpu.SemaphoreType.REGULAR,
        ],
        compiler_params=pltpu.CompilerParams(
            collective_id=0, has_side_effects=True, vmem_limit_bytes=VMEM_GRANT
        ),
    )(
        *(
            pltpu.with_memory_space_constraint(array, pltpu.HBM)
            for array in (
                values_first,
                keys_first,
                queries_first,
                steps_first,
                w_values,
                w_keys,
                w_step,
                gain_first.reshape(1, -1),
                gain_second.reshape(1, -1),
                rates_first,
                skip_first,
                step_bias,
                rates_second,
                skip_second,
            )
        )
    )


def fits_fused(parts, args):
    values, w_values, w_keys = args[0], args[7], args[8]
    slab_count, length, feat_width = values.shape
    heads = args[4].shape[0]
    side = math.isqrt(parts * length)
    return (
        slab_count * heads == parts
        and parts == len(ORDER)
        and (side // parts) * (length // side) % 16 == 0
        and length <= BLOCK
        and length % 256 == 0
        and side * side == parts * length
        and side % parts == 0
        and length % side == 0
        and (length // side) % 8 == 0
        and feat_width // heads == 128
        and w_values.shape[1:] == (128, 128)
        and w_keys.shape[1:] == (128, 256)
    )


def solution(mesh):
    parts = mesh.shape["seq"]

    def chosen(*args):
        if fits_fused(parts, args):
            return local_fused(parts, *args)
        return local(*args)

    placed = (
        P("slab", "seq", "head"),
        P("slab", "seq", "head"),
        P("slab", "seq", "head"),
        P("slab", "head", "seq"),
        P("head"),
        P("head"),
        P("head"),
        P("head", None, None),
        P("head", None, None),
        P("head", None),
        P("head"),
        P("head"),
        P("head"),
        P("head"),
    )
    return jax.shard_map(
        chosen, mesh=mesh, in_specs=placed, out_specs=P("slab", "seq", "head"), check_vma=False
    )
```

```python
import functools
import math

import jax
import jax.numpy as jnp
from jax import lax
from jax.experimental import pallas as pl
from jax.experimental.pallas import tpu as pltpu
from jax.sharding import PartitionSpec as P

N = 128
BLOCK = 256
ROWS_DEV = 8
VMEM_GRANT = 16 << 20
GROUP = 2
ORDER = (0, 1, 2, 3)
FINISH = ((2, 3), (0,), (1,))
MAPS_TWO = (True, False)
MAPS_THREE = (False, False)
ACROSS_TWO = (True, False)
ACROSS_THREE = (True, True)
CHAIN = (False, True)


def cumulated(terms, axis):
    size = terms.shape[axis]
    ranks = lax.iota(jnp.int32, size)
    upper = (ranks[:, None] <= ranks[None, :]).astype(jnp.float32)
    sums = jnp.einsum(
        "...j,ji->...i",
        jnp.moveaxis(terms, axis, -1),
        upper,
        precision=lax.Precision.HIGHEST,
    )
    return jnp.moveaxis(sums, -1, axis)


def block_terms(values, keys_in, queries, log_decay, block_len):
    slab_count, length, feat_width = values.shape
    head_count = log_decay.shape[1]
    blocks = length // block_len
    value_blocks = values.reshape(
        slab_count, blocks, block_len, head_count, feat_width // head_count
    )
    key_blocks = keys_in.reshape(
        slab_count, blocks, block_len, head_count, keys_in.shape[2] // head_count
    )
    query_blocks = queries.reshape(
        slab_count, blocks, block_len, head_count, queries.shape[2] // head_count
    )
    running = cumulated(log_decay.reshape(slab_count, head_count, blocks, block_len), 3)
    running_sc = jnp.transpose(running, (0, 2, 1, 3))
    running_pos = jnp.transpose(running, (0, 2, 3, 1))
    scores = jnp.einsum(
        "scihn,scjhn->schij", query_blocks, key_blocks, preferred_element_type=jnp.float32
    )
    row_ids = lax.broadcasted_iota(jnp.int32, (block_len, block_len), 0)
    col_ids = lax.broadcasted_iota(jnp.int32, (block_len, block_len), 1)
    spread = running_sc[..., :, None] - running_sc[..., None, :]
    decays = jnp.exp(jnp.where(row_ids >= col_ids, spread, -jnp.inf))
    mixing = (scores * decays).astype(jnp.bfloat16)
    inner_sum = jnp.einsum(
        "schij,scjhp->scihp", mixing, value_blocks, preferred_element_type=jnp.float32
    )
    to_end = jnp.exp(running_pos[:, :, -1:, :] - running_pos)
    weighted = (key_blocks * to_end[..., None]).astype(jnp.bfloat16)
    local_states = jnp.einsum(
        "scjhn,scjhp->schnp", weighted, value_blocks, preferred_element_type=jnp.float32
    )
    block_logs = running_sc[..., -1]
    return (value_blocks, query_blocks, running_pos, inner_sum, local_states, block_logs)


def entry_states(local_states, block_logs):

    def advance(carried, entry_item):
        update, log_total = entry_item
        return (jnp.exp(log_total)[..., None, None] * carried + update, carried)

    start_state = jnp.zeros(local_states.shape[:1] + local_states.shape[2:], jnp.float32)
    final_state, entries = lax.scan(
        advance, start_state, (jnp.moveaxis(local_states, 1, 0), jnp.moveaxis(block_logs, 1, 0))
    )
    return (final_state, jnp.moveaxis(entries, 0, 1))


def carry_into(final_state, device_log):
    log_totals = lax.all_gather(device_log[None], "seq", axis=0, tiled=True)
    my_index = lax.axis_index("seq")
    ranks_all = lax.iota(jnp.int32, log_totals.shape[0])
    between = jnp.logical_and(
        ranks_all[None, :] > ranks_all[:, None], ranks_all[None, :] < my_index
    ).astype(jnp.float32)
    span_logs = jnp.einsum("dk,ksh->dsh", between, log_totals, precision=lax.Precision.HIGHEST)
    weights = jnp.where((ranks_all < my_index)[:, None, None], jnp.exp(span_logs), 0.0)
    return jnp.sum(
        weights[..., None, None] * lax.all_gather(final_state[None], "seq", axis=0, tiled=True),
        axis=0,
    )


def selective_scan(values, keys_in, queries, log_decay, skip, gain):
    block_len = min(BLOCK, values.shape[1])
    value_blocks, query_blocks, running_pos, inner_sum, local_states, block_logs = block_terms(
        values, keys_in, queries, log_decay, block_len
    )
    final_state, entries = entry_states(local_states, block_logs)
    carried = carry_into(final_state, jnp.sum(block_logs, axis=1))
    before = cumulated(block_logs, 1) - block_logs
    states = (entries + jnp.exp(before)[..., None, None] * carried[:, None]).astype(jnp.bfloat16)
    outer_sum = jnp.einsum(
        "scihn,schnp->scihp", query_blocks, states, preferred_element_type=jnp.float32
    )
    raw_out = (
        inner_sum
        + outer_sum * jnp.exp(running_pos)[..., None]
        + skip[:, None] * value_blocks.astype(jnp.float32)
    )
    scaled = raw_out * lax.rsqrt(jnp.mean(raw_out * raw_out, axis=-1, keepdims=True) + 1e-05)
    normed = (scaled * gain.reshape(skip.shape[0], -1)).astype(jnp.bfloat16)
    return normed.reshape(normed.shape[0], -1, normed.shape[3] * normed.shape[4])


def project_rows(features, w_values, w_keys, w_step):
    slab_count, length, feat_width = features.shape
    head_count = w_values.shape[0]
    split_feat = features.reshape(slab_count, length, head_count, feat_width // head_count)
    values_two = jnp.einsum(
        "slhp,hpk->slhk", split_feat, w_values, preferred_element_type=jnp.float32
    ).astype(jnp.bfloat16)
    keys_two = jnp.einsum(
        "slhp,hpk->slhk", split_feat, w_keys, preferred_element_type=jnp.float32
    ).astype(jnp.bfloat16)
    step_pre = jnp.einsum(
        "slhp,hp->slh", split_feat, w_step, preferred_element_type=jnp.float32
    ).astype(jnp.bfloat16)
    return (values_two, keys_two, step_pre)


def second_scan(values_two, keys_two, step_pre, step_bias, rates_second, skip_second, gain_second):
    slab_count, length, head_count, key_width = keys_two.shape
    step_size = jax.nn.softplus(step_pre.astype(jnp.float32) + step_bias)
    log_decay = -rates_second[None, :, None] * jnp.transpose(step_size, (0, 2, 1))
    return selective_scan(
        values_two.reshape(slab_count, length, -1),
        keys_two[..., :N].reshape(slab_count, length, -1),
        keys_two[..., N:].reshape(slab_count, length, -1),
        log_decay,
        skip_second,
        gain_second,
    )


def columns_from(received):
    slab_count, rows_all, cols_here, last_width = received.shape
    return jnp.transpose(received, (0, 2, 1, 3)).reshape(
        slab_count, cols_here * rows_all, last_width
    )


def local(
    values_first,
    keys_first,
    queries_first,
    steps_first,
    rates_first,
    skip_first,
    gain_first,
    w_values,
    w_keys,
    w_step,
    step_bias,
    rates_second,
    skip_second,
    gain_second,
):
    log_first = -rates_first[None, :, None] * steps_first
    first_out = selective_scan(
        values_first, keys_first, queries_first, log_first, skip_first, gain_first
    )
    slab_count, length, feat_width = first_out.shape
    home_grid = first_out.reshape(slab_count, ROWS_DEV, length // ROWS_DEV, feat_width)
    received = lax.all_to_all(home_grid, "seq", split_axis=2, concat_axis=1, tiled=True)
    rows_all = received.shape[1]
    cols_here = received.shape[2]
    values_two, keys_two, step_pre = project_rows(columns_from(received), w_values, w_keys, w_step)
    result = second_scan(
        values_two, keys_two, step_pre, step_bias, rates_second, skip_second, gain_second
    )
    column_out = result.reshape(received.shape[0], cols_here, rows_all, result.shape[2])
    home_back = lax.all_to_all(column_out, "seq", split_axis=2, concat_axis=1, tiled=True)
    second_home = jnp.transpose(home_back, (0, 2, 1, 3)).reshape(slab_count, length, feat_width)
    return (first_out.astype(jnp.float32) + second_home.astype(jnp.float32)).astype(jnp.bfloat16)


def cumsum_rows(rows, upper):
    high = rows.astype(jnp.bfloat16).astype(jnp.float32)
    rest = rows - high
    mid = rest.astype(jnp.bfloat16).astype(jnp.float32)
    low = rest - mid
    count = rows.shape[0]
    stacked = jnp.concatenate([high, mid, low, jnp.zeros_like(low)], axis=0).astype(jnp.bfloat16)
    sums = jnp.dot(stacked, upper, preferred_element_type=jnp.float32)
    return sums[:count] + sums[count : 2 * count] + sums[2 * count : 3 * count]


def dot_nt(left, right):
    return lax.dot_general(
        left, right, (((1,), (1,)), ((), ())), preferred_element_type=jnp.float32
    )


def dot_tn(left, right):
    return lax.dot_general(
        left, right, (((0,), (0,)), ((), ())), preferred_element_type=jnp.float32
    )


def column_of(run_row, width):
    return jnp.transpose(jnp.broadcast_to(run_row, (width, run_row.shape[1])))


def inner_part(values, keys_in, queries, run_row, run_col, skip):
    length, width = values.shape
    half = length // 2
    lower = lax.broadcasted_iota(jnp.int32, (half, half), 0) >= lax.broadcasted_iota(
        jnp.int32, (half, half), 1
    )
    reps = half // width

    def decay(rows, columns, masked):
        left = jnp.concatenate([run_col[rows]] * reps, axis=1) if reps > 1 else run_col[rows]
        spread = left - run_row[:, columns]
        return jnp.exp(jnp.where(lower, spread, -jnp.inf) if masked else spread)

    top, bottom = slice(0, half), slice(half, length)
    scores_top = dot_nt(queries[top], keys_in[top])
    scores_bottom = dot_nt(queries[bottom], keys_in)
    mix_top = (scores_top * decay(top, top, True)).astype(jnp.bfloat16)
    mix_bottom = jnp.concatenate(
        [
            (scores_bottom[:, top] * decay(bottom, top, False)).astype(jnp.bfloat16),
            (scores_bottom[:, bottom] * decay(bottom, bottom, True)).astype(jnp.bfloat16),
        ],
        axis=1,
    )
    inner = jnp.concatenate(
        [
            jnp.dot(mix_top, values[top], preferred_element_type=jnp.float32),
            jnp.dot(mix_bottom, values, preferred_element_type=jnp.float32),
        ],
        axis=0,
    )
    return inner + skip * values.astype(jnp.float32)


def state_part(values, keys_in, run_col):
    last = run_col[run_col.shape[0] - 1 :, :]
    weighted = (keys_in.astype(jnp.float32) * jnp.exp(last - run_col)).astype(jnp.bfloat16)
    return dot_tn(weighted, values)


def outer_part(queries, run_col, state):
    outer = jnp.dot(queries, state.astype(jnp.bfloat16), preferred_element_type=jnp.float32)
    return jnp.exp(run_col) * outer


def advanced(state, run_col, update):
    return jnp.exp(run_col[run_col.shape[0] - 1 :, :]) * state + update


def norm_factor(raw):
    return lax.rsqrt(jnp.mean(raw * raw, axis=1, keepdims=True) + 1e-05)


def decay_outer(queries, run_col, state):
    outer = jnp.dot(queries, state, preferred_element_type=jnp.float32)
    return jnp.exp(run_col) * outer


def inner_any_order(values, keys_in, queries, run_row, run_col, bias, skip):
    length, width = values.shape
    left = jnp.concatenate([run_col] * (length // width), axis=1)
    scores = dot_nt(queries, keys_in)
    mixing = (scores * jnp.exp(left - run_row + bias)).astype(jnp.bfloat16)
    inner = jnp.dot(mixing, values, preferred_element_type=jnp.float32)
    return inner + skip * values.astype(jnp.float32)


def fused_kernel(parts, heads, side, *refs):
    values, keys_in, queries, steps, w_values, w_keys = refs[:6]
    small_in, out = refs[6:14], refs[14]
    v_buf, k_buf, q_buf, step_buf, wv_buf, wk_buf = refs[15:21]
    small = refs[21:29]
    w_step, gain_first, gain_second = small[:3]
    rates_first, skip_first, step_bias, rates_second, skip_second = small[3:]
    row_buf, col_buf, update_buf, raw_buf, stage_state, stage_raw = refs[29:35]
    state_in, back_in, far_in, rows_in, raw_in, maps_in = refs[35:41]
    first_buf, column_buf, second_buf, home_buf, bias_buf, upper_buf, run_state = refs[41:48]
    own_sem, unit_sem, state_send, rows_send, raw_send, maps_send = refs[48:54]
    state_recv, back_recv, far_recv, rows_recv, raw_recv, maps_recv = refs[54:60]
    first_send, first_recv, second_send, second_recv, ready = refs[60:]
    me = lax.axis_index("seq")
    length, width = raw_buf.shape[1:]
    slabs = parts // heads
    last_part = parts - 1
    rows_here, cols_here = side // parts, length // side
    chunk = rows_here * cols_here
    groups = parts // GROUP
    my_head = lax.rem(me, heads)
    mesh_id = pl.DeviceIdType.MESH
    even = lax.rem(lax.axis_index("head"), 2) == 0

    def chosen(modes):
        if modes[0] == modes[1]:
            return me >= 0 if modes[0] else me < 0
        return even if modes[0] else jnp.logical_not(even)

    maps_two, maps_three = chosen(MAPS_TWO), chosen(MAPS_THREE)
    chain = chosen(CHAIN)
    far_needed = jnp.logical_not(maps_three | chain)
    across_two, across_three = chosen(ACROSS_TWO), chosen(ACROSS_THREE)
    whole_two, whole_three = jnp.logical_not(across_two), jnp.logical_not(across_three)
    states_two, states_three = jnp.logical_not(maps_two), jnp.logical_not(maps_three)
    left = me < 2
    started = []

    def send(condition, copy):
        @pl.when(condition)
        def _():
            copy.start()

        started.append((condition, copy))


    def lanes(head):
        return slice(head * width, (head + 1) * width)

    def of_unit(array, unit):
        return array[unit // heads, :, lanes(unit % heads)]

    barrier = pltpu.get_barrier_semaphore()

    def greet(sources, target):
        @pl.when(sources)
        def _():
            pl.semaphore_signal(
                barrier, inc=1, device_id={"seq": target}, device_id_type=mesh_id
            )

    for target in range(1, parts):
        greet(me != target, target)
    greet(me == 1, 0)

    step_copy = pltpu.make_async_copy(steps, step_buf, own_sem.at[0])
    step_copy.start()
    small_copies = [
        pltpu.make_async_copy(src, dst, own_sem.at[3 + index])
        for index, (src, dst) in enumerate(zip(small_in, small))
    ]
    unit_copies = [
        [
            pltpu.make_async_copy(src.at[slab], dst.at[slab], unit_sem.at[kind, slab])
            for slab in range(slabs)
        ]
        for kind, (src, dst) in enumerate(((keys_in, k_buf), (values, v_buf), (queries, q_buf)))
    ]
    weight_copies = [
        pltpu.make_async_copy(w_values.at[my_head], wv_buf, own_sem.at[1]),
        pltpu.make_async_copy(w_keys.at[my_head], wk_buf, own_sem.at[2]),
    ]
    early = [*unit_copies[0], *unit_copies[1]]
    late = [*unit_copies[2], *small_copies[:3], *small_copies[4:], *weight_copies]
    small_copies[3].start()
    for copy in early + late:
        copy.start()

    square = (length, length)
    upper = jnp.where(
        lax.broadcasted_iota(jnp.int32, square, 0) <= lax.broadcasted_iota(jnp.int32, square, 1),
        1.0,
        0.0,
    ).astype(jnp.bfloat16)

    def remote(src, dst, send_sem, recv_sem, target):
        return pltpu.make_async_remote_copy(
            src_ref=src,
            dst_ref=dst,
            send_sem=send_sem,
            recv_sem=recv_sem,
            device_id={"seq": target},
            device_id_type=mesh_id,
        )

    def state_copy(unit, target):
        return remote(
            stage_state.at[unit],
            state_in.at[unit],
            state_send.at[target, unit],
            state_recv.at[unit],
            target,
        )

    def back_copy():
        return remote(stage_state.at[0], back_in, state_send.at[0, 0], back_recv, 0)

    def far_copy(unit, target):
        return remote(
            stage_state.at[unit],
            far_in.at[unit],
            state_send.at[target, unit],
            far_recv.at[unit],
            target,
        )

    def rows_copy(source, target):
        return remote(
            row_buf, rows_in.at[source], rows_send.at[target], rows_recv.at[source], target
        )

    def raw_copy(source, target):
        return remote(
            stage_raw.at[target],
            raw_in.at[source],
            raw_send.at[target],
            raw_recv.at[source],
            target,
        )

    def maps_copy(source, target):
        return remote(
            queries.at[target // heads, :, lanes(target % heads)],
            maps_in.at[source],
            maps_send.at[target],
            maps_recv.at[source],
            target,
        )

    def first_copy(unit, group, source):
        return remote(
            first_buf.at[unit, pl.ds(group * GROUP, GROUP)],
            column_buf.at[pl.ds(group * GROUP, GROUP), source],
            first_send.at[unit, group],
            first_recv.at[source, group],
            unit,
        )

    def second_copy(group, target, source):
        return remote(
            second_buf.at[target, pl.ds(group * GROUP, GROUP)],
            home_buf.at[source, pl.ds(group * GROUP, GROUP)],
            second_send.at[target, group],
            second_recv.at[source, group],
            target,
        )

    step_copy.wait()
    small_copies[3].wait()
    logs = [
        -rates_first[head] * step_buf[slab, head : head + 1, :]
        for slab in range(slabs)
        for head in range(heads)
    ]
    logs = jnp.concatenate(logs + logs[:1] * (-parts % 8), axis=0)
    running = cumsum_rows(logs, upper)
    row_buf[...] = running
    columns_of = [column_of(running[unit : unit + 1], width) for unit in range(parts)]
    for copy in early:
        copy.wait()
    @pl.when(me > 1)
    def _():
        pl.semaphore_wait(barrier, last_part)

    @pl.when(me == last_part)
    def _():
        pl.semaphore_signal(ready, inc=1, device_id={"seq": 0}, device_id_type=mesh_id)

    for target in (0, 1):
        send((me == 2) & maps_two, maps_copy(2, target))
        send((me == 3) & maps_three, maps_copy(3, target))
    send((me == 3) & across_three, maps_copy(3, 2))
    updates = [
        state_part(of_unit(v_buf, unit), of_unit(k_buf, unit), columns_of[unit])
        for unit in range(parts)
    ]
    for unit in range(parts):
        stage_state[unit] = updates[unit].astype(jnp.bfloat16)

    rows_right = far_needed | across_two | whole_three
    send((me == 2) & rows_right, rows_copy(2, 3))
    for unit in (0, 1):
        send((me == 2) & far_needed, far_copy(unit, 3))
    send((me == 2) & across_two, far_copy(3, 3))
    send((me == 2) & whole_three, far_copy(2, 3))
    for target in (0, 1):
        send((me == 2) & (maps_two | maps_three), rows_copy(2, target))
        send((me == 3) & maps_three, rows_copy(3, target))
        send((me == 2) & maps_three, far_copy(target, target))
    send((me == 3) & across_three, rows_copy(3, 2))

    @pl.when(me == 0)
    def _():
        pl.semaphore_wait(barrier, 1)

    for unit in range(parts):
        send(me == 0, state_copy(unit, 1))

    @pl.when(me == 0)
    def _():
        state_in[...] = jnp.zeros_like(state_in)

    for unit in range(parts):
        col_buf[unit] = columns_of[unit]
        update_buf[unit] = updates[unit]
    for copy in late:
        copy.wait()
    raws = [
        inner_part(
            of_unit(v_buf, unit),
            of_unit(k_buf, unit),
            of_unit(q_buf, unit),
            running[unit : unit + 1],
            columns_of[unit],
            skip_first[unit % heads],
        )
        for unit in range(parts)
    ]
    for unit in range(parts):
        raw_buf[unit] = raws[unit]
        stage_raw[unit] = raws[unit].astype(jnp.bfloat16)

    for target in (0, 1):
        send((me == 2) & maps_two, raw_copy(2, target))
        send((me == 3) & maps_three, raw_copy(3, target))
    send((me == 2) & across_two, maps_copy(2, 3))
    send((me == 2) & across_two, raw_copy(2, 3))
    send((me == 3) & across_three, raw_copy(3, 2))

    def rank_of(index):
        owner, inside = lax.div(index, chunk), lax.rem(index, chunk)
        row, col = lax.div(inside, cols_here), lax.rem(inside, cols_here)
        return col * side + owner * rows_here + row

    rank_sub = rank_of(lax.broadcasted_iota(jnp.int32, (length, width), 0))
    rank_sub = jnp.concatenate([rank_sub] * (length // width), axis=1)
    rank_lane = rank_of(lax.broadcasted_iota(jnp.int32, (8, length), 1))[0:1]
    bias_buf[...] = jnp.where(rank_lane <= rank_sub, 0.0, -jnp.inf)
    upper_buf[...] = jnp.where(rank_sub <= rank_lane, 1.0, 0.0).astype(jnp.bfloat16)

    def ordered(normed):
        return [
            jnp.concatenate(
                [
                    normed[row * side + block * cols_here : row * side + (block + 1) * cols_here]
                    for row in range(rows_here)
                ],
                axis=0,
            ).astype(jnp.bfloat16)
            for block in range(parts)
        ]

    def finish(unit):
        raw = raw_buf[unit] + decay_outer(of_unit(q_buf, unit), col_buf[unit], state_in[unit])
        normed = raw * norm_factor(raw) * gain_first[:, lanes(unit % heads)]
        for block, piece in enumerate(ordered(normed)):
            first_buf[unit, block] = piece

        @pl.when(me == unit)
        def _():
            for block in range(parts):
                column_buf[block, unit] = first_buf[unit, block]

    def send_first(condition, *units):
        for group in range(groups):
            for unit in units:
                send(condition, first_copy(unit, group, me))

    @pl.when(me == 1)
    def _():
        pl.semaphore_wait(barrier, last_part)

    for unit in ORDER:
        @pl.when(me == 1)
        def _():
            state_copy(unit, 1).wait_recv()
            last = jnp.exp(col_buf[unit, length - 1 :, :])
            carried = last * state_in[unit].astype(jnp.float32) + update_buf[unit]
            stage_state[unit] = carried.astype(jnp.bfloat16)

        if unit > 1:
            send((me == 1) & (across_two if unit == 3 else whole_three), state_copy(unit, 3))
            send((me == 1) & (whole_two if unit == 3 else me == 1), state_copy(unit, 2))
        else:
            send((me == 1) & far_needed, state_copy(unit, 3))
            send((me == 1) & (states_two | chain), state_copy(unit, 2))
            if unit == 0:
                send((me == 1) & (maps_two | maps_three), back_copy())

    for units in FINISH:
        @pl.when(left)
        def _():
            for unit in units:
                finish(unit)

        if units == (1,):
            send_first(me == 0, *units)
        else:
            send_first(me == 1, *[unit for unit in units if unit != 1])

    def state_three(base, unit):
        row = rows_in[2, pl.ds(unit, 1), :]
        last = jnp.exp(jnp.broadcast_to(row[:, length - 1 :], (1, width)))
        carried = last * base.astype(jnp.float32) + far_in[unit].astype(jnp.float32)
        return carried.astype(jnp.bfloat16)

    @pl.when(((me == 3) & rows_right) | (left & (maps_two | maps_three)))
    def _():
        rows_copy(2, me).wait_recv()

    def advance(unit):
        state_copy(unit, 2).wait_recv()
        last = jnp.exp(col_buf[unit, length - 1 :, :])
        carried = last * state_in[unit].astype(jnp.float32) + update_buf[unit]
        stage_state[unit] = carried.astype(jnp.bfloat16)

    for unit in (0, 1):
        @pl.when((me == 2) & (states_two | chain))
        def _():
            advance(unit)

        send((me == 2) & chain, state_copy(unit, 3))

        @pl.when((me == 2) & states_two)
        def _():
            finish(unit)

        @pl.when((me == 3) & states_three)
        def _():
            state_copy(unit, 3).wait_recv()

            @pl.when(far_needed)
            def _():
                far_copy(unit, 3).wait_recv()
                state_in[unit] = state_three(state_in[unit], unit)

            finish(unit)

        send_first(((me == 2) & states_two) | ((me == 3) & states_three), unit)

    def pick(head, select):
        chosen_one = select(0)
        for index in range(1, heads):
            chosen_one = jnp.where(head == index, select(index), chosen_one)
        return chosen_one

    gain_one = pick(my_head, lambda h: gain_first[:, lanes(h)])

    def absorb(source, state):
        maps_copy(source, 0).wait_recv()
        raw_copy(source, me).wait_recv()
        run_col = column_of(rows_in[source, pl.ds(me, 1), :], width)
        raw = raw_in[source].astype(jnp.float32) + decay_outer(maps_in[source], run_col, state)
        normed = raw * norm_factor(raw) * gain_one
        for block, piece in enumerate(ordered(normed)):
            column_buf[block, source] = piece

    @pl.when((me == 2) & whole_two)
    def _():
        advance(3)

    send((me == 2) & whole_two, state_copy(3, 3))

    @pl.when((me == 2) & whole_two)
    def _():
        finish(3)

    send_first((me == 2) & whole_two, 3)

    @pl.when((me == 3) & whole_three)
    def _():
        state_copy(2, 3).wait_recv()
        far_copy(2, 3).wait_recv()
        state_in[2] = state_three(state_in[2], 2)
        finish(2)

    send_first((me == 3) & whole_three, 2)

    @pl.when(me == 2)
    def _():
        state_copy(2, 2).wait_recv()
        finish(2)

    @pl.when((me == 2) & across_three)
    def _():
        rows_copy(3, 2).wait_recv()
        last = jnp.exp(col_buf[2, length - 1 :, :])
        carried = last * state_in[2].astype(jnp.float32) + update_buf[2]
        absorb(3, carried.astype(jnp.bfloat16))

    @pl.when(me == 3)
    def _():
        state_copy(3, 3).wait_recv()

        @pl.when(across_two)
        def _():
            absorb(2, state_in[3])

            far_copy(3, 3).wait_recv()
            state_in[3] = state_three(state_in[3], 3)

        finish(3)

    @pl.when(me == 0)
    def _():
        pl.semaphore_wait(ready, 1)

    send_first(me == 0, 2, 3)

    for owner in (0, 1):
        if owner == 0:
            @pl.when((me == 0) & (maps_two | maps_three))
            def _():
                back_copy().wait_recv()

        base = back_in if owner == 0 else stage_state.at[1]

        @pl.when((me == owner) & maps_two)
        def _():
            absorb(2, base[...])

        @pl.when((me == owner) & maps_three)
        def _():
            far_copy(owner, owner).wait_recv()
            rows_copy(3, owner).wait_recv()
            absorb(3, state_three(base[...], owner))

    def whole(source):
        if source < 2:
            return me != source
        own = (me == 3) & across_two if source == 2 else (me == 2) & across_three
        absorbed = left & (maps_two if source == 2 else maps_three)
        return jnp.logical_not(own | absorbed | (me == source))

    step_row = pick(my_head, lambda h: w_step[...].astype(jnp.float32)[h : h + 1, :])
    step_rows = jnp.broadcast_to(step_row, (16, width)).astype(jnp.bfloat16)
    gain_two = pick(my_head, lambda h: gain_second[:, lanes(h)])

    def local_terms(columns):
        values_two = jnp.dot(columns, wv_buf[...], preferred_element_type=jnp.float32).astype(
            jnp.bfloat16
        )
        keys_two = jnp.dot(columns, wk_buf[...], preferred_element_type=jnp.float32).astype(
            jnp.bfloat16
        )
        pre = dot_nt(step_rows, columns)[0:8].astype(jnp.bfloat16).astype(jnp.float32)
        shifted = pre + step_bias[my_head]
        soft = jnp.maximum(shifted, 0.0) + jnp.log1p(jnp.exp(-jnp.abs(shifted)))
        run_row = cumsum_rows(-rates_second[my_head] * soft, upper_buf[...])[0:1]
        run_col = column_of(run_row, width)
        half = keys_two.shape[1] // 2
        keys_now, queries_now = keys_two[:, :half], keys_two[:, half:]
        raw = inner_any_order(
            values_two,
            keys_now,
            queries_now,
            run_row,
            run_col,
            bias_buf[...],
            skip_second[my_head],
        )
        return raw, queries_now, run_col, state_part(values_two, keys_now, run_col)

    for group in range(groups):
        for source in range(parts):
            @pl.when(whole(source))
            def _():
                first_copy(me, group, source).wait_recv()

        blocks = range(group * GROUP, (group + 1) * GROUP)
        terms = [local_terms(column_buf[block].reshape(length, width)) for block in blocks]
        for block, (raw, queries_now, run_col, update) in zip(blocks, terms):
            if block == 0:
                state = update
            else:
                before = run_state[...] if block == blocks[0] else state
                raw = raw + outer_part(queries_now, run_col, before)
                state = advanced(before, run_col, update)
            normed = (raw * norm_factor(raw) * gain_two).astype(jnp.bfloat16)
            for target in range(parts):
                piece = normed[target * chunk : (target + 1) * chunk].astype(jnp.float32)
                piece = piece + column_buf[block, target].astype(jnp.float32)
                second_buf[target, block] = piece.astype(jnp.bfloat16)
        run_state[...] = state
        for target in range(parts):
            send(me != target, second_copy(group, target, me))

            @pl.when(me == target)
            def _():
                for block in blocks:
                    home_buf[target, block] = second_buf[target, block]

    for condition, copy in started:
        @pl.when(condition)
        def _():
            copy.wait_send()

    for group in range(groups):
        ready_pairs = range(
            max((group + 1) * GROUP - max(GROUP, 2), 0), (group + 1) * GROUP // 2 * 2, 2
        )
        for unit in range(parts):
            @pl.when(me != unit)
            def _():
                second_copy(group, me, unit).wait_recv()

            for pair in ready_pairs:
                total = [home_buf[unit, block].astype(jnp.float32) for block in (pair, pair + 1)]
                for row in range(rows_here):
                    place = slice(row * cols_here, (row + 1) * cols_here)
                    out[
                        unit // heads,
                        pl.ds(row * side + pair * cols_here, 2 * cols_here),
                        lanes(unit % heads),
                    ] = jnp.concatenate([part[place] for part in total], axis=0).astype(
                        jnp.bfloat16
                    )


def local_fused(
    parts,
    values_first,
    keys_first,
    queries_first,
    steps_first,
    rates_first,
    skip_first,
    gain_first,
    w_values,
    w_keys,
    w_step,
    step_bias,
    rates_second,
    skip_second,
    gain_second,
):
    slab_count, length, feat_width = values_first.shape
    heads = rates_first.shape[0]
    width = feat_width // heads
    side = math.isqrt(parts * length)
    chunk = length // parts
    groups = parts // GROUP
    anywhere = pl.BlockSpec(memory_space=pl.ANY)
    dma = pltpu.SemaphoreType.DMA

    def vmem(dtype, *shape):
        return pltpu.VMEM(shape, dtype)

    bf16, f32 = jnp.bfloat16, jnp.float32
    return pl.pallas_call(
        functools.partial(fused_kernel, parts, heads, side),
        out_shape=jax.ShapeDtypeStruct(values_first.shape, bf16),
        in_specs=[anywhere] * 14,
        out_specs=pl.BlockSpec(memory_space=pltpu.VMEM),
        scratch_shapes=[
            vmem(bf16, *values_first.shape),
            vmem(bf16, *keys_first.shape),
            vmem(bf16, *queries_first.shape),
            vmem(f32, *steps_first.shape),
            vmem(bf16, *w_values.shape[1:]),
            vmem(bf16, *w_keys.shape[1:]),
            vmem(bf16, *w_step.shape),
            vmem(f32, 1, feat_width),
            vmem(f32, 1, feat_width),
        ]
        + [pltpu.SMEM((heads,), f32)] * 5
        + [
            vmem(f32, parts + -parts % 8, length),
            vmem(f32, parts, length, width),
            vmem(f32, parts, width, width),
            vmem(f32, parts, length, width),
            vmem(bf16, parts, width, width),
            vmem(bf16, parts, length, width),
            vmem(bf16, parts, width, width),
            vmem(bf16, width, width),
            vmem(bf16, parts, width, width),
            vmem(f32, parts, parts + -parts % 8, length),
            vmem(bf16, parts, length, width),
            vmem(bf16, parts, length, width),
            vmem(bf16, parts, parts, chunk, width),
            vmem(bf16, parts, parts, chunk, width),
            vmem(bf16, parts, parts, chunk, width),
            vmem(bf16, parts, parts, chunk, width),
            vmem(f32, length, length),
            vmem(bf16, length, length),
            vmem(f32, width, width),
            dma((11,)),
            dma((3, parts)),
            dma((parts, parts)),
            dma((parts,)),
            dma((parts,)),
            dma((parts,)),
            dma((parts,)),
            dma,
            dma((parts,)),
            dma((parts,)),
            dma((parts,)),
            dma((parts,)),
            dma((parts, groups)),
            dma((parts, groups)),
            dma((parts, groups)),
            dma((parts, groups)),
            pltpu.SemaphoreType.REGULAR,
        ],
        compiler_params=pltpu.CompilerParams(
            collective_id=0, has_side_effects=True, vmem_limit_bytes=VMEM_GRANT
        ),
    )(
        *(
            pltpu.with_memory_space_constraint(array, pltpu.HBM)
            for array in (
                values_first,
                keys_first,
                queries_first,
                steps_first,
                w_values,
                w_keys,
                w_step,
                gain_first.reshape(1, -1),
                gain_second.reshape(1, -1),
                rates_first,
                skip_first,
                step_bias,
                rates_second,
                skip_second,
            )
        )
    )


def fits_fused(parts, args):
    values, w_values, w_keys = args[0], args[7], args[8]
    slab_count, length, feat_width = values.shape
    heads = args[4].shape[0]
    side = math.isqrt(parts * length)
    return (
        slab_count * heads == parts
        and parts == len(ORDER)
        and (side // parts) * (length // side) % 16 == 0
        and length <= BLOCK
        and length % 256 == 0
        and side * side == parts * length
        and side % parts == 0
        and length % side == 0
        and (length // side) % 8 == 0
        and feat_width // heads == 128
        and w_values.shape[1:] == (128, 128)
        and w_keys.shape[1:] == (128, 256)
    )


def solution(mesh):
    parts = mesh.shape["seq"]

    def chosen(*args):
        if fits_fused(parts, args):
            return local_fused(parts, *args)
        return local(*args)

    placed = (
        P("slab", "seq", "head"),
        P("slab", "seq", "head"),
        P("slab", "seq", "head"),
        P("slab", "head", "seq"),
        P("head"),
        P("head"),
        P("head"),
        P("head", None, None),
        P("head", None, None),
        P("head", None),
        P("head"),
        P("head"),
        P("head"),
        P("head"),
    )
    return jax.shard_map(
        chosen, mesh=mesh, in_specs=placed, out_specs=P("slab", "seq", "head"), check_vma=False
    )
```

```python
import functools
import math

import jax
import jax.numpy as jnp
from jax import lax
from jax.experimental import pallas as pl
from jax.experimental.pallas import tpu as pltpu
from jax.sharding import PartitionSpec as P

N = 128
BLOCK = 256
ROWS_DEV = 8
VMEM_GRANT = 16 << 20
GROUP = 2
ORDER = (0, 1, 2, 3)
FINISH = ((2, 3), (0,), (1,))
MAPS_TWO = (True, False)
MAPS_THREE = (False, False)
ACROSS_TWO = (True, False)
ACROSS_THREE = (True, True)
CHAIN = (False, True)


def cumulated(terms, axis):
    size = terms.shape[axis]
    ranks = lax.iota(jnp.int32, size)
    upper = (ranks[:, None] <= ranks[None, :]).astype(jnp.float32)
    sums = jnp.einsum(
        "...j,ji->...i",
        jnp.moveaxis(terms, axis, -1),
        upper,
        precision=lax.Precision.HIGHEST,
    )
    return jnp.moveaxis(sums, -1, axis)


def block_terms(values, keys_in, queries, log_decay, block_len):
    slab_count, length, feat_width = values.shape
    head_count = log_decay.shape[1]
    blocks = length // block_len
    value_blocks = values.reshape(
        slab_count, blocks, block_len, head_count, feat_width // head_count
    )
    key_blocks = keys_in.reshape(
        slab_count, blocks, block_len, head_count, keys_in.shape[2] // head_count
    )
    query_blocks = queries.reshape(
        slab_count, blocks, block_len, head_count, queries.shape[2] // head_count
    )
    running = cumulated(log_decay.reshape(slab_count, head_count, blocks, block_len), 3)
    running_sc = jnp.transpose(running, (0, 2, 1, 3))
    running_pos = jnp.transpose(running, (0, 2, 3, 1))
    scores = jnp.einsum(
        "scihn,scjhn->schij", query_blocks, key_blocks, preferred_element_type=jnp.float32
    )
    row_ids = lax.broadcasted_iota(jnp.int32, (block_len, block_len), 0)
    col_ids = lax.broadcasted_iota(jnp.int32, (block_len, block_len), 1)
    spread = running_sc[..., :, None] - running_sc[..., None, :]
    decays = jnp.exp(jnp.where(row_ids >= col_ids, spread, -jnp.inf))
    mixing = (scores * decays).astype(jnp.bfloat16)
    inner_sum = jnp.einsum(
        "schij,scjhp->scihp", mixing, value_blocks, preferred_element_type=jnp.float32
    )
    to_end = jnp.exp(running_pos[:, :, -1:, :] - running_pos)
    weighted = (key_blocks * to_end[..., None]).astype(jnp.bfloat16)
    local_states = jnp.einsum(
        "scjhn,scjhp->schnp", weighted, value_blocks, preferred_element_type=jnp.float32
    )
    block_logs = running_sc[..., -1]
    return (value_blocks, query_blocks, running_pos, inner_sum, local_states, block_logs)


def entry_states(local_states, block_logs):

    def advance(carried, entry_item):
        update, log_total = entry_item
        return (jnp.exp(log_total)[..., None, None] * carried + update, carried)

    start_state = jnp.zeros(local_states.shape[:1] + local_states.shape[2:], jnp.float32)
    final_state, entries = lax.scan(
        advance, start_state, (jnp.moveaxis(local_states, 1, 0), jnp.moveaxis(block_logs, 1, 0))
    )
    return (final_state, jnp.moveaxis(entries, 0, 1))


def carry_into(final_state, device_log):
    log_totals = lax.all_gather(device_log[None], "seq", axis=0, tiled=True)
    my_index = lax.axis_index("seq")
    ranks_all = lax.iota(jnp.int32, log_totals.shape[0])
    between = jnp.logical_and(
        ranks_all[None, :] > ranks_all[:, None], ranks_all[None, :] < my_index
    ).astype(jnp.float32)
    span_logs = jnp.einsum("dk,ksh->dsh", between, log_totals, precision=lax.Precision.HIGHEST)
    weights = jnp.where((ranks_all < my_index)[:, None, None], jnp.exp(span_logs), 0.0)
    return jnp.sum(
        weights[..., None, None] * lax.all_gather(final_state[None], "seq", axis=0, tiled=True),
        axis=0,
    )


def selective_scan(values, keys_in, queries, log_decay, skip, gain):
    block_len = min(BLOCK, values.shape[1])
    value_blocks, query_blocks, running_pos, inner_sum, local_states, block_logs = block_terms(
        values, keys_in, queries, log_decay, block_len
    )
    final_state, entries = entry_states(local_states, block_logs)
    carried = carry_into(final_state, jnp.sum(block_logs, axis=1))
    before = cumulated(block_logs, 1) - block_logs
    states = (entries + jnp.exp(before)[..., None, None] * carried[:, None]).astype(jnp.bfloat16)
    outer_sum = jnp.einsum(
        "scihn,schnp->scihp", query_blocks, states, preferred_element_type=jnp.float32
    )
    raw_out = (
        inner_sum
        + outer_sum * jnp.exp(running_pos)[..., None]
        + skip[:, None] * value_blocks.astype(jnp.float32)
    )
    scaled = raw_out * lax.rsqrt(jnp.mean(raw_out * raw_out, axis=-1, keepdims=True) + 1e-05)
    normed = (scaled * gain.reshape(skip.shape[0], -1)).astype(jnp.bfloat16)
    return normed.reshape(normed.shape[0], -1, normed.shape[3] * normed.shape[4])


def project_rows(features, w_values, w_keys, w_step):
    slab_count, length, feat_width = features.shape
    head_count = w_values.shape[0]
    split_feat = features.reshape(slab_count, length, head_count, feat_width // head_count)
    values_two = jnp.einsum(
        "slhp,hpk->slhk", split_feat, w_values, preferred_element_type=jnp.float32
    ).astype(jnp.bfloat16)
    keys_two = jnp.einsum(
        "slhp,hpk->slhk", split_feat, w_keys, preferred_element_type=jnp.float32
    ).astype(jnp.bfloat16)
    step_pre = jnp.einsum(
        "slhp,hp->slh", split_feat, w_step, preferred_element_type=jnp.float32
    ).astype(jnp.bfloat16)
    return (values_two, keys_two, step_pre)


def second_scan(values_two, keys_two, step_pre, step_bias, rates_second, skip_second, gain_second):
    slab_count, length, head_count, key_width = keys_two.shape
    step_size = jax.nn.softplus(step_pre.astype(jnp.float32) + step_bias)
    log_decay = -rates_second[None, :, None] * jnp.transpose(step_size, (0, 2, 1))
    return selective_scan(
        values_two.reshape(slab_count, length, -1),
        keys_two[..., :N].reshape(slab_count, length, -1),
        keys_two[..., N:].reshape(slab_count, length, -1),
        log_decay,
        skip_second,
        gain_second,
    )


def columns_from(received):
    slab_count, rows_all, cols_here, last_width = received.shape
    return jnp.transpose(received, (0, 2, 1, 3)).reshape(
        slab_count, cols_here * rows_all, last_width
    )


def local(
    values_first,
    keys_first,
    queries_first,
    steps_first,
    rates_first,
    skip_first,
    gain_first,
    w_values,
    w_keys,
    w_step,
    step_bias,
    rates_second,
    skip_second,
    gain_second,
):
    log_first = -rates_first[None, :, None] * steps_first
    first_out = selective_scan(
        values_first, keys_first, queries_first, log_first, skip_first, gain_first
    )
    slab_count, length, feat_width = first_out.shape
    home_grid = first_out.reshape(slab_count, ROWS_DEV, length // ROWS_DEV, feat_width)
    received = lax.all_to_all(home_grid, "seq", split_axis=2, concat_axis=1, tiled=True)
    rows_all = received.shape[1]
    cols_here = received.shape[2]
    values_two, keys_two, step_pre = project_rows(columns_from(received), w_values, w_keys, w_step)
    result = second_scan(
        values_two, keys_two, step_pre, step_bias, rates_second, skip_second, gain_second
    )
    column_out = result.reshape(received.shape[0], cols_here, rows_all, result.shape[2])
    home_back = lax.all_to_all(column_out, "seq", split_axis=2, concat_axis=1, tiled=True)
    second_home = jnp.transpose(home_back, (0, 2, 1, 3)).reshape(slab_count, length, feat_width)
    return (first_out.astype(jnp.float32) + second_home.astype(jnp.float32)).astype(jnp.bfloat16)


def cumsum_rows(rows, upper):
    high = rows.astype(jnp.bfloat16).astype(jnp.float32)
    rest = rows - high
    mid = rest.astype(jnp.bfloat16).astype(jnp.float32)
    low = rest - mid
    count = rows.shape[0]
    stacked = jnp.concatenate([high, mid, low, jnp.zeros_like(low)], axis=0).astype(jnp.bfloat16)
    sums = jnp.dot(stacked, upper, preferred_element_type=jnp.float32)
    return sums[:count] + sums[count : 2 * count] + sums[2 * count : 3 * count]


def dot_nt(left, right):
    return lax.dot_general(
        left, right, (((1,), (1,)), ((), ())), preferred_element_type=jnp.float32
    )


def dot_tn(left, right):
    return lax.dot_general(
        left, right, (((0,), (0,)), ((), ())), preferred_element_type=jnp.float32
    )


def column_of(run_row, width):
    return jnp.transpose(jnp.broadcast_to(run_row, (width, run_row.shape[1])))


def inner_part(values, keys_in, queries, run_row, run_col, skip):
    length, width = values.shape
    half = length // 2
    lower = lax.broadcasted_iota(jnp.int32, (half, half), 0) >= lax.broadcasted_iota(
        jnp.int32, (half, half), 1
    )
    reps = half // width

    def decay(rows, columns, masked):
        left = jnp.concatenate([run_col[rows]] * reps, axis=1) if reps > 1 else run_col[rows]
        spread = left - run_row[:, columns]
        return jnp.exp(jnp.where(lower, spread, -jnp.inf) if masked else spread)

    top, bottom = slice(0, half), slice(half, length)
    scores_top = dot_nt(queries[top], keys_in[top])
    scores_bottom = dot_nt(queries[bottom], keys_in)
    mix_top = (scores_top * decay(top, top, True)).astype(jnp.bfloat16)
    mix_bottom = jnp.concatenate(
        [
            (scores_bottom[:, top] * decay(bottom, top, False)).astype(jnp.bfloat16),
            (scores_bottom[:, bottom] * decay(bottom, bottom, True)).astype(jnp.bfloat16),
        ],
        axis=1,
    )
    inner = jnp.concatenate(
        [
            jnp.dot(mix_top, values[top], preferred_element_type=jnp.float32),
            jnp.dot(mix_bottom, values, preferred_element_type=jnp.float32),
        ],
        axis=0,
    )
    return inner + skip * values.astype(jnp.float32)


def state_part(values, keys_in, run_col):
    last = run_col[run_col.shape[0] - 1 :, :]
    weighted = (keys_in.astype(jnp.float32) * jnp.exp(last - run_col)).astype(jnp.bfloat16)
    return dot_tn(weighted, values)


def outer_part(queries, run_col, state):
    outer = jnp.dot(queries, state.astype(jnp.bfloat16), preferred_element_type=jnp.float32)
    return jnp.exp(run_col) * outer


def advanced(state, run_col, update):
    return jnp.exp(run_col[run_col.shape[0] - 1 :, :]) * state + update


def norm_factor(raw):
    return lax.rsqrt(jnp.mean(raw * raw, axis=1, keepdims=True) + 1e-05)


def decay_outer(queries, run_col, state):
    outer = jnp.dot(queries, state, preferred_element_type=jnp.float32)
    return jnp.exp(run_col) * outer


def inner_any_order(values, keys_in, queries, run_row, run_col, bias, skip):
    length, width = values.shape
    left = jnp.concatenate([run_col] * (length // width), axis=1)
    scores = dot_nt(queries, keys_in)
    mixing = (scores * jnp.exp(left - run_row + bias)).astype(jnp.bfloat16)
    inner = jnp.dot(mixing, values, preferred_element_type=jnp.float32)
    return inner + skip * values.astype(jnp.float32)


def fused_kernel(parts, heads, side, *refs):
    values, keys_in, queries, steps, w_values, w_keys = refs[:6]
    small_in, out = refs[6:14], refs[14]
    v_buf, k_buf, q_buf, step_buf, wv_buf, wk_buf = refs[15:21]
    small = refs[21:29]
    w_step, gain_first, gain_second = small[:3]
    rates_first, skip_first, step_bias, rates_second, skip_second = small[3:]
    row_buf, col_buf, update_buf, raw_buf, stage_state, stage_raw = refs[29:35]
    state_in, back_in, far_in, rows_in, raw_in, maps_in = refs[35:41]
    first_buf, column_buf, second_buf, home_buf, bias_buf, upper_buf, run_state = refs[41:48]
    own_sem, unit_sem, state_send, rows_send, raw_send, maps_send = refs[48:54]
    state_recv, back_recv, far_recv, rows_recv, raw_recv, maps_recv = refs[54:60]
    first_send, first_recv, second_send, second_recv, ready = refs[60:]
    me = lax.axis_index("seq")
    length, width = raw_buf.shape[1:]
    slabs = parts // heads
    last_part = parts - 1
    rows_here, cols_here = side // parts, length // side
    chunk = rows_here * cols_here
    groups = parts // GROUP
    my_head = lax.rem(me, heads)
    mesh_id = pl.DeviceIdType.MESH
    even = lax.rem(lax.axis_index("head"), 2) == 0

    def chosen(modes):
        if modes[0] == modes[1]:
            return me >= 0 if modes[0] else me < 0
        return even if modes[0] else jnp.logical_not(even)

    maps_two, maps_three = chosen(MAPS_TWO), chosen(MAPS_THREE)
    chain = chosen(CHAIN)
    far_needed = jnp.logical_not(maps_three | chain)
    across_two, across_three = chosen(ACROSS_TWO), chosen(ACROSS_THREE)
    whole_two, whole_three = jnp.logical_not(across_two), jnp.logical_not(across_three)
    states_two, states_three = jnp.logical_not(maps_two), jnp.logical_not(maps_three)
    left = me < 2
    started = []

    def send(condition, copy):
        @pl.when(condition)
        def _():
            copy.start()

        started.append((condition, copy))


    def lanes(head):
        return slice(head * width, (head + 1) * width)

    def of_unit(array, unit):
        return array[unit // heads, :, lanes(unit % heads)]

    barrier = pltpu.get_barrier_semaphore()

    def greet(sources, target):
        @pl.when(sources)
        def _():
            pl.semaphore_signal(
                barrier, inc=1, device_id={"seq": target}, device_id_type=mesh_id
            )

    for target in range(1, parts):
        greet(me != target, target)
    greet(me == 1, 0)

    step_copy = pltpu.make_async_copy(steps, step_buf, own_sem.at[0])
    step_copy.start()
    small_copies = [
        pltpu.make_async_copy(src, dst, own_sem.at[3 + index])
        for index, (src, dst) in enumerate(zip(small_in, small))
    ]
    unit_copies = [
        [
            pltpu.make_async_copy(src.at[slab], dst.at[slab], unit_sem.at[kind, slab])
            for slab in range(slabs)
        ]
        for kind, (src, dst) in enumerate(((keys_in, k_buf), (values, v_buf), (queries, q_buf)))
    ]
    weight_copies = [
        pltpu.make_async_copy(w_values.at[my_head], wv_buf, own_sem.at[1]),
        pltpu.make_async_copy(w_keys.at[my_head], wk_buf, own_sem.at[2]),
    ]
    early = [*unit_copies[0], *unit_copies[1]]
    late = [*unit_copies[2], *small_copies[:3], *small_copies[4:], *weight_copies]
    small_copies[3].start()
    for copy in early + late:
        copy.start()

    square = (length, length)
    upper = jnp.where(
        lax.broadcasted_iota(jnp.int32, square, 0) <= lax.broadcasted_iota(jnp.int32, square, 1),
        1.0,
        0.0,
    ).astype(jnp.bfloat16)

    def remote(src, dst, send_sem, recv_sem, target):
        return pltpu.make_async_remote_copy(
            src_ref=src,
            dst_ref=dst,
            send_sem=send_sem,
            recv_sem=recv_sem,
            device_id={"seq": target},
            device_id_type=mesh_id,
        )

    def state_copy(unit, target):
        return remote(
            stage_state.at[unit],
            state_in.at[unit],
            state_send.at[target, unit],
            state_recv.at[unit],
            target,
        )

    def back_copy():
        return remote(stage_state.at[0], back_in, state_send.at[0, 0], back_recv, 0)

    def far_copy(unit, target):
        return remote(
            stage_state.at[unit],
            far_in.at[unit],
            state_send.at[target, unit],
            far_recv.at[unit],
            target,
        )

    def rows_copy(source, target):
        return remote(
            row_buf, rows_in.at[source], rows_send.at[target], rows_recv.at[source], target
        )

    def raw_copy(source, target):
        return remote(
            stage_raw.at[target],
            raw_in.at[source],
            raw_send.at[target],
            raw_recv.at[source],
            target,
        )

    def maps_copy(source, target):
        return remote(
            queries.at[target // heads, :, lanes(target % heads)],
            maps_in.at[source],
            maps_send.at[target],
            maps_recv.at[source],
            target,
        )

    def first_copy(unit, group, source):
        return remote(
            first_buf.at[unit, pl.ds(group * GROUP, GROUP)],
            column_buf.at[pl.ds(group * GROUP, GROUP), source],
            first_send.at[unit, group],
            first_recv.at[source, group],
            unit,
        )

    def second_copy(group, target, source):
        return remote(
            second_buf.at[target, pl.ds(group * GROUP, GROUP)],
            home_buf.at[source, pl.ds(group * GROUP, GROUP)],
            second_send.at[target, group],
            second_recv.at[source, group],
            target,
        )

    step_copy.wait()
    small_copies[3].wait()
    logs = [
        -rates_first[head] * step_buf[slab, head : head + 1, :]
        for slab in range(slabs)
        for head in range(heads)
    ]
    logs = jnp.concatenate(logs + logs[:1] * (-parts % 8), axis=0)
    running = cumsum_rows(logs, upper)
    row_buf[...] = running
    columns_of = [column_of(running[unit : unit + 1], width) for unit in range(parts)]
    for copy in early:
        copy.wait()
    @pl.when(me > 1)
    def _():
        pl.semaphore_wait(barrier, last_part)

    @pl.when(me == last_part)
    def _():
        pl.semaphore_signal(ready, inc=1, device_id={"seq": 0}, device_id_type=mesh_id)

    for target in (0, 1):
        send((me == 2) & maps_two, maps_copy(2, target))
        send((me == 3) & maps_three, maps_copy(3, target))
    send((me == 3) & across_three, maps_copy(3, 2))
    updates = [
        state_part(of_unit(v_buf, unit), of_unit(k_buf, unit), columns_of[unit])
        for unit in range(parts)
    ]
    for unit in range(parts):
        stage_state[unit] = updates[unit].astype(jnp.bfloat16)

    rows_right = far_needed | across_two | whole_three
    send((me == 2) & rows_right, rows_copy(2, 3))
    for unit in (0, 1):
        send((me == 2) & far_needed, far_copy(unit, 3))
    send((me == 2) & across_two, far_copy(3, 3))
    send((me == 2) & whole_three, far_copy(2, 3))
    for target in (0, 1):
        send((me == 2) & (maps_two | maps_three), rows_copy(2, target))
        send((me == 3) & maps_three, rows_copy(3, target))
        send((me == 2) & maps_three, far_copy(target, target))
    send((me == 3) & across_three, rows_copy(3, 2))

    @pl.when(me == 0)
    def _():
        pl.semaphore_wait(barrier, 1)

    for unit in range(parts):
        send(me == 0, state_copy(unit, 1))

    @pl.when(me == 0)
    def _():
        state_in[...] = jnp.zeros_like(state_in)

    for unit in range(parts):
        col_buf[unit] = columns_of[unit]
        update_buf[unit] = updates[unit]
    for copy in late:
        copy.wait()
    raws = [
        inner_part(
            of_unit(v_buf, unit),
            of_unit(k_buf, unit),
            of_unit(q_buf, unit),
            running[unit : unit + 1],
            columns_of[unit],
            skip_first[unit % heads],
        )
        for unit in range(parts)
    ]
    for unit in range(parts):
        raw_buf[unit] = raws[unit]
        stage_raw[unit] = raws[unit].astype(jnp.bfloat16)

    for target in (0, 1):
        send((me == 2) & maps_two, raw_copy(2, target))
        send((me == 3) & maps_three, raw_copy(3, target))
    send((me == 2) & across_two, maps_copy(2, 3))
    send((me == 2) & across_two, raw_copy(2, 3))
    send((me == 3) & across_three, raw_copy(3, 2))

    def rank_of(index):
        owner, inside = lax.div(index, chunk), lax.rem(index, chunk)
        row, col = lax.div(inside, cols_here), lax.rem(inside, cols_here)
        return col * side + owner * rows_here + row

    rank_sub = rank_of(lax.broadcasted_iota(jnp.int32, (length, width), 0))
    rank_sub = jnp.concatenate([rank_sub] * (length // width), axis=1)
    rank_lane = rank_of(lax.broadcasted_iota(jnp.int32, (8, length), 1))[0:1]
    bias_buf[...] = jnp.where(rank_lane <= rank_sub, 0.0, -jnp.inf)
    upper_buf[...] = jnp.where(rank_sub <= rank_lane, 1.0, 0.0).astype(jnp.bfloat16)

    def ordered(normed):
        return [
            jnp.concatenate(
                [
                    normed[row * side + block * cols_here : row * side + (block + 1) * cols_here]
                    for row in range(rows_here)
                ],
                axis=0,
            ).astype(jnp.bfloat16)
            for block in range(parts)
        ]

    def finish(unit):
        raw = raw_buf[unit] + decay_outer(of_unit(q_buf, unit), col_buf[unit], state_in[unit])
        normed = raw * norm_factor(raw) * gain_first[:, lanes(unit % heads)]
        for block, piece in enumerate(ordered(normed)):
            first_buf[unit, block] = piece

        @pl.when(me == unit)
        def _():
            for block in range(parts):
                column_buf[block, unit] = first_buf[unit, block]

    def send_first(condition, *units):
        for group in range(groups):
            for unit in units:
                send(condition, first_copy(unit, group, me))

    @pl.when(me == 1)
    def _():
        pl.semaphore_wait(barrier, last_part)

    for unit in ORDER:
        @pl.when(me == 1)
        def _():
            state_copy(unit, 1).wait_recv()
            last = jnp.exp(col_buf[unit, length - 1 :, :])
            carried = last * state_in[unit].astype(jnp.float32) + update_buf[unit]
            stage_state[unit] = carried.astype(jnp.bfloat16)

        if unit > 1:
            send((me == 1) & (across_two if unit == 3 else whole_three), state_copy(unit, 3))
            send((me == 1) & (whole_two if unit == 3 else me == 1), state_copy(unit, 2))
        else:
            send((me == 1) & far_needed, state_copy(unit, 3))
            send((me == 1) & (states_two | chain), state_copy(unit, 2))
            if unit == 0:
                send((me == 1) & (maps_two | maps_three), back_copy())

    for units in FINISH:
        @pl.when(left)
        def _():
            for unit in units:
                finish(unit)

        if units == (1,):
            send_first(me == 0, *units)
        else:
            send_first(me == 1, *[unit for unit in units if unit != 1])

    def state_three(base, unit):
        row = rows_in[2, pl.ds(unit, 1), :]
        last = jnp.exp(jnp.broadcast_to(row[:, length - 1 :], (1, width)))
        carried = last * base.astype(jnp.float32) + far_in[unit].astype(jnp.float32)
        return carried.astype(jnp.bfloat16)

    @pl.when(((me == 3) & rows_right) | (left & (maps_two | maps_three)))
    def _():
        rows_copy(2, me).wait_recv()

    def advance(unit):
        state_copy(unit, 2).wait_recv()
        last = jnp.exp(col_buf[unit, length - 1 :, :])
        carried = last * state_in[unit].astype(jnp.float32) + update_buf[unit]
        stage_state[unit] = carried.astype(jnp.bfloat16)

    for unit in (0, 1):
        @pl.when((me == 2) & (states_two | chain))
        def _():
            advance(unit)

        send((me == 2) & chain, state_copy(unit, 3))

        @pl.when((me == 2) & states_two)
        def _():
            finish(unit)

        @pl.when((me == 3) & states_three)
        def _():
            state_copy(unit, 3).wait_recv()

            @pl.when(far_needed)
            def _():
                far_copy(unit, 3).wait_recv()
                state_in[unit] = state_three(state_in[unit], unit)

            finish(unit)

        send_first(((me == 2) & states_two) | ((me == 3) & states_three), unit)

    def pick(head, select):
        chosen_one = select(0)
        for index in range(1, heads):
            chosen_one = jnp.where(head == index, select(index), chosen_one)
        return chosen_one

    gain_one = pick(my_head, lambda h: gain_first[:, lanes(h)])

    def absorb(source, state):
        maps_copy(source, 0).wait_recv()
        raw_copy(source, me).wait_recv()
        run_col = column_of(rows_in[source, pl.ds(me, 1), :], width)
        raw = raw_in[source].astype(jnp.float32) + decay_outer(maps_in[source], run_col, state)
        normed = raw * norm_factor(raw) * gain_one
        for block, piece in enumerate(ordered(normed)):
            column_buf[block, source] = piece

    @pl.when((me == 2) & whole_two)
    def _():
        advance(3)

    send((me == 2) & whole_two, state_copy(3, 3))

    @pl.when((me == 2) & whole_two)
    def _():
        finish(3)

    send_first((me == 2) & whole_two, 3)

    @pl.when((me == 3) & whole_three)
    def _():
        state_copy(2, 3).wait_recv()
        far_copy(2, 3).wait_recv()
        state_in[2] = state_three(state_in[2], 2)
        finish(2)

    send_first((me == 3) & whole_three, 2)

    @pl.when(me == 2)
    def _():
        state_copy(2, 2).wait_recv()
        finish(2)

    @pl.when((me == 2) & across_three)
    def _():
        rows_copy(3, 2).wait_recv()
        last = jnp.exp(col_buf[2, length - 1 :, :])
        carried = last * state_in[2].astype(jnp.float32) + update_buf[2]
        absorb(3, carried.astype(jnp.bfloat16))

    @pl.when(me == 3)
    def _():
        state_copy(3, 3).wait_recv()

        @pl.when(across_two)
        def _():
            absorb(2, state_in[3])

            far_copy(3, 3).wait_recv()
            state_in[3] = state_three(state_in[3], 3)

        finish(3)

    @pl.when(me == 0)
    def _():
        pl.semaphore_wait(ready, 1)

    send_first(me == 0, 2, 3)

    for owner in (0, 1):
        if owner == 0:
            @pl.when((me == 0) & (maps_two | maps_three))
            def _():
                back_copy().wait_recv()

        base = back_in if owner == 0 else stage_state.at[1]

        @pl.when((me == owner) & maps_two)
        def _():
            absorb(2, base[...])

        @pl.when((me == owner) & maps_three)
        def _():
            far_copy(owner, owner).wait_recv()
            rows_copy(3, owner).wait_recv()
            absorb(3, state_three(base[...], owner))

    def whole(source):
        if source < 2:
            return me != source
        own = (me == 3) & across_two if source == 2 else (me == 2) & across_three
        absorbed = left & (maps_two if source == 2 else maps_three)
        return jnp.logical_not(own | absorbed | (me == source))

    step_row = pick(my_head, lambda h: w_step[...].astype(jnp.float32)[h : h + 1, :])
    step_rows = jnp.broadcast_to(step_row, (16, width)).astype(jnp.bfloat16)
    gain_two = pick(my_head, lambda h: gain_second[:, lanes(h)])

    def local_terms(columns):
        values_two = jnp.dot(columns, wv_buf[...], preferred_element_type=jnp.float32).astype(
            jnp.bfloat16
        )
        keys_two = jnp.dot(columns, wk_buf[...], preferred_element_type=jnp.float32).astype(
            jnp.bfloat16
        )
        pre = dot_nt(step_rows, columns)[0:8].astype(jnp.bfloat16).astype(jnp.float32)
        shifted = pre + step_bias[my_head]
        soft = jnp.maximum(shifted, 0.0) + jnp.log1p(jnp.exp(-jnp.abs(shifted)))
        run_row = cumsum_rows(-rates_second[my_head] * soft, upper_buf[...])[0:1]
        run_col = column_of(run_row, width)
        half = keys_two.shape[1] // 2
        keys_now, queries_now = keys_two[:, :half], keys_two[:, half:]
        raw = inner_any_order(
            values_two,
            keys_now,
            queries_now,
            run_row,
            run_col,
            bias_buf[...],
            skip_second[my_head],
        )
        return raw, queries_now, run_col, state_part(values_two, keys_now, run_col)

    for group in range(groups):
        for source in range(parts):
            @pl.when(whole(source))
            def _():
                first_copy(me, group, source).wait_recv()

        blocks = range(group * GROUP, (group + 1) * GROUP)
        terms = [local_terms(column_buf[block].reshape(length, width)) for block in blocks]
        for block, (raw, queries_now, run_col, update) in zip(blocks, terms):
            if block == 0:
                state = update
            else:
                before = run_state[...] if block == blocks[0] else state
                raw = raw + outer_part(queries_now, run_col, before)
                state = advanced(before, run_col, update)
            normed = (raw * norm_factor(raw) * gain_two).astype(jnp.bfloat16)
            for target in range(parts):
                piece = normed[target * chunk : (target + 1) * chunk].astype(jnp.float32)
                piece = piece + column_buf[block, target].astype(jnp.float32)
                second_buf[target, block] = piece.astype(jnp.bfloat16)
        if group < groups - 1:
            run_state[...] = state

        for target in range(parts):
            send(me != target, second_copy(group, target, me))

            @pl.when(me == target)
            def _():
                for block in blocks:
                    home_buf[target, block] = second_buf[target, block]

    for condition, copy in started:
        @pl.when(condition)
        def _():
            copy.wait_send()

    for group in range(groups):
        ready_pairs = range(
            max((group + 1) * GROUP - max(GROUP, 2), 0), (group + 1) * GROUP // 2 * 2, 2
        )
        for unit in range(parts):
            @pl.when(me != unit)
            def _():
                second_copy(group, me, unit).wait_recv()

            for pair in ready_pairs:
                total = [home_buf[unit, block].astype(jnp.float32) for block in (pair, pair + 1)]
                for row in range(rows_here):
                    place = slice(row * cols_here, (row + 1) * cols_here)
                    out[
                        unit // heads,
                        pl.ds(row * side + pair * cols_here, 2 * cols_here),
                        lanes(unit % heads),
                    ] = jnp.concatenate([part[place] for part in total], axis=0).astype(
                        jnp.bfloat16
                    )


def local_fused(
    parts,
    values_first,
    keys_first,
    queries_first,
    steps_first,
    rates_first,
    skip_first,
    gain_first,
    w_values,
    w_keys,
    w_step,
    step_bias,
    rates_second,
    skip_second,
    gain_second,
):
    slab_count, length, feat_width = values_first.shape
    heads = rates_first.shape[0]
    width = feat_width // heads
    side = math.isqrt(parts * length)
    chunk = length // parts
    groups = parts // GROUP
    anywhere = pl.BlockSpec(memory_space=pl.ANY)
    dma = pltpu.SemaphoreType.DMA

    def vmem(dtype, *shape):
        return pltpu.VMEM(shape, dtype)

    bf16, f32 = jnp.bfloat16, jnp.float32
    return pl.pallas_call(
        functools.partial(fused_kernel, parts, heads, side),
        out_shape=jax.ShapeDtypeStruct(values_first.shape, bf16),
        in_specs=[anywhere] * 14,
        out_specs=pl.BlockSpec(memory_space=pltpu.VMEM),
        scratch_shapes=[
            vmem(bf16, *values_first.shape),
            vmem(bf16, *keys_first.shape),
            vmem(bf16, *queries_first.shape),
            vmem(f32, *steps_first.shape),
            vmem(bf16, *w_values.shape[1:]),
            vmem(bf16, *w_keys.shape[1:]),
            vmem(bf16, *w_step.shape),
            vmem(f32, 1, feat_width),
            vmem(f32, 1, feat_width),
        ]
        + [pltpu.SMEM((heads,), f32)] * 5
        + [
            vmem(f32, parts + -parts % 8, length),
            vmem(f32, parts, length, width),
            vmem(f32, parts, width, width),
            vmem(f32, parts, length, width),
            vmem(bf16, parts, width, width),
            vmem(bf16, parts, length, width),
            vmem(bf16, parts, width, width),
            vmem(bf16, width, width),
            vmem(bf16, parts, width, width),
            vmem(f32, parts, parts + -parts % 8, length),
            vmem(bf16, parts, length, width),
            vmem(bf16, parts, length, width),
            vmem(bf16, parts, parts, chunk, width),
            vmem(bf16, parts, parts, chunk, width),
            vmem(bf16, parts, parts, chunk, width),
            vmem(bf16, parts, parts, chunk, width),
            vmem(f32, length, length),
            vmem(bf16, length, length),
            vmem(f32, width, width),
            dma((11,)),
            dma((3, parts)),
            dma((parts, parts)),
            dma((parts,)),
            dma((parts,)),
            dma((parts,)),
            dma((parts,)),
            dma,
            dma((parts,)),
            dma((parts,)),
            dma((parts,)),
            dma((parts,)),
            dma((parts, groups)),
            dma((parts, groups)),
            dma((parts, groups)),
            dma((parts, groups)),
            pltpu.SemaphoreType.REGULAR,
        ],
        compiler_params=pltpu.CompilerParams(
            collective_id=0, has_side_effects=True, vmem_limit_bytes=VMEM_GRANT
        ),
    )(
        *(
            pltpu.with_memory_space_constraint(array, pltpu.HBM)
            for array in (
                values_first,
                keys_first,
                queries_first,
                steps_first,
                w_values,
                w_keys,
                w_step,
                gain_first.reshape(1, -1),
                gain_second.reshape(1, -1),
                rates_first,
                skip_first,
                step_bias,
                rates_second,
                skip_second,
            )
        )
    )


def fits_fused(parts, args):
    values, w_values, w_keys = args[0], args[7], args[8]
    slab_count, length, feat_width = values.shape
    heads = args[4].shape[0]
    side = math.isqrt(parts * length)
    return (
        slab_count * heads == parts
        and parts == len(ORDER)
        and (side // parts) * (length // side) % 16 == 0
        and length <= BLOCK
        and length % 256 == 0
        and side * side == parts * length
        and side % parts == 0
        and length % side == 0
        and (length // side) % 8 == 0
        and feat_width // heads == 128
        and w_values.shape[1:] == (128, 128)
        and w_keys.shape[1:] == (128, 256)
    )


def solution(mesh):
    parts = mesh.shape["seq"]

    def chosen(*args):
        if fits_fused(parts, args):
            return local_fused(parts, *args)
        return local(*args)

    placed = (
        P("slab", "seq", "head"),
        P("slab", "seq", "head"),
        P("slab", "seq", "head"),
        P("slab", "head", "seq"),
        P("head"),
        P("head"),
        P("head"),
        P("head", None, None),
        P("head", None, None),
        P("head", None),
        P("head"),
        P("head"),
        P("head"),
        P("head"),
    )
    return jax.shard_map(
        chosen, mesh=mesh, in_specs=placed, out_specs=P("slab", "seq", "head"), check_vma=False
    )
```

```python
import functools
import math

import jax
import jax.numpy as jnp
from jax import lax
from jax.experimental import pallas as pl
from jax.experimental.pallas import tpu as pltpu
from jax.sharding import PartitionSpec as P

N = 128
BLOCK = 256
ROWS_DEV = 8
VMEM_GRANT = 16 << 20
GROUP = 2
ORDER = (0, 1, 2, 3)
FINISH = ((2, 3), (0,), (1,))
MAPS_TWO = (True, False)
MAPS_THREE = (False, False)
ACROSS_TWO = (True, False)
ACROSS_THREE = (True, True)
CHAIN = (False, True)


def cumulated(terms, axis):
    size = terms.shape[axis]
    ranks = lax.iota(jnp.int32, size)
    upper = (ranks[:, None] <= ranks[None, :]).astype(jnp.float32)
    sums = jnp.einsum(
        "...j,ji->...i",
        jnp.moveaxis(terms, axis, -1),
        upper,
        precision=lax.Precision.HIGHEST,
    )
    return jnp.moveaxis(sums, -1, axis)


def block_terms(values, keys_in, queries, log_decay, block_len):
    slab_count, length, feat_width = values.shape
    head_count = log_decay.shape[1]
    blocks = length // block_len
    value_blocks = values.reshape(
        slab_count, blocks, block_len, head_count, feat_width // head_count
    )
    key_blocks = keys_in.reshape(
        slab_count, blocks, block_len, head_count, keys_in.shape[2] // head_count
    )
    query_blocks = queries.reshape(
        slab_count, blocks, block_len, head_count, queries.shape[2] // head_count
    )
    running = cumulated(log_decay.reshape(slab_count, head_count, blocks, block_len), 3)
    running_sc = jnp.transpose(running, (0, 2, 1, 3))
    running_pos = jnp.transpose(running, (0, 2, 3, 1))
    scores = jnp.einsum(
        "scihn,scjhn->schij", query_blocks, key_blocks, preferred_element_type=jnp.float32
    )
    row_ids = lax.broadcasted_iota(jnp.int32, (block_len, block_len), 0)
    col_ids = lax.broadcasted_iota(jnp.int32, (block_len, block_len), 1)
    spread = running_sc[..., :, None] - running_sc[..., None, :]
    decays = jnp.exp(jnp.where(row_ids >= col_ids, spread, -jnp.inf))
    mixing = (scores * decays).astype(jnp.bfloat16)
    inner_sum = jnp.einsum(
        "schij,scjhp->scihp", mixing, value_blocks, preferred_element_type=jnp.float32
    )
    to_end = jnp.exp(running_pos[:, :, -1:, :] - running_pos)
    weighted = (key_blocks * to_end[..., None]).astype(jnp.bfloat16)
    local_states = jnp.einsum(
        "scjhn,scjhp->schnp", weighted, value_blocks, preferred_element_type=jnp.float32
    )
    block_logs = running_sc[..., -1]
    return (value_blocks, query_blocks, running_pos, inner_sum, local_states, block_logs)


def entry_states(local_states, block_logs):

    def advance(carried, entry_item):
        update, log_total = entry_item
        return (jnp.exp(log_total)[..., None, None] * carried + update, carried)

    start_state = jnp.zeros(local_states.shape[:1] + local_states.shape[2:], jnp.float32)
    final_state, entries = lax.scan(
        advance, start_state, (jnp.moveaxis(local_states, 1, 0), jnp.moveaxis(block_logs, 1, 0))
    )
    return (final_state, jnp.moveaxis(entries, 0, 1))


def carry_into(final_state, device_log):
    log_totals = lax.all_gather(device_log[None], "seq", axis=0, tiled=True)
    my_index = lax.axis_index("seq")
    ranks_all = lax.iota(jnp.int32, log_totals.shape[0])
    between = jnp.logical_and(
        ranks_all[None, :] > ranks_all[:, None], ranks_all[None, :] < my_index
    ).astype(jnp.float32)
    span_logs = jnp.einsum("dk,ksh->dsh", between, log_totals, precision=lax.Precision.HIGHEST)
    weights = jnp.where((ranks_all < my_index)[:, None, None], jnp.exp(span_logs), 0.0)
    return jnp.sum(
        weights[..., None, None] * lax.all_gather(final_state[None], "seq", axis=0, tiled=True),
        axis=0,
    )


def selective_scan(values, keys_in, queries, log_decay, skip, gain):
    block_len = min(BLOCK, values.shape[1])
    value_blocks, query_blocks, running_pos, inner_sum, local_states, block_logs = block_terms(
        values, keys_in, queries, log_decay, block_len
    )
    final_state, entries = entry_states(local_states, block_logs)
    carried = carry_into(final_state, jnp.sum(block_logs, axis=1))
    before = cumulated(block_logs, 1) - block_logs
    states = (entries + jnp.exp(before)[..., None, None] * carried[:, None]).astype(jnp.bfloat16)
    outer_sum = jnp.einsum(
        "scihn,schnp->scihp", query_blocks, states, preferred_element_type=jnp.float32
    )
    raw_out = (
        inner_sum
        + outer_sum * jnp.exp(running_pos)[..., None]
        + skip[:, None] * value_blocks.astype(jnp.float32)
    )
    scaled = raw_out * lax.rsqrt(jnp.mean(raw_out * raw_out, axis=-1, keepdims=True) + 1e-05)
    normed = (scaled * gain.reshape(skip.shape[0], -1)).astype(jnp.bfloat16)
    return normed.reshape(normed.shape[0], -1, normed.shape[3] * normed.shape[4])


def project_rows(features, w_values, w_keys, w_step):
    slab_count, length, feat_width = features.shape
    head_count = w_values.shape[0]
    split_feat = features.reshape(slab_count, length, head_count, feat_width // head_count)
    values_two = jnp.einsum(
        "slhp,hpk->slhk", split_feat, w_values, preferred_element_type=jnp.float32
    ).astype(jnp.bfloat16)
    keys_two = jnp.einsum(
        "slhp,hpk->slhk", split_feat, w_keys, preferred_element_type=jnp.float32
    ).astype(jnp.bfloat16)
    step_pre = jnp.einsum(
        "slhp,hp->slh", split_feat, w_step, preferred_element_type=jnp.float32
    ).astype(jnp.bfloat16)
    return (values_two, keys_two, step_pre)


def second_scan(values_two, keys_two, step_pre, step_bias, rates_second, skip_second, gain_second):
    slab_count, length, head_count, key_width = keys_two.shape
    step_size = jax.nn.softplus(step_pre.astype(jnp.float32) + step_bias)
    log_decay = -rates_second[None, :, None] * jnp.transpose(step_size, (0, 2, 1))
    return selective_scan(
        values_two.reshape(slab_count, length, -1),
        keys_two[..., :N].reshape(slab_count, length, -1),
        keys_two[..., N:].reshape(slab_count, length, -1),
        log_decay,
        skip_second,
        gain_second,
    )


def columns_from(received):
    slab_count, rows_all, cols_here, last_width = received.shape
    return jnp.transpose(received, (0, 2, 1, 3)).reshape(
        slab_count, cols_here * rows_all, last_width
    )


def local(
    values_first,
    keys_first,
    queries_first,
    steps_first,
    rates_first,
    skip_first,
    gain_first,
    w_values,
    w_keys,
    w_step,
    step_bias,
    rates_second,
    skip_second,
    gain_second,
):
    log_first = -rates_first[None, :, None] * steps_first
    first_out = selective_scan(
        values_first, keys_first, queries_first, log_first, skip_first, gain_first
    )
    slab_count, length, feat_width = first_out.shape
    home_grid = first_out.reshape(slab_count, ROWS_DEV, length // ROWS_DEV, feat_width)
    received = lax.all_to_all(home_grid, "seq", split_axis=2, concat_axis=1, tiled=True)
    rows_all = received.shape[1]
    cols_here = received.shape[2]
    values_two, keys_two, step_pre = project_rows(columns_from(received), w_values, w_keys, w_step)
    result = second_scan(
        values_two, keys_two, step_pre, step_bias, rates_second, skip_second, gain_second
    )
    column_out = result.reshape(received.shape[0], cols_here, rows_all, result.shape[2])
    home_back = lax.all_to_all(column_out, "seq", split_axis=2, concat_axis=1, tiled=True)
    second_home = jnp.transpose(home_back, (0, 2, 1, 3)).reshape(slab_count, length, feat_width)
    return (first_out.astype(jnp.float32) + second_home.astype(jnp.float32)).astype(jnp.bfloat16)


def cumsum_rows(rows, upper):
    high = rows.astype(jnp.bfloat16).astype(jnp.float32)
    rest = rows - high
    mid = rest.astype(jnp.bfloat16).astype(jnp.float32)
    low = rest - mid
    count = rows.shape[0]
    stacked = jnp.concatenate([high, mid, low, jnp.zeros_like(low)], axis=0).astype(jnp.bfloat16)
    sums = jnp.dot(stacked, upper, preferred_element_type=jnp.float32)
    return sums[:count] + sums[count : 2 * count] + sums[2 * count : 3 * count]


def dot_nt(left, right):
    return lax.dot_general(
        left, right, (((1,), (1,)), ((), ())), preferred_element_type=jnp.float32
    )


def dot_tn(left, right):
    return lax.dot_general(
        left, right, (((0,), (0,)), ((), ())), preferred_element_type=jnp.float32
    )


def column_of(run_row, width):
    return jnp.transpose(jnp.broadcast_to(run_row, (width, run_row.shape[1])))


def inner_part(values, keys_in, queries, run_row, run_col, skip):
    length, width = values.shape
    half = length // 2
    lower = lax.broadcasted_iota(jnp.int32, (half, half), 0) >= lax.broadcasted_iota(
        jnp.int32, (half, half), 1
    )
    reps = half // width

    def decay(rows, columns, masked):
        left = jnp.concatenate([run_col[rows]] * reps, axis=1) if reps > 1 else run_col[rows]
        spread = left - run_row[:, columns]
        return jnp.exp(jnp.where(lower, spread, -jnp.inf) if masked else spread)

    top, bottom = slice(0, half), slice(half, length)
    scores_top = dot_nt(queries[top], keys_in[top])
    scores_bottom = dot_nt(queries[bottom], keys_in)
    mix_top = (scores_top * decay(top, top, True)).astype(jnp.bfloat16)
    mix_bottom = jnp.concatenate(
        [
            (scores_bottom[:, top] * decay(bottom, top, False)).astype(jnp.bfloat16),
            (scores_bottom[:, bottom] * decay(bottom, bottom, True)).astype(jnp.bfloat16),
        ],
        axis=1,
    )
    inner = jnp.concatenate(
        [
            jnp.dot(mix_top, values[top], preferred_element_type=jnp.float32),
            jnp.dot(mix_bottom, values, preferred_element_type=jnp.float32),
        ],
        axis=0,
    )
    return inner + skip * values.astype(jnp.float32)


def state_part(values, keys_in, run_col):
    last = run_col[run_col.shape[0] - 1 :, :]
    weighted = (keys_in.astype(jnp.float32) * jnp.exp(last - run_col)).astype(jnp.bfloat16)
    return dot_tn(weighted, values)


def outer_part(queries, run_col, state):
    outer = jnp.dot(queries, state.astype(jnp.bfloat16), preferred_element_type=jnp.float32)
    return jnp.exp(run_col) * outer


def advanced(state, run_col, update):
    return jnp.exp(run_col[run_col.shape[0] - 1 :, :]) * state + update


def norm_factor(raw):
    return lax.rsqrt(jnp.mean(raw * raw, axis=1, keepdims=True) + 1e-05)


def decay_outer(queries, run_col, state):
    outer = jnp.dot(queries, state, preferred_element_type=jnp.float32)
    return jnp.exp(run_col) * outer


def inner_any_order(values, keys_in, queries, run_row, run_col, bias, skip):
    length, width = values.shape
    left = jnp.concatenate([run_col] * (length // width), axis=1)
    scores = dot_nt(queries, keys_in)
    mixing = (scores * jnp.exp(left - run_row + bias)).astype(jnp.bfloat16)
    inner = jnp.dot(mixing, values, preferred_element_type=jnp.float32)
    return inner + skip * values.astype(jnp.float32)


def fused_kernel(parts, heads, side, *refs):
    values, keys_in, queries, steps, w_values, w_keys = refs[:6]
    small_in, out = refs[6:14], refs[14]
    v_buf, k_buf, q_buf, step_buf, wv_buf, wk_buf = refs[15:21]
    small = refs[21:29]
    w_step, gain_first, gain_second = small[:3]
    rates_first, skip_first, step_bias, rates_second, skip_second = small[3:]
    row_buf, col_buf, update_buf, raw_buf, stage_state, stage_raw = refs[29:35]
    state_in, back_in, far_in, rows_in, raw_in, maps_in = refs[35:41]
    first_buf, column_buf, second_buf, home_buf, bias_buf, upper_buf, run_state = refs[41:48]
    own_sem, unit_sem, state_send, rows_send, raw_send, maps_send = refs[48:54]
    state_recv, back_recv, far_recv, rows_recv, raw_recv, maps_recv = refs[54:60]
    first_send, first_recv, second_send, second_recv, ready = refs[60:]
    me = lax.axis_index("seq")
    length, width = raw_buf.shape[1:]
    slabs = parts // heads
    last_part = parts - 1
    rows_here, cols_here = side // parts, length // side
    chunk = rows_here * cols_here
    groups = parts // GROUP
    my_head = lax.rem(me, heads)
    mesh_id = pl.DeviceIdType.MESH
    even = lax.rem(lax.axis_index("head"), 2) == 0

    def chosen(modes):
        if modes[0] == modes[1]:
            return me >= 0 if modes[0] else me < 0
        return even if modes[0] else jnp.logical_not(even)

    maps_two, maps_three = chosen(MAPS_TWO), chosen(MAPS_THREE)
    chain = chosen(CHAIN)
    far_needed = jnp.logical_not(maps_three | chain)
    across_two, across_three = chosen(ACROSS_TWO), chosen(ACROSS_THREE)
    whole_two, whole_three = jnp.logical_not(across_two), jnp.logical_not(across_three)
    states_two, states_three = jnp.logical_not(maps_two), jnp.logical_not(maps_three)
    left = me < 2
    started = []

    def send(condition, copy):
        @pl.when(condition)
        def _():
            copy.start()

        started.append((condition, copy))


    def lanes(head):
        return slice(head * width, (head + 1) * width)

    def of_unit(array, unit):
        return array[unit // heads, :, lanes(unit % heads)]

    barrier = pltpu.get_barrier_semaphore()

    def greet(sources, target):
        @pl.when(sources)
        def _():
            pl.semaphore_signal(
                barrier, inc=1, device_id={"seq": target}, device_id_type=mesh_id
            )

    for target in range(1, parts):
        greet(me != target, target)
    greet(me == 1, 0)

    step_copy = pltpu.make_async_copy(steps, step_buf, own_sem.at[0])
    step_copy.start()
    small_copies = [
        pltpu.make_async_copy(src, dst, own_sem.at[3 + index])
        for index, (src, dst) in enumerate(zip(small_in, small))
    ]
    unit_copies = [
        [
            pltpu.make_async_copy(src.at[slab], dst.at[slab], unit_sem.at[kind, slab])
            for slab in range(slabs)
        ]
        for kind, (src, dst) in enumerate(((keys_in, k_buf), (values, v_buf), (queries, q_buf)))
    ]
    weight_copies = [
        pltpu.make_async_copy(w_values.at[my_head], wv_buf, own_sem.at[1]),
        pltpu.make_async_copy(w_keys.at[my_head], wk_buf, own_sem.at[2]),
    ]
    early = [*unit_copies[0], *unit_copies[1]]
    late = [*unit_copies[2], *small_copies[:3], *small_copies[4:], *weight_copies]
    small_copies[3].start()
    for copy in early + late:
        copy.start()

    square = (length, length)
    upper = jnp.where(
        lax.broadcasted_iota(jnp.int32, square, 0) <= lax.broadcasted_iota(jnp.int32, square, 1),
        1.0,
        0.0,
    ).astype(jnp.bfloat16)

    def remote(src, dst, send_sem, recv_sem, target):
        return pltpu.make_async_remote_copy(
            src_ref=src,
            dst_ref=dst,
            send_sem=send_sem,
            recv_sem=recv_sem,
            device_id={"seq": target},
            device_id_type=mesh_id,
        )

    def state_copy(unit, target):
        return remote(
            stage_state.at[unit],
            state_in.at[unit],
            state_send.at[target, unit],
            state_recv.at[unit],
            target,
        )

    def back_copy():
        return remote(stage_state.at[0], back_in, state_send.at[0, 0], back_recv, 0)

    def far_copy(unit, target):
        return remote(
            stage_state.at[unit],
            far_in.at[unit],
            state_send.at[target, unit],
            far_recv.at[unit],
            target,
        )

    def rows_copy(source, target):
        return remote(
            row_buf, rows_in.at[source], rows_send.at[target], rows_recv.at[source], target
        )

    def raw_copy(source, target):
        return remote(
            stage_raw.at[target],
            raw_in.at[source],
            raw_send.at[target],
            raw_recv.at[source],
            target,
        )

    def maps_copy(source, target):
        return remote(
            queries.at[target // heads, :, lanes(target % heads)],
            maps_in.at[source],
            maps_send.at[target],
            maps_recv.at[source],
            target,
        )

    def first_copy(unit, group, source):
        return remote(
            first_buf.at[unit, pl.ds(group * GROUP, GROUP)],
            column_buf.at[pl.ds(group * GROUP, GROUP), source],
            first_send.at[unit, group],
            first_recv.at[source, group],
            unit,
        )

    def second_copy(group, target, source):
        return remote(
            second_buf.at[target, pl.ds(group * GROUP, GROUP)],
            home_buf.at[source, pl.ds(group * GROUP, GROUP)],
            second_send.at[target, group],
            second_recv.at[source, group],
            target,
        )

    step_copy.wait()
    small_copies[3].wait()
    logs = [
        -rates_first[head] * step_buf[slab, head : head + 1, :]
        for slab in range(slabs)
        for head in range(heads)
    ]
    logs = jnp.concatenate(logs + logs[:1] * (-parts % 8), axis=0)
    running = cumsum_rows(logs, upper)
    row_buf[...] = running
    columns_of = [column_of(running[unit : unit + 1], width) for unit in range(parts)]
    for copy in early:
        copy.wait()
    @pl.when(me > 1)
    def _():
        pl.semaphore_wait(barrier, last_part)

    @pl.when(me == last_part)
    def _():
        pl.semaphore_signal(ready, inc=1, device_id={"seq": 0}, device_id_type=mesh_id)

    for target in (0, 1):
        send((me == 2) & maps_two, maps_copy(2, target))
        send((me == 3) & maps_three, maps_copy(3, target))
    send((me == 3) & across_three, maps_copy(3, 2))
    updates = [
        state_part(of_unit(v_buf, unit), of_unit(k_buf, unit), columns_of[unit])
        for unit in range(parts)
    ]
    for unit in range(parts):
        stage_state[unit] = updates[unit].astype(jnp.bfloat16)

    rows_right = far_needed | across_two | whole_three
    send((me == 2) & rows_right, rows_copy(2, 3))
    for unit in (0, 1):
        send((me == 2) & far_needed, far_copy(unit, 3))
    send((me == 2) & across_two, far_copy(3, 3))
    send((me == 2) & whole_three, far_copy(2, 3))
    for target in (0, 1):
        send((me == 2) & (maps_two | maps_three), rows_copy(2, target))
        send((me == 3) & maps_three, rows_copy(3, target))
        send((me == 2) & maps_three, far_copy(target, target))
    send((me == 3) & across_three, rows_copy(3, 2))

    @pl.when(me == 0)
    def _():
        pl.semaphore_wait(barrier, 1)

    for unit in range(parts):
        send(me == 0, state_copy(unit, 1))

    @pl.when(me == 0)
    def _():
        state_in[...] = jnp.zeros_like(state_in)

    for unit in range(parts):
        col_buf[unit] = columns_of[unit]
        update_buf[unit] = updates[unit]
    for copy in late:
        copy.wait()
    raws = [
        inner_part(
            of_unit(v_buf, unit),
            of_unit(k_buf, unit),
            of_unit(q_buf, unit),
            running[unit : unit + 1],
            columns_of[unit],
            skip_first[unit % heads],
        )
        for unit in range(parts)
    ]
    for unit in range(parts):
        raw_buf[unit] = raws[unit]
        stage_raw[unit] = raws[unit].astype(jnp.bfloat16)

    for target in (0, 1):
        send((me == 2) & maps_two, raw_copy(2, target))
        send((me == 3) & maps_three, raw_copy(3, target))
    send((me == 2) & across_two, maps_copy(2, 3))
    send((me == 2) & across_two, raw_copy(2, 3))
    send((me == 3) & across_three, raw_copy(3, 2))

    def rank_of(index):
        owner, inside = lax.div(index, chunk), lax.rem(index, chunk)
        row, col = lax.div(inside, cols_here), lax.rem(inside, cols_here)
        return col * side + owner * rows_here + row

    rank_sub = rank_of(lax.broadcasted_iota(jnp.int32, (length, width), 0))
    rank_sub = jnp.concatenate([rank_sub] * (length // width), axis=1)
    rank_lane = rank_of(lax.broadcasted_iota(jnp.int32, (8, length), 1))[0:1]
    bias_buf[...] = jnp.where(rank_lane <= rank_sub, 0.0, -jnp.inf)
    upper_buf[...] = jnp.where(rank_sub <= rank_lane, 1.0, 0.0).astype(jnp.bfloat16)

    def ordered(normed):
        return [
            jnp.concatenate(
                [
                    normed[row * side + block * cols_here : row * side + (block + 1) * cols_here]
                    for row in range(rows_here)
                ],
                axis=0,
            ).astype(jnp.bfloat16)
            for block in range(parts)
        ]

    def finish(unit):
        raw = raw_buf[unit] + decay_outer(of_unit(q_buf, unit), col_buf[unit], state_in[unit])
        normed = raw * norm_factor(raw) * gain_first[:, lanes(unit % heads)]
        for block, piece in enumerate(ordered(normed)):
            first_buf[unit, block] = piece

        @pl.when(me == unit)
        def _():
            for block in range(parts):
                column_buf[block, unit] = first_buf[unit, block]

    def send_first(condition, *units):
        for group in range(groups):
            for unit in units:
                send(condition, first_copy(unit, group, me))

    @pl.when(me == 1)
    def _():
        pl.semaphore_wait(barrier, last_part)

    for unit in ORDER:
        @pl.when(me == 1)
        def _():
            state_copy(unit, 1).wait_recv()
            last = jnp.exp(col_buf[unit, length - 1 :, :])
            carried = last * state_in[unit].astype(jnp.float32) + update_buf[unit]
            stage_state[unit] = carried.astype(jnp.bfloat16)

        if unit > 1:
            send((me == 1) & (across_two if unit == 3 else whole_three), state_copy(unit, 3))
            send((me == 1) & (whole_two if unit == 3 else me == 1), state_copy(unit, 2))
        else:
            send((me == 1) & far_needed, state_copy(unit, 3))
            send((me == 1) & (states_two | chain), state_copy(unit, 2))
            if unit == 0:
                send((me == 1) & (maps_two | maps_three), back_copy())

    for units in FINISH:
        @pl.when(left)
        def _():
            for unit in units:
                finish(unit)

        if units == (1,):
            send_first(me == 0, *units)
        else:
            send_first(me == 1, *[unit for unit in units if unit != 1])

    def state_three(base, unit):
        row = rows_in[2, pl.ds(unit, 1), :]
        last = jnp.exp(jnp.broadcast_to(row[:, length - 1 :], (1, width)))
        carried = last * base.astype(jnp.float32) + far_in[unit].astype(jnp.float32)
        return carried.astype(jnp.bfloat16)

    @pl.when(((me == 3) & rows_right) | (left & (maps_two | maps_three)))
    def _():
        rows_copy(2, me).wait_recv()

    def advance(unit):
        state_copy(unit, 2).wait_recv()
        last = jnp.exp(col_buf[unit, length - 1 :, :])
        carried = last * state_in[unit].astype(jnp.float32) + update_buf[unit]
        stage_state[unit] = carried.astype(jnp.bfloat16)

    for unit in (0, 1):
        @pl.when((me == 2) & (states_two | chain))
        def _():
            advance(unit)

        send((me == 2) & chain, state_copy(unit, 3))

        @pl.when((me == 2) & states_two)
        def _():
            finish(unit)

        @pl.when((me == 3) & states_three)
        def _():
            state_copy(unit, 3).wait_recv()

            @pl.when(far_needed)
            def _():
                far_copy(unit, 3).wait_recv()
                state_in[unit] = state_three(state_in[unit], unit)

            finish(unit)

        send_first(((me == 2) & states_two) | ((me == 3) & states_three), unit)

    def pick(head, select):
        chosen_one = select(0)
        for index in range(1, heads):
            chosen_one = jnp.where(head == index, select(index), chosen_one)
        return chosen_one

    gain_one = pick(my_head, lambda h: gain_first[:, lanes(h)])

    def absorb(source, state):
        maps_copy(source, 0).wait_recv()
        raw_copy(source, me).wait_recv()
        run_col = column_of(rows_in[source, pl.ds(me, 1), :], width)
        raw = raw_in[source].astype(jnp.float32) + decay_outer(maps_in[source], run_col, state)
        normed = raw * norm_factor(raw) * gain_one
        for block, piece in enumerate(ordered(normed)):
            column_buf[block, source] = piece

    @pl.when((me == 2) & whole_two)
    def _():
        advance(3)

    send((me == 2) & whole_two, state_copy(3, 3))

    @pl.when((me == 2) & whole_two)
    def _():
        finish(3)

    send_first((me == 2) & whole_two, 3)

    @pl.when((me == 3) & whole_three)
    def _():
        state_copy(2, 3).wait_recv()
        far_copy(2, 3).wait_recv()
        state_in[2] = state_three(state_in[2], 2)
        finish(2)

    send_first((me == 3) & whole_three, 2)

    @pl.when(me == 2)
    def _():
        state_copy(2, 2).wait_recv()
        finish(2)

    @pl.when((me == 2) & across_three)
    def _():
        rows_copy(3, 2).wait_recv()
        last = jnp.exp(col_buf[2, length - 1 :, :])
        carried = last * state_in[2].astype(jnp.float32) + update_buf[2]
        absorb(3, carried.astype(jnp.bfloat16))

    @pl.when(me == 3)
    def _():
        state_copy(3, 3).wait_recv()

        @pl.when(across_two)
        def _():
            absorb(2, state_in[3])

            far_copy(3, 3).wait_recv()
            state_in[3] = state_three(state_in[3], 3)

        finish(3)

    @pl.when(me == 0)
    def _():
        pl.semaphore_wait(ready, 1)

    for unit in (2, 3):
        send(me == 0, first_copy(unit, 0, me))

    for owner in (0, 1):
        if owner == 0:
            @pl.when((me == 0) & (maps_two | maps_three))
            def _():
                back_copy().wait_recv()

        base = back_in if owner == 0 else stage_state.at[1]

        @pl.when((me == owner) & maps_two)
        def _():
            absorb(2, base[...])

        @pl.when((me == owner) & maps_three)
        def _():
            far_copy(owner, owner).wait_recv()
            rows_copy(3, owner).wait_recv()
            absorb(3, state_three(base[...], owner))

    for group in range(1, groups):
        for unit in (2, 3):
            send(me == 0, first_copy(unit, group, me))

    def whole(source):
        if source < 2:
            return me != source
        own = (me == 3) & across_two if source == 2 else (me == 2) & across_three
        absorbed = left & (maps_two if source == 2 else maps_three)
        return jnp.logical_not(own | absorbed | (me == source))

    step_row = pick(my_head, lambda h: w_step[...].astype(jnp.float32)[h : h + 1, :])
    step_rows = jnp.broadcast_to(step_row, (16, width)).astype(jnp.bfloat16)
    gain_two = pick(my_head, lambda h: gain_second[:, lanes(h)])

    def local_terms(columns):
        values_two = jnp.dot(columns, wv_buf[...], preferred_element_type=jnp.float32).astype(
            jnp.bfloat16
        )
        keys_two = jnp.dot(columns, wk_buf[...], preferred_element_type=jnp.float32).astype(
            jnp.bfloat16
        )
        pre = dot_nt(step_rows, columns)[0:8].astype(jnp.bfloat16).astype(jnp.float32)
        shifted = pre + step_bias[my_head]
        soft = jnp.maximum(shifted, 0.0) + jnp.log1p(jnp.exp(-jnp.abs(shifted)))
        run_row = cumsum_rows(-rates_second[my_head] * soft, upper_buf[...])[0:1]
        run_col = column_of(run_row, width)
        half = keys_two.shape[1] // 2
        keys_now, queries_now = keys_two[:, :half], keys_two[:, half:]
        raw = inner_any_order(
            values_two,
            keys_now,
            queries_now,
            run_row,
            run_col,
            bias_buf[...],
            skip_second[my_head],
        )
        return raw, queries_now, run_col, state_part(values_two, keys_now, run_col)

    for group in range(groups):
        for source in range(parts):
            @pl.when(whole(source))
            def _():
                first_copy(me, group, source).wait_recv()

        blocks = range(group * GROUP, (group + 1) * GROUP)
        terms = [local_terms(column_buf[block].reshape(length, width)) for block in blocks]
        for block, (raw, queries_now, run_col, update) in zip(blocks, terms):
            if block == 0:
                state = update
            else:
                before = run_state[...] if block == blocks[0] else state
                raw = raw + outer_part(queries_now, run_col, before)
                state = advanced(before, run_col, update)
            normed = (raw * norm_factor(raw) * gain_two).astype(jnp.bfloat16)
            for target in range(parts):
                piece = normed[target * chunk : (target + 1) * chunk].astype(jnp.float32)
                piece = piece + column_buf[block, target].astype(jnp.float32)
                second_buf[target, block] = piece.astype(jnp.bfloat16)
        if group < groups - 1:
            run_state[...] = state

        for target in range(parts):
            send(me != target, second_copy(group, target, me))

            @pl.when(me == target)
            def _():
                for block in blocks:
                    home_buf[target, block] = second_buf[target, block]

    for condition, copy in started:
        @pl.when(condition)
        def _():
            copy.wait_send()

    for group in range(groups):
        ready_pairs = range(
            max((group + 1) * GROUP - max(GROUP, 2), 0), (group + 1) * GROUP // 2 * 2, 2
        )
        for unit in range(parts):
            @pl.when(me != unit)
            def _():
                second_copy(group, me, unit).wait_recv()

            for pair in ready_pairs:
                total = [home_buf[unit, block].astype(jnp.float32) for block in (pair, pair + 1)]
                for row in range(rows_here):
                    place = slice(row * cols_here, (row + 1) * cols_here)
                    out[
                        unit // heads,
                        pl.ds(row * side + pair * cols_here, 2 * cols_here),
                        lanes(unit % heads),
                    ] = jnp.concatenate([part[place] for part in total], axis=0).astype(
                        jnp.bfloat16
                    )


def local_fused(
    parts,
    values_first,
    keys_first,
    queries_first,
    steps_first,
    rates_first,
    skip_first,
    gain_first,
    w_values,
    w_keys,
    w_step,
    step_bias,
    rates_second,
    skip_second,
    gain_second,
):
    slab_count, length, feat_width = values_first.shape
    heads = rates_first.shape[0]
    width = feat_width // heads
    side = math.isqrt(parts * length)
    chunk = length // parts
    groups = parts // GROUP
    anywhere = pl.BlockSpec(memory_space=pl.ANY)
    dma = pltpu.SemaphoreType.DMA

    def vmem(dtype, *shape):
        return pltpu.VMEM(shape, dtype)

    bf16, f32 = jnp.bfloat16, jnp.float32
    return pl.pallas_call(
        functools.partial(fused_kernel, parts, heads, side),
        out_shape=jax.ShapeDtypeStruct(values_first.shape, bf16),
        in_specs=[anywhere] * 14,
        out_specs=pl.BlockSpec(memory_space=pltpu.VMEM),
        scratch_shapes=[
            vmem(bf16, *values_first.shape),
            vmem(bf16, *keys_first.shape),
            vmem(bf16, *queries_first.shape),
            vmem(f32, *steps_first.shape),
            vmem(bf16, *w_values.shape[1:]),
            vmem(bf16, *w_keys.shape[1:]),
            vmem(bf16, *w_step.shape),
            vmem(f32, 1, feat_width),
            vmem(f32, 1, feat_width),
        ]
        + [pltpu.SMEM((heads,), f32)] * 5
        + [
            vmem(f32, parts + -parts % 8, length),
            vmem(f32, parts, length, width),
            vmem(f32, parts, width, width),
            vmem(f32, parts, length, width),
            vmem(bf16, parts, width, width),
            vmem(bf16, parts, length, width),
            vmem(bf16, parts, width, width),
            vmem(bf16, width, width),
            vmem(bf16, parts, width, width),
            vmem(f32, parts, parts + -parts % 8, length),
            vmem(bf16, parts, length, width),
            vmem(bf16, parts, length, width),
            vmem(bf16, parts, parts, chunk, width),
            vmem(bf16, parts, parts, chunk, width),
            vmem(bf16, parts, parts, chunk, width),
            vmem(bf16, parts, parts, chunk, width),
            vmem(f32, length, length),
            vmem(bf16, length, length),
            vmem(f32, width, width),
            dma((11,)),
            dma((3, parts)),
            dma((parts, parts)),
            dma((parts,)),
            dma((parts,)),
            dma((parts,)),
            dma((parts,)),
            dma,
            dma((parts,)),
            dma((parts,)),
            dma((parts,)),
            dma((parts,)),
            dma((parts, groups)),
            dma((parts, groups)),
            dma((parts, groups)),
            dma((parts, groups)),
            pltpu.SemaphoreType.REGULAR,
        ],
        compiler_params=pltpu.CompilerParams(
            collective_id=0, has_side_effects=True, vmem_limit_bytes=VMEM_GRANT
        ),
    )(
        *(
            pltpu.with_memory_space_constraint(array, pltpu.HBM)
            for array in (
                values_first,
                keys_first,
                queries_first,
                steps_first,
                w_values,
                w_keys,
                w_step,
                gain_first.reshape(1, -1),
                gain_second.reshape(1, -1),
                rates_first,
                skip_first,
                step_bias,
                rates_second,
                skip_second,
            )
        )
    )


def fits_fused(parts, args):
    values, w_values, w_keys = args[0], args[7], args[8]
    slab_count, length, feat_width = values.shape
    heads = args[4].shape[0]
    side = math.isqrt(parts * length)
    return (
        slab_count * heads == parts
        and parts == len(ORDER)
        and (side // parts) * (length // side) % 16 == 0
        and length <= BLOCK
        and length % 256 == 0
        and side * side == parts * length
        and side % parts == 0
        and length % side == 0
        and (length // side) % 8 == 0
        and feat_width // heads == 128
        and w_values.shape[1:] == (128, 128)
        and w_keys.shape[1:] == (128, 256)
    )


def solution(mesh):
    parts = mesh.shape["seq"]

    def chosen(*args):
        if fits_fused(parts, args):
            return local_fused(parts, *args)
        return local(*args)

    placed = (
        P("slab", "seq", "head"),
        P("slab", "seq", "head"),
        P("slab", "seq", "head"),
        P("slab", "head", "seq"),
        P("head"),
        P("head"),
        P("head"),
        P("head", None, None),
        P("head", None, None),
        P("head", None),
        P("head"),
        P("head"),
        P("head"),
        P("head"),
    )
    return jax.shard_map(
        chosen, mesh=mesh, in_specs=placed, out_specs=P("slab", "seq", "head"), check_vma=False
    )
```
